32 devices in a mesh: wave: 4 (over z), tile: 8 (over y, x, core).
Axes of the slice: x: 2, y: 2, z: 4, core: 2. Of those that a mesh axis runs over, the one named last changes fastest.
Arguments:
- warm_start: float32 [4, 2, 256, 1024], P('wave', None, 'tile'), may hold values from -30 to 30
- class_map: int32 [256, 1024], P('tile'), may hold values from 0 to 7
- conductivities: float32 [8], replicated, may hold values from 0.1 to 10
- wavenumbers: float32 [4], P('wave'), may hold values from 0.05 to 2
- weights: float32 [4], P('wave'), may hold values from 0.1 to 1
- source_row: int32 [2], replicated, may hold values from 0 to 255
- source_col: int32 [2], replicated, may hold values from 0 to 1023
- electrode_row: int32 [64], replicated, may hold values from 0 to 255
Outputs:
- potentials: float32 [2, 256, 1024], P(None, 'tile', 'wave')
- readings: float32 [2, 64], replicated
The draws below stay inside these ranges and needn't reach their ends.
All inputs are finite; a program needn't handle non-finite values.
Results may differ from the reference program's by a relative error of at most 0.0003.
Values sent between devices are 32-bit elements; how exact they have to be, the bound alone decides.
No kernel may reach another device: no remote copies, remote signals or barrier semaphores. Data moves between devices by JAX's collectives and lax.ppermute only.
A program may use at most 64 MiB of HBM per device.

```python
import math
import jax
import jax.numpy as jnp
from jax import lax

SRC = 2
NY = 1024
ITERS = 3
NCLASS = 8
NELEC = 64
NK = 4
NX = 256


def draw_warm_start(key, part):
    first_key = jax.random.fold_in(key, 11)
    shape = (NK, SRC, NX, NY)
    row_frac = jnp.arange(NX, dtype=jnp.float32) / NX
    col_frac = jnp.arange(NY, dtype=jnp.float32) / NY
    values = jnp.clip(jax.random.normal(first_key, shape, jnp.float32), -5.0, 5.0)
    scale = jnp.power(10.0, row_frac - 0.5)[:, None] * jnp.power(10.0, 0.5 * col_frac - 0.25)[None, :]
    return values * scale[None, None]


def with_ends(drawn, rng, least, top_value):
    place = [jax.random.randint(jax.random.fold_in(rng, axis), (), 0, length) for axis, length in enumerate(drawn.shape)]
    widest = drawn.shape.index(max(drawn.shape))
    next_to = place[:widest] + [(place[widest] + 1) % drawn.shape[widest]] + place[widest + 1:]
    return drawn.at[tuple(place)].set(least).at[tuple(next_to)].set(top_value)


def level_of(own_key, extent, pieces, low, largest):
    def one(dim, shards_of):
        steps = jax.random.uniform(jax.random.fold_in(jax.random.fold_in(own_key, 6), dim), (shards_of,), jnp.float32, low / len(pieces), largest / len(pieces))
        return jnp.repeat(jnp.exp(steps), extent[dim] // shards_of).reshape((-1,) + (1,) * (len(extent) - dim - 1))

    level = one(*pieces[0])
    for cut in pieces[1:]:
        level = level * one(*cut)
    return level


def setup_inputs(seed: int = 0) -> dict:
    streams_of = jax.random.split(jax.random.key(seed), 9)
    warm_start = draw_warm_start(jax.random.fold_in(streams_of[8], 71), 0)
    class_map = with_ends(jax.random.randint(streams_of[1], (NX, NY), 0, NCLASS), jax.random.fold_in(streams_of[1], 1), 0, NCLASS - 1).astype(jnp.int32)
    conductivities = jnp.clip(jnp.exp(jax.random.uniform(streams_of[2], (NCLASS,), jnp.float32, math.log(0.1), math.log(10.0))), 0.1, 10.0)
    wavenumbers = jnp.clip(jnp.exp(math.log(2.0) - 3.6888794 * jax.random.uniform(streams_of[3], (NK,), jnp.float32) ** level_of(streams_of[3], (NK,), ((0, 4),), -0.2, 0.2)), 0.05, 2.0)
    weights = jnp.clip(jnp.exp(math.log(1.0) - 2.3025851 * jax.random.uniform(streams_of[4], (NK,), jnp.float32) ** level_of(streams_of[4], (NK,), ((0, 4),), -0.2, 0.2)), 0.1, 1.0)
    source_row = jax.random.randint(streams_of[5], (SRC,), 0, NX).astype(jnp.int32)
    source_col = jax.random.randint(streams_of[6], (SRC,), 0, NY).astype(jnp.int32)
    electrode_row = with_ends(jax.random.randint(streams_of[7], (NELEC,), 0, NX), jax.random.fold_in(streams_of[7], 1), 0, NX - 1).astype(jnp.int32)
    return {"warm_start": warm_start, "class_map": class_map, "conductivities": conductivities, "wavenumbers": wavenumbers, "weights": weights, "source_row": source_row, "source_col": source_col, "electrode_row": electrode_row}


source_strength = 50.0


def harmonic(left_val, right_val):
    return 2.0 * left_val * right_val / (left_val + right_val)


def reference(warm_start, class_map, conductivities, wavenumbers, weights, source_row, source_col, electrode_row):
    sigma = conductivities[class_map]
    sigma_pad = jnp.pad(sigma, ((1, 1), (0, 0)))
    face_row = harmonic(sigma_pad[:-1], sigma_pad[1:])
    face_up = face_row[:-1]
    face_down = face_row[1:]
    col_inner = harmonic(sigma[:, :-1], sigma[:, 1:])
    face_left = jnp.concatenate([jnp.zeros((NX, 1), jnp.float32), col_inner], axis=1)
    face_right = jnp.concatenate([col_inner, sigma[:, -1:]], axis=1)
    base = face_up + face_down + face_left + face_right
    row_ids = jnp.arange(NX, dtype=jnp.int32)
    col_ids = jnp.arange(NY, dtype=jnp.int32)
    hits = (row_ids[None, :, None] == source_row[:, None, None]) & (col_ids[None, None, :] == source_col[:, None, None])
    rhs = source_strength * hits.astype(jnp.float32)

    def one_wave(total, inputs):
        warm, wave_num, weight = inputs
        diag = base + (wave_num * wave_num) * sigma

        def operate(values):
            row_padded = jnp.pad(values, ((0, 0), (1, 1), (0, 0)))
            col_padded = jnp.pad(values, ((0, 0), (0, 0), (1, 1)))
            return (diag * values - face_up * row_padded[:, :-2] - face_down * row_padded[:, 2:]
                    - face_left * col_padded[:, :, :-2] - face_right * col_padded[:, :, 2:])

        def inner(first, second):
            return jnp.sum(first * second, axis=(1, 2))[:, None, None]

        field = warm
        residual = rhs - operate(field)
        scaled = residual / diag
        direction = scaled
        gamma_now = inner(residual, scaled)
        for iteration in range(ITERS):
            image = operate(direction)
            step_size = gamma_now / inner(direction, image)
            field = field + step_size * direction
            residual = residual - step_size * image
            scaled = residual / diag
            gamma_next = inner(residual, scaled)
            direction = scaled + (gamma_next / gamma_now) * direction
            gamma_now = gamma_next
        return total + weight * field, None

    potentials, _ = lax.scan(one_wave, jnp.zeros((SRC, NX, NY), jnp.float32), (warm_start, wavenumbers, weights))
    readings = potentials[:, electrode_row, 0]
    return potentials, readings
```

```python
import jax
import jax.numpy as jnp
from jax import lax
from jax.sharding import PartitionSpec as P

ITERS = 3
SOURCE_STRENGTH = 50.0
TINY = 1e-30


def harmonic(left_val, right_val):
    return 2.0 * left_val * right_val / jnp.maximum(left_val + right_val, TINY)


def safe_div(num, den):
    return jnp.where(den > 0.0, num / jnp.where(den > 0.0, den, 1.0), 0.0)


def tree_sum(values):
    values = list(values)
    while len(values) > 1:
        values = [values[i] + values[i + 1] for i in range(0, len(values), 2)]
    return values[0]


def swap(value, axis, mask, size):
    return lax.ppermute(value, axis, [(i, i ^ mask) for i in range(size)])


def tile_total(value, axis):
    size = lax.axis_size(axis)
    bit = 1
    while bit < size:
        masks = [bit]
        if bit > 1 and bit * 2 < size:
            masks.append(bit * 2)
        offsets = [0]
        for mask in masks:
            offsets += [o ^ mask for o in offsets]
        value = tree_sum([value] + [swap(value, axis, o, size) for o in offsets[1:]])
        bit = masks[-1] * 2
    return value


def step_polynomial(moments):
    def inner(poly):
        return sum(a * b * moments[i + j] for i, a in enumerate(poly) for j, b in enumerate(poly))

    def energy(poly):
        return sum(
            a * b * (moments[i + j] - moments[i + j + 1])
            for i, a in enumerate(poly)
            for j, b in enumerate(poly)
        )

    one = jnp.ones_like(moments[0])
    zero = jnp.zeros_like(moments[0])
    res, way, total = [one], [one], [zero] * ITERS
    gamma = moments[0]
    for iteration in range(ITERS):
        alpha = safe_div(gamma, energy(way))
        total = [t + alpha * (way[i] if i < len(way) else zero) for i, t in enumerate(total)]
        if iteration + 1 < ITERS:
            longer = way + [zero]
            shifted = [zero] + way
            res = [r - alpha * (a - b) for r, a, b in zip(res + [zero], longer, shifted)]
            gamma_next = jnp.maximum(inner(res), 0.0)
            ratio = safe_div(gamma_next, gamma)
            way = [r + ratio * a for r, a in zip(res, longer)]
            gamma = gamma_next
    return total


def shards(
    warm_start,
    class_map,
    conductivities,
    wavenumbers,
    weights,
    source_row,
    source_col,
    electrode_row,
):
    rows, depth = class_map.shape
    sources = warm_start.shape[1]
    tiles, waves = lax.axis_size("tile"), lax.axis_size("wave")
    tile, wave = lax.axis_index("tile"), lax.axis_index("wave")
    halo = ITERS + 1
    even = tile % 2 == 0
    field = warm_start[0]
    ids = class_map.astype(jnp.float32) + 1.0
    stacked = jnp.concatenate([field, ids[None]], axis=0)
    first, last = stacked[:, :halo], stacked[:, rows - halo :]
    near = swap(jnp.where(even, last, first), "tile", 1, tiles)
    far_pairs = [(i, i + 1) for i in range(1, tiles - 1, 2)]
    far = lax.ppermute(
        jnp.where(even, first, last), "tile", far_pairs + [(j, i) for i, j in far_pairs]
    )
    before = jnp.where(even, far, near)
    after = jnp.where(even, near, far)
    wide = jnp.concatenate([before, stacked, after], axis=1)
    start, ids = wide[:sources], wide[sources]
    total_rows = rows + 2 * halo
    sigma = jnp.zeros_like(ids)
    for c in range(conductivities.shape[0]):
        sigma = jnp.where(ids == c + 1.0, conductivities[c], sigma)
    edge_row = jnp.zeros((1, depth), jnp.float32)
    edge_col = jnp.zeros((total_rows, 1), jnp.float32)
    face_row = harmonic(sigma[:-1], sigma[1:])
    face_up = jnp.concatenate([edge_row, face_row], axis=0)
    face_down = jnp.concatenate([face_row, edge_row], axis=0)
    col_inner = harmonic(sigma[:, :-1], sigma[:, 1:])
    face_left = jnp.concatenate([edge_col, col_inner], axis=1)
    face_right = jnp.concatenate([col_inner, sigma[:, -1:]], axis=1)
    wave_num = wavenumbers[0]
    diag = face_up + face_down + face_left + face_right + wave_num * wave_num * sigma
    inverse = 1.0 / jnp.maximum(diag, TINY)
    global_row = tile * rows - halo + jnp.arange(total_rows, dtype=jnp.int32)
    col_ids = jnp.arange(depth, dtype=jnp.int32)
    hits = (global_row[None, :, None] == source_row[:, None, None]) & (
        col_ids[None, None, :] == source_col[:, None, None]
    )

    def spread(values):
        row_padded = jnp.pad(values, ((0, 0), (1, 1), (0, 0)))
        col_padded = jnp.pad(values, ((0, 0), (0, 0), (1, 1)))
        return (
            face_up * row_padded[:, :-2]
            + face_down * row_padded[:, 2:]
            + face_left * col_padded[:, :, :-2]
            + face_right * col_padded[:, :, 2:]
        ) * inverse

    basis = [jnp.where(hits, SOURCE_STRENGTH, 0.0) * inverse - (start - spread(start))]
    for _ in range(ITERS):
        basis.append(spread(basis[-1]))
    own = [b[:, halo : halo + rows] for b in basis]
    own_diag = diag[halo : halo + rows]
    moments = [
        jnp.sum(own_diag * own[n // 2] * own[n - n // 2], axis=(1, 2)) for n in range(2 * ITERS)
    ]
    parts = [field] + own[:ITERS]
    tops = jnp.stack([p[:, :, 0] for p in parts])
    own_row = tile * rows + jnp.arange(rows, dtype=jnp.int32)
    picker = own_row[:, None] == electrode_row[None, :]
    picked = jnp.sum(jnp.where(picker, tops[:, :, :, None], 0.0), axis=2)
    electrodes = electrode_row.shape[0]
    packed = jnp.concatenate([picked.reshape(-1), jnp.stack(moments).reshape(-1)])
    packed = tile_total(packed, "tile")
    picked = packed[: picked.size].reshape(picked.shape)
    moments = packed[picked.size :].reshape(2 * ITERS, sources)
    poly = step_polynomial([moments[n] for n in range(2 * ITERS)])

    def combine(vectors):
        out = vectors[0]
        for coefficient, vector in zip(poly, vectors[1:]):
            out = out + coefficient.reshape((sources,) + (1,) * (vector.ndim - 1)) * vector
        return weights[0] * out

    weighted = combine(parts)
    local_read = combine([picked[i] for i in range(ITERS + 1)])
    share = depth // waves
    pieces, reads = [], []
    for mask in range(waves):
        block = lax.dynamic_slice_in_dim(weighted, (wave ^ mask) * share, share, 2)
        payload = jnp.concatenate([block.reshape(-1), local_read.reshape(-1)])
        if mask:
            payload = swap(payload, "wave", mask, waves)
        pieces.append(payload[: block.size])
        reads.append(payload[block.size :])
    potentials = tree_sum(pieces).reshape(sources, rows, share)
    readings = tree_sum(reads).reshape(sources, electrodes)
    return (potentials, readings)


def solution(mesh):
    return jax.shard_map(
        shards,
        mesh=mesh,
        in_specs=(
            P("wave", None, "tile", None),
            P("tile", None),
            P(),
            P("wave"),
            P("wave"),
            P(),
            P(),
            P(),
        ),
        out_specs=(P(None, "tile", "wave"), P()),
        check_vma=False,
    )
```

```python
import functools

import jax
import jax.numpy as jnp
from jax import lax
from jax.experimental import pallas as pl
from jax.experimental.pallas import tpu as pltpu
from jax.sharding import PartitionSpec as P

ITERS = 3
SOURCE_STRENGTH = 50.0
TINY = 1e-30
LANES = 128
SUBLANES = 8


def harmonic(left_val, right_val):
    return 2.0 * left_val * right_val / jnp.maximum(left_val + right_val, TINY)


def safe_div(num, den):
    return jnp.where(den > 0.0, num / jnp.where(den > 0.0, den, 1.0), 0.0)


def tree_sum(values):
    values = list(values)
    while len(values) > 1:
        values = [values[i] + values[i + 1] for i in range(0, len(values), 2)]
    return values[0]


def swap(value, axis, mask, size):
    return lax.ppermute(value, axis, [(i, i ^ mask) for i in range(size)])


def tile_total(value, axis):
    size = lax.axis_size(axis)
    bit = 1
    while bit < size:
        masks = [bit]
        if bit > 1 and bit * 2 < size:
            masks.append(bit * 2)
        offsets = [0]
        for mask in masks:
            offsets += [o ^ mask for o in offsets]
        value = tree_sum([value] + [swap(value, axis, o, size) for o in offsets[1:]])
        bit = masks[-1] * 2
    return value


def step_polynomial(moments):
    def inner(poly):
        return sum(a * b * moments[i + j] for i, a in enumerate(poly) for j, b in enumerate(poly))

    def energy(poly):
        return sum(
            a * b * (moments[i + j] - moments[i + j + 1])
            for i, a in enumerate(poly)
            for j, b in enumerate(poly)
        )

    one = jnp.ones_like(moments[0])
    zero = jnp.zeros_like(moments[0])
    res, way, total = [one], [one], [zero] * ITERS
    gamma = moments[0]
    for iteration in range(ITERS):
        alpha = safe_div(gamma, energy(way))
        total = [t + alpha * (way[i] if i < len(way) else zero) for i, t in enumerate(total)]
        if iteration + 1 < ITERS:
            longer = way + [zero]
            shifted = [zero] + way
            res = [r - alpha * (a - b) for r, a, b in zip(res + [zero], longer, shifted)]
            gamma_next = jnp.maximum(inner(res), 0.0)
            ratio = safe_div(gamma_next, gamma)
            way = [r + ratio * a for r, a in zip(res, longer)]
            gamma = gamma_next
    return total


def vmem_call(kernel, out_shape, inputs, scratch=()):
    spec = pl.BlockSpec(memory_space=pltpu.VMEM)
    return pl.pallas_call(
        kernel,
        out_shape=out_shape,
        in_specs=[spec] * len(inputs),
        out_specs=jax.tree.map(lambda _: spec, out_shape),
        scratch_shapes=list(scratch),
    )(*inputs)


def stencil_kernel(
    n_class, par_ref, field_ref, class_ref, halo_ref, *refs
):
    x_ref = refs[0]
    basis_refs = refs[1 : 1 + ITERS]
    pay_ref, sig_ref, left_ref, up_ref, down_ref, west_ref, east_ref, diag_ref = refs[1 + ITERS :]
    sources, rows, depth = field_ref.shape
    total = x_ref.shape[2]
    chunks = depth // LANES
    lane = lax.broadcasted_iota(jnp.int32, (total, LANES), 1)
    row = lax.broadcasted_iota(jnp.int32, (total, LANES), 0)

    def scalar(i):
        return par_ref[0:1, i : i + 1]

    def cols(c):
        return slice(c * LANES, (c + 1) * LANES)

    values = [scalar(i) for i in range(n_class)]
    square = scalar(n_class) * scalar(n_class)
    base = scalar(n_class + 2)
    for c in range(chunks):
        ids = jnp.concatenate(
            [class_ref[:, cols(c)].astype(jnp.float32) + 1.0, halo_ref[sources, :, cols(c)]], axis=0
        )
        sigma = jnp.zeros((total, LANES), jnp.float32)
        for i, value in enumerate(values):
            sigma = jnp.where(ids == i + 1.0, value, sigma)
        sig_ref[c] = sigma
        for s in range(sources):
            x_ref[s, c] = jnp.concatenate([field_ref[s, :, cols(c)], halo_ref[s, :, cols(c)]], axis=0)

    def from_left(ref, c):
        here = pltpu.roll(ref[c], 1, 1)
        other = pltpu.roll(ref[c - 1 if c else chunks - 1], 1, 1)
        return jnp.where(lane == 0, other, here)

    def from_right(ref, c):
        here = pltpu.roll(ref[c], LANES - 1, 1)
        other = pltpu.roll(ref[(c + 1) % chunks], LANES - 1, 1)
        return jnp.where(lane == LANES - 1, other, here)

    for c in range(chunks):
        face = harmonic(from_left(sig_ref, c), sig_ref[c])
        left_ref[c] = jnp.where(lane == 0, 0.0, face) if c == 0 else face

    far_row = jnp.where(row < total - (total - rows) // 2, row, row - total).astype(jnp.float32)
    for c in range(chunks):
        sigma = sig_ref[c]
        up = harmonic(pltpu.roll(sigma, 1, 0), sigma)
        down = pltpu.roll(up, total - 1, 0)
        left = left_ref[c]
        right = from_right(left_ref, c)
        diag = up + down + left + right + square * sigma
        if c == chunks - 1:
            diag = diag + jnp.where(lane == LANES - 1, sigma, 0.0)
        inverse = 1.0 / jnp.maximum(diag, TINY)
        diag_ref[c] = diag
        up_ref[c] = up * inverse
        down_ref[c] = down * inverse
        west_ref[c] = left * inverse
        east_ref[c] = right * inverse
        for s in range(sources):
            hit = (far_row + base == scalar(n_class + 3 + s)) & (
                (lane + c * LANES).astype(jnp.float32) == scalar(n_class + 3 + sources + s)
            )
            basis_refs[0][s, c] = jnp.where(hit, SOURCE_STRENGTH * inverse, 0.0)

    def spread(ref, s, c):
        here = ref[s, c]
        return (
            up_ref[c] * pltpu.roll(here, 1, 0)
            + down_ref[c] * pltpu.roll(here, total - 1, 0)
            + west_ref[c] * from_left(ref.at[s], c)
            + east_ref[c] * from_right(ref.at[s], c)
        )

    def fold(value):
        out = value[0:SUBLANES]
        for r in range(SUBLANES, rows, SUBLANES):
            out = out + value[r : r + SUBLANES]
        return out

    moments = [[None] * sources for _ in range(2 * ITERS)]

    def add(n, s, value):
        moments[n][s] = value if moments[n][s] is None else moments[n][s] + value

    for c in range(chunks):
        for s in range(sources):
            first = basis_refs[0][s, c] - (x_ref[s, c] - spread(x_ref, s, c))
            basis_refs[0][s, c] = first
            own = first[:rows]
            add(0, s, fold(diag_ref[c, :rows] * own * own))
    for i in range(ITERS):
        for c in range(chunks):
            for s in range(sources):
                new = spread(basis_refs[i], s, c)
                own = new[:rows]
                weighted = diag_ref[c, :rows] * own
                add(2 * i + 1, s, fold(weighted * basis_refs[i][s, c, :rows]))
                if i + 1 < ITERS:
                    basis_refs[i + 1][s, c] = new
                    add(2 * i + 2, s, fold(weighted * own))

    spot = (lax.broadcasted_iota(jnp.int32, (rows, LANES), 0)).astype(jnp.float32) + base
    picker = spot == par_ref[1:2, :]
    lines = []
    for ref in (x_ref, *basis_refs):
        for s in range(sources):
            top = jnp.broadcast_to(ref[s, 0, :rows, 0:1], (rows, LANES))
            lines.append(jnp.sum(fold(jnp.where(picker, top, 0.0)), axis=0, keepdims=True))
    for n in range(2 * ITERS):
        for s in range(sources):
            lines.append(jnp.sum(moments[n][s], axis=0, keepdims=True))
    pay_ref[...] = jnp.zeros(pay_ref.shape, jnp.float32)
    for i, line in enumerate(lines):
        pay_ref[i : i + 1, :] = line


def combine_kernel(waves, par_ref, pay_ref, *refs):
    part_refs = refs[: ITERS + 1]
    out_refs = refs[ITERS + 1 :]
    sources, chunks, total, _ = part_refs[0].shape
    n_parts = ITERS + 1
    first = n_parts * sources
    sums = jnp.sum(pay_ref[first : first + 2 * ITERS * sources, :], axis=1, keepdims=True)
    poly = step_polynomial(
        [sums[n * sources : (n + 1) * sources] for n in range(2 * ITERS)]
    )
    weight = par_ref[0:1, 0:1]
    scale = [[weight * p[s : s + 1] for p in poly] for s in range(sources)]
    read = []
    for s in range(sources):
        line = weight * pay_ref[s : s + 1, :]
        for i in range(ITERS):
            line = line + scale[s][i] * pay_ref[(i + 1) * sources + s : (i + 1) * sources + s + 1, :]
        read.append(line)
    share = out_refs[0].shape[1]
    rows = (out_refs[0].shape[0] - SUBLANES) // sources
    split = share % LANES == 0
    wave = lax.axis_index("wave") if split else 0
    per = share // LANES
    for mask, out_ref in enumerate(out_refs):
        block = wave ^ mask if split else 0
        for s in range(sources):
            for k in range(per):
                value = weight * part_refs[0][s, block * per + k, :rows]
                for i in range(ITERS):
                    value = value + scale[s][i] * part_refs[i + 1][s, block * per + k, :rows]
                out_ref[s * rows : (s + 1) * rows, k * LANES : (k + 1) * LANES] = value
        out_ref[sources * rows :, :] = jnp.zeros((SUBLANES, share), jnp.float32)
        for s in range(sources):
            out_ref[sources * rows + s : sources * rows + s + 1, :LANES] = read[s]


def sum_kernel(*refs):
    part_refs, (field_ref, read_ref) = refs[:-2], refs[-2:]
    sources, rows, share = field_ref.shape
    electrodes = read_ref.shape[1]
    for s in range(sources):
        field_ref[s] = tree_sum([r[s * rows : (s + 1) * rows, :] for r in part_refs])
    last = tree_sum([r[sources * rows :, :LANES] for r in part_refs])
    read_ref[...] = last[:sources, :electrodes]


def shards(
    warm_start,
    class_map,
    conductivities,
    wavenumbers,
    weights,
    source_row,
    source_col,
    electrode_row,
):
    rows, depth = class_map.shape
    sources = warm_start.shape[1]
    n_class = conductivities.shape[0]
    electrodes = electrode_row.shape[0]
    tiles, waves = lax.axis_size("tile"), lax.axis_size("wave")
    tile, wave = lax.axis_index("tile"), lax.axis_index("wave")
    halo = ITERS + 1
    even = tile % 2 == 0
    field = warm_start[0]

    def rim(at):
        ids = class_map[at : at + halo].astype(jnp.float32) + 1.0
        return jnp.concatenate([field[:, at : at + halo], ids[None]], axis=0)

    first, last = rim(0), rim(rows - halo)
    near = swap(jnp.where(even, last, first), "tile", 1, tiles)
    far_pairs = [(i, i + 1) for i in range(1, tiles - 1, 2)]
    far = lax.ppermute(
        jnp.where(even, first, last), "tile", far_pairs + [(j, i) for i, j in far_pairs]
    )
    params = jnp.concatenate(
        [
            conductivities,
            wavenumbers,
            weights,
            (tile * rows).astype(jnp.float32)[None],
            source_row.astype(jnp.float32),
            source_col.astype(jnp.float32),
        ]
    )
    params = jnp.stack(
        [
            jnp.pad(params, (0, LANES - params.shape[0])),
            jnp.pad(
                electrode_row.astype(jnp.float32), (0, LANES - electrodes), constant_values=-1.0
            ),
        ]
    )
    rim_wide = jnp.where(
        even, jnp.concatenate([near, far], axis=1), jnp.concatenate([far, near], axis=1)
    )
    total, chunks = rows + 2 * halo, depth // LANES
    f32 = jnp.float32
    wide = jax.ShapeDtypeStruct((sources, chunks, total, LANES), f32)
    n_lines = sources * (3 * ITERS + 1)
    lines = -(-n_lines // SUBLANES) * SUBLANES
    parts = vmem_call(
        functools.partial(stencil_kernel, n_class),
        [wide] * (ITERS + 1) + [jax.ShapeDtypeStruct((lines, LANES), f32)],
        [params, field, class_map, rim_wide],
        [pltpu.VMEM((chunks, total, LANES), f32)] * 7,
    )
    parts, packed = parts[:-1], parts[-1]
    packed = tile_total(packed, "tile")
    share = depth // waves
    split = share % LANES == 0
    width = share if split else depth
    block = jax.ShapeDtypeStruct((sources * rows + SUBLANES, width), f32)
    pieces = vmem_call(
        functools.partial(combine_kernel, waves),
        [block] * (waves if split else 1),
        [params[:, n_class + 1 : n_class + 2], packed, *parts],
    )
    if not split:
        n = sources * rows
        read = pieces[0][n : n + sources, :electrodes].reshape(-1, share)
        pieces = [
            jnp.concatenate(
                [lax.dynamic_slice_in_dim(pieces[0][:n], (wave ^ mask) * share, share, 1), read]
            )
            for mask in range(waves)
        ]
    pieces = [pieces[0]] + [swap(pieces[m], "wave", m, waves) for m in range(1, waves)]
    if not split:
        final = tree_sum(pieces)
        return (
            final[: sources * rows].reshape(sources, rows, share),
            final[sources * rows :].reshape(sources, electrodes),
        )
    return tuple(
        vmem_call(
            sum_kernel,
            [
                jax.ShapeDtypeStruct((sources, rows, share), f32),
                jax.ShapeDtypeStruct((sources, electrodes), f32),
            ],
            pieces,
        )
    )


def solution(mesh):
    return jax.shard_map(
        shards,
        mesh=mesh,
        in_specs=(
            P("wave", None, "tile", None),
            P("tile", None),
            P(),
            P("wave"),
            P("wave"),
            P(),
            P(),
            P(),
        ),
        out_specs=(P(None, "tile", "wave"), P()),
        check_vma=False,
    )
```

```python
import functools

import jax
import jax.numpy as jnp
from jax import lax
from jax.experimental import pallas as pl
from jax.experimental.pallas import tpu as pltpu
from jax.sharding import PartitionSpec as P

ITERS = 3
SOURCE_STRENGTH = 50.0
TINY = 1e-30
LANES = 128
SUBLANES = 8


def harmonic(left_val, right_val):
    return 2.0 * left_val * right_val / jnp.maximum(left_val + right_val, TINY)


def safe_div(num, den):
    return jnp.where(den > 0.0, num / jnp.where(den > 0.0, den, 1.0), 0.0)


def tree_sum(values):
    values = list(values)
    while len(values) > 1:
        values = [values[i] + values[i + 1] for i in range(0, len(values), 2)]
    return values[0]


def swap(value, axis, mask, size):
    return lax.ppermute(value, axis, [(i, i ^ mask) for i in range(size)])


def tile_total(value, axis):
    size = lax.axis_size(axis)
    bit = 1
    while bit < size:
        masks = [bit]
        if bit > 1 and bit * 2 < size:
            masks.append(bit * 2)
        offsets = [0]
        for mask in masks:
            offsets += [o ^ mask for o in offsets]
        value = tree_sum([value] + [swap(value, axis, o, size) for o in offsets[1:]])
        bit = masks[-1] * 2
    return value


def step_polynomial(moments):
    def inner(poly):
        return sum(a * b * moments[i + j] for i, a in enumerate(poly) for j, b in enumerate(poly))

    def energy(poly):
        return sum(
            a * b * (moments[i + j] - moments[i + j + 1])
            for i, a in enumerate(poly)
            for j, b in enumerate(poly)
        )

    one = jnp.ones_like(moments[0])
    zero = jnp.zeros_like(moments[0])
    res, way, total = [one], [one], [zero] * ITERS
    gamma = moments[0]
    for iteration in range(ITERS):
        alpha = safe_div(gamma, energy(way))
        total = [t + alpha * (way[i] if i < len(way) else zero) for i, t in enumerate(total)]
        if iteration + 1 < ITERS:
            longer = way + [zero]
            shifted = [zero] + way
            res = [r - alpha * (a - b) for r, a, b in zip(res + [zero], longer, shifted)]
            gamma_next = jnp.maximum(inner(res), 0.0)
            ratio = safe_div(gamma_next, gamma)
            way = [r + ratio * a for r, a in zip(res, longer)]
            gamma = gamma_next
    return total


def vmem_call(kernel, out_shape, inputs, scratch=()):
    spec = pl.BlockSpec(memory_space=pltpu.VMEM)
    return pl.pallas_call(
        kernel,
        out_shape=out_shape,
        in_specs=[spec] * len(inputs),
        out_specs=jax.tree.map(lambda _: spec, out_shape),
        scratch_shapes=list(scratch),
        compiler_params=pltpu.CompilerParams(vmem_limit_bytes=16 << 20),
    )(*inputs)


def stencil_kernel(
    n_class, par_ref, field_ref, class_ref, halo_ref, *refs
):
    x_ref = refs[0]
    basis_refs = refs[1 : 1 + ITERS]
    pay_ref, sig_ref, left_ref, up_ref, down_ref, west_ref, east_ref, diag_ref = refs[1 + ITERS :]
    sources, rows, depth = field_ref.shape
    total = x_ref.shape[2]
    chunks = depth // LANES
    lane = lax.broadcasted_iota(jnp.int32, (total, LANES), 1)
    row = lax.broadcasted_iota(jnp.int32, (total, LANES), 0)

    def scalar(i):
        return par_ref[0:1, i : i + 1]

    def cols(c):
        return slice(c * LANES, (c + 1) * LANES)

    values = [scalar(i) for i in range(n_class)]
    square = scalar(n_class) * scalar(n_class)
    base = scalar(n_class + 2)
    for c in range(chunks):
        ids = jnp.concatenate(
            [class_ref[:, cols(c)].astype(jnp.float32) + 1.0, halo_ref[sources, :, cols(c)]], axis=0
        )
        sigma = jnp.zeros((total, LANES), jnp.float32)
        for i, value in enumerate(values):
            sigma = jnp.where(ids == i + 1.0, value, sigma)
        sig_ref[c] = sigma
        for s in range(sources):
            x_ref[s, c] = jnp.concatenate([field_ref[s, :, cols(c)], halo_ref[s, :, cols(c)]], axis=0)

    def from_left(ref, c):
        here = pltpu.roll(ref[c], 1, 1)
        other = pltpu.roll(ref[c - 1 if c else chunks - 1], 1, 1)
        return jnp.where(lane == 0, other, here)

    def from_right(ref, c):
        here = pltpu.roll(ref[c], LANES - 1, 1)
        other = pltpu.roll(ref[(c + 1) % chunks], LANES - 1, 1)
        return jnp.where(lane == LANES - 1, other, here)

    for c in range(chunks):
        face = harmonic(from_left(sig_ref, c), sig_ref[c])
        left_ref[c] = jnp.where(lane == 0, 0.0, face) if c == 0 else face

    far_row = jnp.where(row < total - (total - rows) // 2, row, row - total).astype(jnp.float32)
    for c in range(chunks):
        sigma = sig_ref[c]
        up = harmonic(pltpu.roll(sigma, 1, 0), sigma)
        down = pltpu.roll(up, total - 1, 0)
        left = left_ref[c]
        right = from_right(left_ref, c)
        diag = up + down + left + right + square * sigma
        if c == chunks - 1:
            diag = diag + jnp.where(lane == LANES - 1, sigma, 0.0)
        inverse = 1.0 / jnp.maximum(diag, TINY)
        diag_ref[c] = diag
        up_ref[c] = up * inverse
        down_ref[c] = down * inverse
        west_ref[c] = left * inverse
        east_ref[c] = right * inverse
        for s in range(sources):
            hit = (far_row + base == scalar(n_class + 3 + s)) & (
                (lane + c * LANES).astype(jnp.float32) == scalar(n_class + 3 + sources + s)
            )
            basis_refs[0][s, c] = jnp.where(hit, SOURCE_STRENGTH * inverse, 0.0)

    def spread(ref, s, c):
        here = ref[s, c]
        return (
            up_ref[c] * pltpu.roll(here, 1, 0)
            + down_ref[c] * pltpu.roll(here, total - 1, 0)
            + west_ref[c] * from_left(ref.at[s], c)
            + east_ref[c] * from_right(ref.at[s], c)
        )

    def fold(value):
        out = value[0:SUBLANES]
        for r in range(SUBLANES, rows, SUBLANES):
            out = out + value[r : r + SUBLANES]
        return out

    moments = [[None] * sources for _ in range(2 * ITERS)]

    def add(n, s, value):
        moments[n][s] = value if moments[n][s] is None else moments[n][s] + value

    for c in range(chunks):
        for s in range(sources):
            first = basis_refs[0][s, c] - (x_ref[s, c] - spread(x_ref, s, c))
            basis_refs[0][s, c] = first
            own = first[:rows]
            add(0, s, fold(diag_ref[c, :rows] * own * own))
    for i in range(ITERS):
        for c in range(chunks):
            for s in range(sources):
                new = spread(basis_refs[i], s, c)
                own = new[:rows]
                weighted = diag_ref[c, :rows] * own
                add(2 * i + 1, s, fold(weighted * basis_refs[i][s, c, :rows]))
                if i + 1 < ITERS:
                    basis_refs[i + 1][s, c] = new
                    add(2 * i + 2, s, fold(weighted * own))

    spot = (lax.broadcasted_iota(jnp.int32, (rows, LANES), 0)).astype(jnp.float32) + base
    picker = spot == par_ref[1:2, :]
    lines = []
    for ref in (x_ref, *basis_refs):
        for s in range(sources):
            top = jnp.broadcast_to(ref[s, 0, :rows, 0:1], (rows, LANES))
            lines.append(jnp.sum(fold(jnp.where(picker, top, 0.0)), axis=0, keepdims=True))
    for n in range(2 * ITERS):
        for s in range(sources):
            lines.append(jnp.sum(moments[n][s], axis=0, keepdims=True))
    pay_ref[...] = jnp.zeros(pay_ref.shape, jnp.float32)
    for i, line in enumerate(lines):
        pay_ref[i : i + 1, :] = line


def combine_kernel(waves, par_ref, pay_ref, *refs):
    part_refs = refs[: ITERS + 1]
    out_refs = refs[ITERS + 1 :]
    sources, chunks, total, _ = part_refs[0].shape
    n_parts = ITERS + 1
    first = n_parts * sources
    sums = jnp.sum(pay_ref[first : first + 2 * ITERS * sources, :], axis=1, keepdims=True)
    poly = step_polynomial(
        [sums[n * sources : (n + 1) * sources] for n in range(2 * ITERS)]
    )
    weight = par_ref[0:1, 0:1]
    scale = [[weight * p[s : s + 1] for p in poly] for s in range(sources)]
    read = []
    for s in range(sources):
        line = weight * pay_ref[s : s + 1, :]
        for i in range(ITERS):
            line = line + scale[s][i] * pay_ref[(i + 1) * sources + s : (i + 1) * sources + s + 1, :]
        read.append(line)
    share = out_refs[0].shape[1]
    rows = (out_refs[0].shape[0] - SUBLANES) // sources
    split = share % LANES == 0
    wave = lax.axis_index("wave") if split else 0
    per = share // LANES
    for mask, out_ref in enumerate(out_refs):
        block = wave ^ mask if split else 0
        for s in range(sources):
            for k in range(per):
                value = weight * part_refs[0][s, block * per + k, :rows]
                for i in range(ITERS):
                    value = value + scale[s][i] * part_refs[i + 1][s, block * per + k, :rows]
                out_ref[s * rows : (s + 1) * rows, k * LANES : (k + 1) * LANES] = value
        out_ref[sources * rows :, :] = jnp.zeros((SUBLANES, share), jnp.float32)
        for s in range(sources):
            out_ref[sources * rows + s : sources * rows + s + 1, :LANES] = read[s]


def sum_kernel(*refs):
    part_refs, (field_ref, read_ref) = refs[:-2], refs[-2:]
    sources, rows, share = field_ref.shape
    electrodes = read_ref.shape[1]
    for s in range(sources):
        field_ref[s] = tree_sum([r[s * rows : (s + 1) * rows, :] for r in part_refs])
    last = tree_sum([r[sources * rows :, :LANES] for r in part_refs])
    read_ref[...] = last[:sources, :electrodes]


def shards(
    warm_start,
    class_map,
    conductivities,
    wavenumbers,
    weights,
    source_row,
    source_col,
    electrode_row,
):
    rows, depth = class_map.shape
    sources = warm_start.shape[1]
    n_class = conductivities.shape[0]
    electrodes = electrode_row.shape[0]
    tiles, waves = lax.axis_size("tile"), lax.axis_size("wave")
    tile, wave = lax.axis_index("tile"), lax.axis_index("wave")
    halo = ITERS + 1
    even = tile % 2 == 0
    field = warm_start[0]

    def rim(at):
        ids = class_map[at : at + halo].astype(jnp.float32) + 1.0
        return jnp.concatenate([field[:, at : at + halo], ids[None]], axis=0)

    first, last = rim(0), rim(rows - halo)
    near = swap(jnp.where(even, last, first), "tile", 1, tiles)
    far_pairs = [(i, i + 1) for i in range(1, tiles - 1, 2)]
    far = lax.ppermute(
        jnp.where(even, first, last), "tile", far_pairs + [(j, i) for i, j in far_pairs]
    )
    params = jnp.concatenate(
        [
            conductivities,
            wavenumbers,
            weights,
            (tile * rows).astype(jnp.float32)[None],
            source_row.astype(jnp.float32),
            source_col.astype(jnp.float32),
        ]
    )
    params = jnp.stack(
        [
            jnp.pad(params, (0, LANES - params.shape[0])),
            jnp.pad(
                electrode_row.astype(jnp.float32), (0, LANES - electrodes), constant_values=-1.0
            ),
        ]
    )
    rim_wide = jnp.where(
        even, jnp.concatenate([near, far], axis=1), jnp.concatenate([far, near], axis=1)
    )
    total, chunks = rows + 2 * halo, depth // LANES
    f32 = jnp.float32
    wide = jax.ShapeDtypeStruct((sources, chunks, total, LANES), f32)
    n_lines = sources * (3 * ITERS + 1)
    lines = -(-n_lines // SUBLANES) * SUBLANES
    parts = vmem_call(
        functools.partial(stencil_kernel, n_class),
        [wide] * (ITERS + 1) + [jax.ShapeDtypeStruct((lines, LANES), f32)],
        [params, field, class_map, rim_wide],
        [pltpu.VMEM((chunks, total, LANES), f32)] * 7,
    )
    parts, packed = parts[:-1], parts[-1]
    packed = tile_total(packed, "tile")
    share = depth // waves
    split = share % LANES == 0
    width = share if split else depth
    block = jax.ShapeDtypeStruct((sources * rows + SUBLANES, width), f32)
    pieces = vmem_call(
        functools.partial(combine_kernel, waves),
        [block] * (waves if split else 1),
        [params[:, n_class + 1 : n_class + 2], packed, *parts],
    )
    if not split:
        n = sources * rows
        read = pieces[0][n : n + sources, :electrodes].reshape(-1, share)
        pieces = [
            jnp.concatenate(
                [lax.dynamic_slice_in_dim(pieces[0][:n], (wave ^ mask) * share, share, 1), read]
            )
            for mask in range(waves)
        ]
    pieces = [pieces[0]] + [swap(pieces[m], "wave", m, waves) for m in range(1, waves)]
    if not split:
        final = tree_sum(pieces)
        return (
            final[: sources * rows].reshape(sources, rows, share),
            final[sources * rows :].reshape(sources, electrodes),
        )
    return tuple(
        vmem_call(
            sum_kernel,
            [
                jax.ShapeDtypeStruct((sources, rows, share), f32),
                jax.ShapeDtypeStruct((sources, electrodes), f32),
            ],
            pieces,
        )
    )


def solution(mesh):
    return jax.shard_map(
        shards,
        mesh=mesh,
        in_specs=(
            P("wave", None, "tile", None),
            P("tile", None),
            P(),
            P("wave"),
            P("wave"),
            P(),
            P(),
            P(),
        ),
        out_specs=(P(None, "tile", "wave"), P()),
        check_vma=False,
    )
```

```python
import functools

import jax
import jax.numpy as jnp
from jax import lax
from jax.experimental import pallas as pl
from jax.experimental.pallas import tpu as pltpu
from jax.sharding import PartitionSpec as P

ITERS = 3
SOURCE_STRENGTH = 50.0
TINY = 1e-30
LANES = 128
SUBLANES = 8


def harmonic(left_val, right_val):
    return 2.0 * left_val * right_val / jnp.maximum(left_val + right_val, TINY)


def safe_div(num, den):
    return jnp.where(den > 0.0, num / jnp.where(den > 0.0, den, 1.0), 0.0)


def tree_sum(values):
    values = list(values)
    while len(values) > 1:
        values = [values[i] + values[i + 1] for i in range(0, len(values), 2)]
    return values[0]


def swap(value, axis, mask, size):
    return lax.ppermute(value, axis, [(i, i ^ mask) for i in range(size)])


def tile_parts(value, axis):
    size = lax.axis_size(axis)
    parts = [value]
    bit = 1
    while bit < size:
        value = tree_sum(parts)
        masks = [bit]
        if bit > 1 and bit * 2 < size:
            masks.append(bit * 2)
        offsets = [0]
        for mask in masks:
            offsets += [o ^ mask for o in offsets]
        parts = [value] + [swap(value, axis, o, size) for o in offsets[1:]]
        bit = masks[-1] * 2
    return parts


def step_polynomial(moments):
    def inner(poly):
        return sum(a * b * moments[i + j] for i, a in enumerate(poly) for j, b in enumerate(poly))

    def energy(poly):
        return sum(
            a * b * (moments[i + j] - moments[i + j + 1])
            for i, a in enumerate(poly)
            for j, b in enumerate(poly)
        )

    one = jnp.ones_like(moments[0])
    zero = jnp.zeros_like(moments[0])
    res, way, total = [one], [one], [zero] * ITERS
    gamma = moments[0]
    for iteration in range(ITERS):
        alpha = safe_div(gamma, energy(way))
        total = [t + alpha * (way[i] if i < len(way) else zero) for i, t in enumerate(total)]
        if iteration + 1 < ITERS:
            longer = way + [zero]
            shifted = [zero] + way
            res = [r - alpha * (a - b) for r, a, b in zip(res + [zero], longer, shifted)]
            gamma_next = jnp.maximum(inner(res), 0.0)
            ratio = safe_div(gamma_next, gamma)
            way = [r + ratio * a for r, a in zip(res, longer)]
            gamma = gamma_next
    return total


VMEM = pl.BlockSpec(memory_space=pltpu.VMEM)
PARAMS = pltpu.CompilerParams(vmem_limit_bytes=16 << 20)


def vmem_call(kernel, out_shape, inputs, scratch=()):
    return pl.pallas_call(
        kernel,
        out_shape=out_shape,
        in_specs=[VMEM] * len(inputs),
        out_specs=jax.tree.map(lambda _: VMEM, out_shape),
        scratch_shapes=list(scratch),
        compiler_params=PARAMS,
    )(*inputs)


def cols(c):
    return slice(c * LANES, (c + 1) * LANES)


def add(sums, key, value):
    sums[key] = sums[key] + value if key in sums else value


def edge_kernel(field_hbm, class_hbm, far_ref, near_ref, field_ref, class_ref, sems):
    sources, rows, _ = field_hbm.shape
    halo = far_ref.shape[1]
    copies = []
    for i, at in enumerate((0, rows - SUBLANES)):
        copies.append(
            pltpu.make_async_copy(
                field_hbm.at[:, pl.ds(at, SUBLANES)], field_ref.at[i], sems.at[2 * i]
            )
        )
        copies.append(
            pltpu.make_async_copy(
                class_hbm.at[pl.ds(at, SUBLANES)], class_ref.at[i], sems.at[2 * i + 1]
            )
        )
    for copy in copies:
        copy.start()
    for copy in copies:
        copy.wait()
    even = lax.axis_index("tile") % 2 == 0
    spare = SUBLANES - halo
    for s in range(sources):
        first, last = field_ref[0, s, :halo], field_ref[1, s, spare:]
        far_ref[s] = jnp.where(even, first, last)
        near_ref[s] = jnp.where(even, last, first)
    first = class_ref[0, :halo].astype(jnp.float32) + 1.0
    last = class_ref[1, spare:].astype(jnp.float32) + 1.0
    far_ref[sources] = jnp.where(even, first, last)
    near_ref[sources] = jnp.where(even, last, first)


def from_left(value, other, lane):
    return jnp.where(lane == 0, pltpu.roll(other, 1, 1), pltpu.roll(value, 1, 1))


def from_right(value, other, lane):
    last = LANES - 1
    return jnp.where(lane == last, pltpu.roll(other, last, 1), pltpu.roll(value, last, 1))


def conductivity(ids, cond_ref):
    sigma = jnp.zeros(ids.shape, jnp.float32)
    for i in range(cond_ref.shape[1]):
        sigma = jnp.where(ids == i + 1.0, cond_ref[0:1, i : i + 1], sigma)
    return sigma


def west_faces(sigmas, lane):
    faces = []
    for c, sigma in enumerate(sigmas):
        face = harmonic(from_left(sigma, sigmas[c - 1], lane), sigma)
        faces.append(jnp.where(lane == 0, 0.0, face) if c == 0 else face)
    return faces


def diagonal(up, down, west, east, sigma, square, lane, bottom):
    diag = up + down + west + east + square * sigma
    if bottom:
        diag = diag + jnp.where(lane == LANES - 1, sigma, 0.0)
    return diag, 1.0 / jnp.maximum(diag, TINY)


def source_term(rows_at, lane, c, s, row_ref, col_ref, inverse):
    hit = (rows_at == row_ref[0:1, s : s + 1]) & (lane + c * LANES == col_ref[0:1, s : s + 1])
    return jnp.where(hit, SOURCE_STRENGTH * inverse, 0.0)


def line_sum(value):
    return jnp.sum(value, axis=0, keepdims=True)


def lines_of(tops, sums, sources):
    lines = list(tops)
    for n in range(2 * ITERS):
        for s in range(sources):
            lines.append(line_sum(sums[n, s]))
    return lines


def inner_kernel(
    field_ref, class_ref, cond_ref, wave_ref, row_ref, col_ref, pick_ref, *refs
):
    x_ref, *basis_refs = refs[: 1 + ITERS]
    pay_ref, sig_ref, face_ref = refs[1 + ITERS : 4 + ITERS]
    up_ref, down_ref, west_ref, east_ref, diag_ref, scaled_ref = refs[4 + ITERS :]
    sources, rows, _ = field_ref.shape
    chunks, total = x_ref.shape[1:3]
    halo = (total - rows) // 2
    lane = lax.broadcasted_iota(jnp.int32, (total, LANES), 1)
    row = lax.broadcasted_iota(jnp.int32, (total, LANES), 0)
    rows_at = row + (lax.axis_index("tile") * rows - halo)
    blank = jnp.zeros((halo, LANES), jnp.float32)
    square = wave_ref[...] * wave_ref[...]
    inner = slice(SUBLANES, total - SUBLANES)

    def widened(value):
        return jnp.concatenate([blank, value, blank], axis=0)

    for c in range(chunks):
        ids = class_ref[:, cols(c)].astype(jnp.float32) + 1.0
        sig_ref[c] = widened(conductivity(ids, cond_ref))
        for s in range(sources):
            x_ref[s, c] = widened(field_ref[s, :, cols(c)])
    for c in range(chunks):
        sigma = sig_ref[c]
        face = harmonic(from_left(sigma, sig_ref[c - 1 if c else chunks - 1], lane), sigma)
        west_ref[c] = jnp.where(lane == 0, 0.0, face) if c == 0 else face
    for c in range(chunks):
        sigma = sig_ref[c]
        up = harmonic(pltpu.roll(sigma, 1, 0), sigma)
        face_ref[c] = up
        down = pltpu.roll(up, total - 1, 0)
        east = from_right(west_ref[c], west_ref[(c + 1) % chunks], lane)
        diag, inverse = diagonal(
            up, down, west_ref[c], east, sigma, square, lane, c == chunks - 1
        )
        diag_ref[c] = diag
        up_ref[c] = up * inverse
        down_ref[c] = down * inverse
        for s in range(sources):
            basis_refs[0][s, c] = source_term(rows_at, lane, c, s, row_ref, col_ref, inverse)
        east_ref[c] = east * inverse
        scaled_ref[c] = west_ref[c] * inverse

    def spread(ref, s, c):
        here = ref[s, c]
        return (
            up_ref[c] * pltpu.roll(here, 1, 0)
            + down_ref[c] * pltpu.roll(here, total - 1, 0)
            + scaled_ref[c] * from_left(here, ref[s, c - 1 if c else chunks - 1], lane)
            + east_ref[c] * from_right(here, ref[s, (c + 1) % chunks], lane)
        )

    def fold(value):
        return sum(value[r : r + SUBLANES] for r in range(0, value.shape[0], SUBLANES))

    sums = {}
    for c in range(chunks):
        for s in range(sources):
            first = basis_refs[0][s, c] - (x_ref[s, c] - spread(x_ref, s, c))
            basis_refs[0][s, c] = first
            own = first[inner]
            add(sums, (0, s), fold(diag_ref[c, inner] * own * own))
    for i in range(ITERS):
        for c in range(chunks):
            for s in range(sources):
                new = spread(basis_refs[i], s, c)
                own = new[inner]
                weighted = diag_ref[c, inner] * own
                add(sums, (2 * i + 1, s), fold(weighted * basis_refs[i][s, c, inner]))
                if i + 1 < ITERS:
                    basis_refs[i + 1][s, c] = new
                    add(sums, (2 * i + 2, s), fold(weighted * own))
    picker = rows_at[inner] == pick_ref[...]
    tops = []
    for ref in (x_ref, *basis_refs):
        for s in range(sources):
            top = jnp.broadcast_to(ref[s, 0, inner, 0:1], (total - 2 * SUBLANES, LANES))
            tops.append(line_sum(fold(jnp.where(picker, top, 0.0))))
    pay_ref[...] = jnp.zeros(pay_ref.shape, jnp.float32)
    for i, line in enumerate(lines_of(tops, sums, sources)):
        pay_ref[i : i + 1, :] = line


def outer_kernel(
    far_ref, near_ref, cond_ref, wave_ref, row_ref, col_ref, pick_ref, *refs
):
    x_in, *basis_in = refs[: 1 + ITERS]
    pay_in, sig_in, face_in = refs[1 + ITERS : 4 + ITERS]
    outs = refs[4 + ITERS :]
    x_ref, *basis_refs = outs[: 1 + ITERS]
    pay_ref = outs[1 + ITERS]
    up_ref, down_ref, west_ref, east_ref, diag_ref = outs[2 + ITERS :]
    sources, chunks, total, _ = x_in.shape
    halo = far_ref.shape[1]
    rows = total - 2 * halo
    lane = lax.broadcasted_iota(jnp.int32, (SUBLANES, LANES), 1)
    row = lax.broadcasted_iota(jnp.int32, (SUBLANES, LANES), 0)
    tile = lax.axis_index("tile")
    even = tile % 2 == 0
    square = wave_ref[...] * wave_ref[...]
    ends = (0, 1)
    starts = (0, total - SUBLANES)
    own = (row >= halo, row < SUBLANES - halo)
    rows_at = [row + (tile * rows - halo + at) for at in starts]

    def edge(index, c, inside):
        far, near = far_ref[index, :, cols(c)], near_ref[index, :, cols(c)]
        before, after = jnp.where(even, far, near), jnp.where(even, near, far)
        return (
            jnp.concatenate([before, inside[0]], axis=0),
            jnp.concatenate([inside[1], after], axis=0),
        )

    inside = (slice(halo, SUBLANES), slice(total - SUBLANES, total - halo))
    sigmas = []
    for c in range(chunks):
        both = edge(sources, c, [jnp.zeros((SUBLANES - halo, LANES), jnp.float32)] * 2)
        kept = (sig_in[c, :SUBLANES], sig_in[c, total - SUBLANES :])
        sigmas.append(
            [jnp.where(own[e], kept[e], conductivity(both[e], cond_ref)) for e in ends]
        )
        for s in range(sources):
            both = edge(s, c, [x_in[s, c, i] for i in inside])
            for e in ends:
                x_ref[e, s, c] = both[e]
    west = [west_faces([sigmas[c][e] for c in range(chunks)], lane) for e in ends]
    last = total - SUBLANES
    for c in range(chunks):
        for e in ends:
            sigma = sigmas[c][e]
            above = pltpu.roll(sigma, 1, 0)
            if e:
                above = jnp.where(row == 0, pltpu.roll(sig_in[c, last - SUBLANES : last], 1, 0), above)
            up = harmonic(above, sigma)
            down = pltpu.roll(up, SUBLANES - 1, 0)
            if not e:
                down = jnp.where(
                    row == SUBLANES - 1,
                    pltpu.roll(face_in[c, SUBLANES : 2 * SUBLANES], SUBLANES - 1, 0),
                    down,
                )
            east = from_right(west[e][c], west[e][(c + 1) % chunks], lane)
            diag, inverse = diagonal(
                up, down, west[e][c], east, sigma, square, lane, c == chunks - 1
            )
            diag_ref[e, c] = jnp.where(own[e], diag, 0.0)
            up_ref[e, c] = up * inverse
            down_ref[e, c] = down * inverse
            west_ref[e, c] = west[e][c] * inverse
            east_ref[e, c] = east * inverse
            for s in range(sources):
                basis_refs[0][e, s, c] = source_term(
                    rows_at[e], lane, c, s, row_ref, col_ref, inverse
                )

    def spread(ref, whole, e, s, c):
        here = ref[e, s, c]
        above = pltpu.roll(here, 1, 0)
        below = pltpu.roll(here, SUBLANES - 1, 0)
        if e:
            above = jnp.where(
                row == 0, pltpu.roll(whole[s, c, last - SUBLANES : last], 1, 0), above
            )
        else:
            below = jnp.where(
                row == SUBLANES - 1,
                pltpu.roll(whole[s, c, SUBLANES : 2 * SUBLANES], SUBLANES - 1, 0),
                below,
            )
        return (
            up_ref[e, c] * above
            + down_ref[e, c] * below
            + west_ref[e, c] * from_left(here, ref[e, s, c - 1 if c else chunks - 1], lane)
            + east_ref[e, c] * from_right(here, ref[e, s, (c + 1) % chunks], lane)
        )

    sums = {}
    for c in range(chunks):
        for e in ends:
            for s in range(sources):
                first = basis_refs[0][e, s, c] - (x_ref[e, s, c] - spread(x_ref, x_in, e, s, c))
                basis_refs[0][e, s, c] = first
                add(sums, (0, s), diag_ref[e, c] * first * first)
    for i in range(ITERS):
        for c in range(chunks):
            for e in ends:
                for s in range(sources):
                    new = spread(basis_refs[i], basis_in[i], e, s, c)
                    weighted = diag_ref[e, c] * new
                    add(sums, (2 * i + 1, s), weighted * basis_refs[i][e, s, c])
                    if i + 1 < ITERS:
                        basis_refs[i + 1][e, s, c] = new
                        add(sums, (2 * i + 2, s), weighted * new)
    tops = []
    for ref in (x_ref, *basis_refs):
        for s in range(sources):
            line = 0.0
            for e in ends:
                picker = own[e] & (rows_at[e] == pick_ref[...])
                top = jnp.broadcast_to(ref[e, s, 0, :, 0:1], (SUBLANES, LANES))
                line = line + jnp.where(picker, top, 0.0)
            tops.append(line_sum(line))
    pay_ref[...] = pay_in[...]
    for i, line in enumerate(lines_of(tops, sums, sources)):
        pay_ref[i : i + 1, :] += line


def combine_kernel(n_pay, weight_ref, *refs):
    n_parts = ITERS + 1
    packed = tree_sum([r[...] for r in refs[:n_pay]])
    part_refs = refs[n_pay : n_pay + n_parts]
    edge_refs = refs[n_pay + n_parts : n_pay + 2 * n_parts]
    out_refs = refs[n_pay + 2 * n_parts :]
    sources, _, total, _ = part_refs[0].shape
    share = out_refs[0].shape[1]
    rows = (out_refs[0].shape[0] - SUBLANES) // sources
    halo = (total - rows) // 2
    first = n_parts * sources
    totals = jnp.sum(packed[first : first + 2 * ITERS * sources], axis=1, keepdims=True)
    poly = step_polynomial([totals[n * sources : (n + 1) * sources] for n in range(2 * ITERS)])
    weight = weight_ref[...]
    scale = [[weight] + [weight * p[s : s + 1] for p in poly] for s in range(sources)]
    read = [
        sum(scale[s][i] * packed[i * sources + s : i * sources + s + 1] for i in range(n_parts))
        for s in range(sources)
    ]
    split = len(out_refs) > 1
    wave = lax.axis_index("wave") if split else 0
    per = share // LANES
    inner = slice(SUBLANES, total - SUBLANES)
    for mask, out_ref in enumerate(out_refs):
        block = wave ^ mask if split else 0
        for s in range(sources):
            for k in range(per):
                c = block * per + k
                middle = sum(scale[s][i] * part_refs[i][s, c, inner] for i in range(n_parts))
                top, end = (
                    sum(scale[s][i] * edge_refs[i][e, s, c] for i in range(n_parts)) for e in (0, 1)
                )
                value = jnp.concatenate([top[halo:], middle, end[: SUBLANES - halo]], axis=0)
                out_ref[s * rows : (s + 1) * rows, cols(k)] = value
        out_ref[sources * rows :, :] = jnp.zeros((SUBLANES, share), jnp.float32)
        for s in range(sources):
            out_ref[sources * rows + s : sources * rows + s + 1, :LANES] = read[s]


def sum_kernel(*refs):
    part_refs, (field_ref, read_ref) = refs[:-2], refs[-2:]
    sources, rows, _ = field_ref.shape
    electrodes = read_ref.shape[1]
    for s in range(sources):
        field_ref[s] = tree_sum([r[s * rows : (s + 1) * rows, :] for r in part_refs])
    last = tree_sum([r[sources * rows :, :LANES] for r in part_refs])
    read_ref[...] = last[:sources, :electrodes]


def shards(
    warm_start,
    class_map,
    conductivities,
    wavenumbers,
    weights,
    source_row,
    source_col,
    electrode_row,
):
    rows, depth = class_map.shape
    sources = warm_start.shape[1]
    electrodes = electrode_row.shape[0]
    tiles, waves = lax.axis_size("tile"), lax.axis_size("wave")
    wave = lax.axis_index("wave")
    halo = ITERS + 1
    field = warm_start[0]
    f32 = jnp.float32
    rim = jax.ShapeDtypeStruct((sources + 1, halo, depth), f32)
    hbm = pl.BlockSpec(memory_space=pltpu.HBM)
    far, near = pl.pallas_call(
        edge_kernel,
        out_shape=[rim, rim],
        in_specs=[hbm, hbm],
        out_specs=[VMEM, VMEM],
        scratch_shapes=[
            pltpu.VMEM((2, sources, SUBLANES, depth), f32),
            pltpu.VMEM((2, SUBLANES, depth), jnp.int32),
            pltpu.SemaphoreType.DMA((4,)),
        ],
        compiler_params=PARAMS,
    )(field, class_map)
    far_pairs = [(i, i + 1) for i in range(1, tiles - 1, 2)]
    far = lax.ppermute(far, "tile", far_pairs + [(j, i) for i, j in far_pairs])
    near = swap(near, "tile", 1, tiles)
    total, chunks = rows + 2 * halo, depth // LANES
    small = [
        conductivities[None],
        wavenumbers[None],
        source_row[None],
        source_col[None],
        jnp.pad(electrode_row, (0, LANES - electrodes), constant_values=-1)[None],
    ]
    wide = jax.ShapeDtypeStruct((sources, chunks, total, LANES), f32)
    flat = jax.ShapeDtypeStruct((chunks, total, LANES), f32)
    n_lines = sources * (3 * ITERS + 1)
    pay = jax.ShapeDtypeStruct((-(-n_lines // SUBLANES) * SUBLANES, LANES), f32)
    inside = vmem_call(
        inner_kernel,
        [wide] * (ITERS + 1) + [pay, flat, flat],
        [field, class_map, *small],
        [pltpu.VMEM((chunks, total, LANES), f32)] * 6,
    )
    ends = jax.ShapeDtypeStruct((2, sources, chunks, SUBLANES, LANES), f32)
    outside = vmem_call(
        outer_kernel,
        [ends] * (ITERS + 1) + [pay],
        [far, near, *small, *inside],
        [pltpu.VMEM((2, chunks, SUBLANES, LANES), f32)] * 5,
    )
    packed = tile_parts(outside[-1], "tile")
    share = depth // waves
    split = share % LANES == 0
    width = share if split else depth
    block = jax.ShapeDtypeStruct((sources * rows + SUBLANES, width), f32)
    pieces = vmem_call(
        functools.partial(combine_kernel, len(packed)),
        [block] * (waves if split else 1),
        [weights[None], *packed, *inside[: ITERS + 1], *outside[: ITERS + 1]],
    )
    if not split:
        n = sources * rows
        read = pieces[0][n : n + sources, :electrodes].reshape(-1, share)
        pieces = [
            jnp.concatenate(
                [lax.dynamic_slice_in_dim(pieces[0][:n], (wave ^ mask) * share, share, 1), read]
            )
            for mask in range(waves)
        ]
    pieces = [pieces[0]] + [swap(pieces[m], "wave", m, waves) for m in range(1, waves)]
    if not split:
        final = tree_sum(pieces)
        return (
            final[: sources * rows].reshape(sources, rows, share),
            final[sources * rows :].reshape(sources, electrodes),
        )
    return tuple(
        vmem_call(
            sum_kernel,
            [
                jax.ShapeDtypeStruct((sources, rows, share), f32),
                jax.ShapeDtypeStruct((sources, electrodes), f32),
            ],
            pieces,
        )
    )


def solution(mesh):
    return jax.shard_map(
        shards,
        mesh=mesh,
        in_specs=(
            P("wave", None, "tile", None),
            P("tile", None),
            P(),
            P("wave"),
            P("wave"),
            P(),
            P(),
            P(),
        ),
        out_specs=(P(None, "tile", "wave"), P()),
        check_vma=False,
    )
```

```python
import functools

import jax
import jax.numpy as jnp
from jax import lax
from jax.experimental import pallas as pl
from jax.experimental.pallas import tpu as pltpu
from jax.sharding import PartitionSpec as P

ITERS = 3
SOURCE_STRENGTH = 50.0
TINY = 1e-30
LANES = 128
SUBLANES = 8


def harmonic(left_val, right_val):
    return 2.0 * left_val * right_val / jnp.maximum(left_val + right_val, TINY)


def safe_div(num, den):
    return jnp.where(den > 0.0, num / jnp.where(den > 0.0, den, 1.0), 0.0)


def tree_sum(values):
    values = list(values)
    while len(values) > 1:
        values = [values[i] + values[i + 1] for i in range(0, len(values), 2)]
    return values[0]


def swap(value, axis, mask, size):
    return lax.ppermute(value, axis, [(i, i ^ mask) for i in range(size)])


def tile_parts(value, axis):
    size = lax.axis_size(axis)
    parts = [value]
    bit = 1
    while bit < size:
        value = tree_sum(parts)
        masks = [bit]
        if bit > 1 and bit * 2 < size:
            masks.append(bit * 2)
        offsets = [0]
        for mask in masks:
            offsets += [o ^ mask for o in offsets]
        parts = [value] + [swap(value, axis, o, size) for o in offsets[1:]]
        bit = masks[-1] * 2
    return parts


def step_polynomial(moments):
    def inner(poly):
        return sum(a * b * moments[i + j] for i, a in enumerate(poly) for j, b in enumerate(poly))

    def energy(poly):
        return sum(
            a * b * (moments[i + j] - moments[i + j + 1])
            for i, a in enumerate(poly)
            for j, b in enumerate(poly)
        )

    one = jnp.ones_like(moments[0])
    zero = jnp.zeros_like(moments[0])
    res, way, total = [one], [one], [zero] * ITERS
    gamma = moments[0]
    for iteration in range(ITERS):
        alpha = safe_div(gamma, energy(way))
        total = [t + alpha * (way[i] if i < len(way) else zero) for i, t in enumerate(total)]
        if iteration + 1 < ITERS:
            longer = way + [zero]
            shifted = [zero] + way
            res = [r - alpha * (a - b) for r, a, b in zip(res + [zero], longer, shifted)]
            gamma_next = jnp.maximum(inner(res), 0.0)
            ratio = safe_div(gamma_next, gamma)
            way = [r + ratio * a for r, a in zip(res, longer)]
            gamma = gamma_next
    return total


VMEM = pl.BlockSpec(memory_space=pltpu.VMEM)
PARAMS = pltpu.CompilerParams(vmem_limit_bytes=16 << 20)


def vmem_call(kernel, out_shape, inputs, scratch=()):
    return pl.pallas_call(
        kernel,
        out_shape=out_shape,
        in_specs=[VMEM] * len(inputs),
        out_specs=jax.tree.map(lambda _: VMEM, out_shape),
        scratch_shapes=list(scratch),
        compiler_params=PARAMS,
    )(*inputs)


def cols(c):
    return slice(c * LANES, (c + 1) * LANES)


def add(sums, key, value):
    sums[key] = sums[key] + value if key in sums else value


def edge_kernel(field_hbm, class_hbm, cond_hbm, row_hbm, col_hbm, *refs):
    far_ref, near_ref, par_ref, spot_ref = refs[:4]
    field_ref, class_ref, cond_ref, row_ref, col_ref, sems = refs[4:]
    sources, rows, _ = field_hbm.shape
    halo = far_ref.shape[1]
    pairs = []
    for i, at in enumerate((0, rows - SUBLANES)):
        pairs.append((field_hbm.at[:, pl.ds(at, SUBLANES)], field_ref.at[i]))
        pairs.append((class_hbm.at[pl.ds(at, SUBLANES)], class_ref.at[i]))
    pairs += [
        (cond_hbm, cond_ref),
        (row_hbm, row_ref),
        (col_hbm, col_ref),
    ]
    copies = [
        pltpu.make_async_copy(start, end, sems.at[i]) for i, (start, end) in enumerate(pairs)
    ]
    for copy in copies:
        copy.start()
    for copy in copies:
        copy.wait()
    even = lax.axis_index("tile") % 2 == 0
    spare = SUBLANES - halo
    for s in range(sources):
        first, last = field_ref[0, s, :halo], field_ref[1, s, spare:]
        far_ref[s] = jnp.where(even, first, last)
        near_ref[s] = jnp.where(even, last, first)
    first = class_ref[0, :halo].astype(jnp.float32) + 1.0
    last = class_ref[1, spare:].astype(jnp.float32) + 1.0
    far_ref[sources] = jnp.where(even, first, last)
    near_ref[sources] = jnp.where(even, last, first)
    tile = (SUBLANES, LANES)
    n_class = cond_ref.shape[0]
    for i in range(n_class):
        par_ref[i] = jnp.full(tile, cond_ref[i], jnp.float32)
    for s in range(sources):
        spot_ref[s] = jnp.full(tile, row_ref[s], jnp.int32)
        spot_ref[sources + s] = jnp.full(tile, col_ref[s], jnp.int32)


def neighbours(get, chunks, lane):
    here = get(0)
    last = LANES - 1
    from_right = pltpu.roll(here, last, 1)
    before = None
    for c in range(chunks):
        from_left = pltpu.roll(here, 1, 1)
        left = jnp.where(lane == 0, before, from_left) if c else from_left
        right = from_right
        if c + 1 < chunks:
            following = get(c + 1)
            from_next = pltpu.roll(following, last, 1)
            right = jnp.where(lane == last, from_next, from_right)
        yield c, here, left, right
        before = from_left
        if c + 1 < chunks:
            here, from_right = following, from_next


def conductivity(ids, values):
    sigma = jnp.zeros(ids.shape, jnp.float32)
    for i, value in enumerate(values):
        sigma = jnp.where(ids == i + 1.0, value, sigma)
    return sigma


def tall(tile, rows):
    return jnp.concatenate([tile] * (rows // SUBLANES), axis=0)


def line_sum(value):
    return jnp.sum(value, axis=0, keepdims=True)


def lines_of(tops, sums, sources):
    lines = list(tops)
    for n in range(2 * ITERS):
        for s in range(sources):
            lines.append(line_sum(sums[n, s]))
    return lines


def inner_kernel(field_ref, class_ref, par_ref, wave_ref, spot_ref, pick_ref, *refs):
    x_ref, *basis_refs = refs[: 1 + ITERS]
    pay_ref, sig_ref, side_ref, above_ref, below_ref, hit_ref, square_ref = refs[1 + ITERS : 8 + ITERS]
    up_ref, down_ref, west_ref, east_ref, diag_ref, inv_ref = refs[8 + ITERS :]
    sources, rows, _ = field_ref.shape
    chunks, total = x_ref.shape[1:3]
    n_class = par_ref.shape[0]
    halo = (total - rows) // 2
    lane = lax.broadcasted_iota(jnp.int32, (total, LANES), 1)
    row = lax.broadcasted_iota(jnp.int32, (total, LANES), 0)
    rows_at = row + (lax.axis_index("tile") * rows - halo)
    blank = jnp.zeros((halo, LANES), jnp.float32)
    inner = slice(SUBLANES, total - SUBLANES)
    wave = jnp.broadcast_to(wave_ref[...], (SUBLANES, LANES))
    square_ref[...] = wave * wave
    square = tall(square_ref[...], total)
    values = [tall(par_ref[i], rows) for i in range(n_class)]

    def widened(value):
        return jnp.concatenate([blank, value, blank], axis=0)

    for c in range(chunks):
        ids = class_ref[:, cols(c)].astype(jnp.float32) + 1.0
        sig_ref[c] = widened(conductivity(ids, values))
        for s in range(sources):
            x_ref[s, c] = widened(field_ref[s, :, cols(c)])
    for c, sigma, left, _ in neighbours(lambda c: sig_ref[c], chunks, lane):
        face = harmonic(left, sigma)
        side_ref[c] = jnp.where(lane == 0, 0.0, face) if c == 0 else face
        up = harmonic(pltpu.roll(sigma, 1, 0), sigma)
        above_ref[c] = up
        below_ref[c] = pltpu.roll(up, total - 1, 0)
    at_source = [rows_at == tall(spot_ref[s], total) for s in range(sources)]
    for c, west, _, east in neighbours(lambda c: side_ref[c], chunks, lane):
        up, down = above_ref[c], below_ref[c]
        sigma = sig_ref[c]
        diag = up + down + west + square * sigma
        if c == chunks - 1:
            bottom = lane == LANES - 1
            diag = diag + jnp.where(bottom, sigma, east)
            east = jnp.where(bottom, 0.0, east)
        else:
            diag = diag + east
        inverse = 1.0 / jnp.maximum(diag, TINY)
        diag_ref[c] = diag
        inv_ref[c] = inverse
        up_ref[c] = up * inverse
        down_ref[c] = down * inverse
        west_ref[c] = west * inverse
        east_ref[c] = east * inverse

    def spread(c, here, left, right):
        return (
            up_ref[c] * pltpu.roll(here, 1, 0)
            + down_ref[c] * pltpu.roll(here, total - 1, 0)
            + west_ref[c] * left
            + east_ref[c] * right
        )

    def fold(value):
        return sum(value[r : r + SUBLANES] for r in range(0, value.shape[0], SUBLANES))

    sums = {}
    for s in range(sources):
        column = tall(spot_ref[sources + s], total)
        for c, here, left, right in neighbours(lambda c: x_ref[s, c], chunks, lane):
            charge = jnp.where(
                at_source[s] & (lane + c * LANES == column), SOURCE_STRENGTH, 0.0
            )
            hit_ref[0, s, c] = charge[:SUBLANES]
            hit_ref[1, s, c] = charge[total - SUBLANES :]
            new = charge * inv_ref[c] - (here - spread(c, here, left, right))
            basis_refs[0][s, c] = new
            own = new[inner]
            add(sums, (0, s), fold(diag_ref[c, inner] * own * own))
    for i in range(ITERS):
        for s in range(sources):
            for c, here, left, right in neighbours(lambda c: basis_refs[i][s, c], chunks, lane):
                new = spread(c, here, left, right)
                own = new[inner]
                weighted = diag_ref[c, inner] * own
                add(sums, (2 * i + 1, s), fold(weighted * here[inner]))
                if i + 1 < ITERS:
                    basis_refs[i + 1][s, c] = new
                    add(sums, (2 * i + 2, s), fold(weighted * own))
    picker = rows_at[inner] == pick_ref[...]
    tops = []
    for ref in (x_ref, *basis_refs):
        for s in range(sources):
            top = jnp.broadcast_to(ref[s, 0, inner, 0:1], (total - 2 * SUBLANES, LANES))
            tops.append(line_sum(fold(jnp.where(picker, top, 0.0))))
    pay_ref[...] = jnp.zeros(pay_ref.shape, jnp.float32)
    for i, line in enumerate(lines_of(tops, sums, sources)):
        pay_ref[i : i + 1, :] = line


def outer_kernel(far_ref, near_ref, par_ref, pick_ref, *refs):
    x_in, *basis_in = refs[: 1 + ITERS]
    pay_in, sig_in, side_in, above_in, below_in, hit_in, square_in = refs[1 + ITERS : 8 + ITERS]
    outs = refs[8 + ITERS :]
    x_ref, *basis_refs = outs[: 1 + ITERS]
    pay_ref = outs[1 + ITERS]
    sigma_ref, west_raw, up_ref, down_ref, west_ref, east_ref, diag_ref, inv_ref = outs[2 + ITERS :]
    sources, chunks, total, _ = x_in.shape
    n_class = par_ref.shape[0]
    halo = far_ref.shape[1]
    rows = total - 2 * halo
    lane = lax.broadcasted_iota(jnp.int32, (SUBLANES, LANES), 1)
    row = lax.broadcasted_iota(jnp.int32, (SUBLANES, LANES), 0)
    tile = lax.axis_index("tile")
    even = tile % 2 == 0
    square = square_in[...]
    values = [par_ref[i] for i in range(n_class)]
    upper = row < halo
    last = total - SUBLANES
    own = (jnp.logical_not(upper), upper)

    def came_in(index, c):
        far, near = far_ref[index, :, cols(c)], near_ref[index, :, cols(c)]
        return jnp.concatenate(
            [jnp.where(even, far, near), jnp.where(even, near, far)], axis=0
        )

    def set_in(new, kept):
        return jnp.where(upper, new, kept[:SUBLANES]), jnp.where(upper, kept[last:], new)

    for c in range(chunks):
        sigma_ref[c] = conductivity(came_in(sources, c), values)
        for s in range(sources):
            x_ref[0, s, c], x_ref[1, s, c] = set_in(came_in(s, c), x_in.at[s, c])
    for c, fresh, left, _ in neighbours(lambda c: sigma_ref[c], chunks, lane):
        face = harmonic(left, fresh)
        face = jnp.where(lane == 0, 0.0, face) if c == 0 else face
        west_raw[0, c], west_raw[1, c] = set_in(face, side_in.at[c])
    for e in (0, 1):
        for c, west, _, east in neighbours(lambda c: west_raw[e, c], chunks, lane):
            fresh = sigma_ref[c]
            first, end = set_in(fresh, sig_in.at[c])
            sigma = end if e else first
            face = harmonic(
                jnp.where(upper, pltpu.roll(first, SUBLANES - 1, 0), pltpu.roll(end, 1, 0)), fresh
            )
            if e:
                up = jnp.where(upper, above_in[c, last:], face)
                down = pltpu.roll(up, SUBLANES - 1, 0)
            else:
                down = jnp.where(upper, face, below_in[c, :SUBLANES])
                up = pltpu.roll(down, 1, 0)
            diag = up + down + west + square * sigma
            if c == chunks - 1:
                bottom = lane == LANES - 1
                diag = diag + jnp.where(bottom, sigma, east)
                east = jnp.where(bottom, 0.0, east)
            else:
                diag = diag + east
            inverse = 1.0 / jnp.maximum(diag, TINY)
            diag_ref[e, c] = jnp.where(own[e], diag, 0.0)
            inv_ref[e, c] = inverse
            up_ref[e, c] = up * inverse
            down_ref[e, c] = down * inverse
            west_ref[e, c] = west * inverse
            east_ref[e, c] = east * inverse

    def spread(whole, e, s, c, here, left, right):
        above = pltpu.roll(here, 1, 0)
        below = pltpu.roll(here, SUBLANES - 1, 0)
        if e:
            above = jnp.where(row == 0, whole[s, c, last - 1 : last], above)
        else:
            below = jnp.where(row == SUBLANES - 1, whole[s, c, SUBLANES : SUBLANES + 1], below)
        return (
            up_ref[e, c] * above
            + down_ref[e, c] * below
            + west_ref[e, c] * left
            + east_ref[e, c] * right
        )

    sums = {}
    both = [(e, s) for e in (0, 1) for s in range(sources)]
    for e, s in both:
        for c, here, left, right in neighbours(lambda c: x_ref[e, s, c], chunks, lane):
            new = hit_in[e, s, c] * inv_ref[e, c] - (
                here - spread(x_in, e, s, c, here, left, right)
            )
            basis_refs[0][e, s, c] = new
            add(sums, (0, s), diag_ref[e, c] * new * new)
    for i in range(ITERS):
        for e, s in both:
            for c, here, left, right in neighbours(
                lambda c: basis_refs[i][e, s, c], chunks, lane
            ):
                new = spread(basis_in[i], e, s, c, here, left, right)
                weighted = diag_ref[e, c] * new
                add(sums, (2 * i + 1, s), weighted * here)
                if i + 1 < ITERS:
                    basis_refs[i + 1][e, s, c] = new
                    add(sums, (2 * i + 2, s), weighted * new)
    pickers = [
        own[e] & (row + (tile * rows - halo + at) == pick_ref[...]) for e, at in ((0, 0), (1, last))
    ]
    tops = []
    for ref in (x_ref, *basis_refs):
        for s in range(sources):
            line = 0.0
            for e in (0, 1):
                top = jnp.broadcast_to(ref[e, s, 0, :, 0:1], (SUBLANES, LANES))
                line = line + jnp.where(pickers[e], top, 0.0)
            tops.append(line_sum(line))
    pay_ref[...] = pay_in[...]
    for i, line in enumerate(lines_of(tops, sums, sources)):
        pay_ref[i : i + 1, :] += line


def combine_kernel(n_pay, weight_ref, *refs):
    n_parts = ITERS + 1
    packed = tree_sum([r[...] for r in refs[:n_pay]])
    part_refs = refs[n_pay : n_pay + n_parts]
    edge_refs = refs[n_pay + n_parts : n_pay + 2 * n_parts]
    out_refs = refs[n_pay + 2 * n_parts :]
    sources, _, total, _ = part_refs[0].shape
    share = out_refs[0].shape[1]
    rows = (out_refs[0].shape[0] - SUBLANES) // sources
    halo = (total - rows) // 2
    first = n_parts * sources
    totals = jnp.sum(packed[first : first + 2 * ITERS * sources], axis=1, keepdims=True)
    poly = step_polynomial([totals[n * sources : (n + 1) * sources] for n in range(2 * ITERS)])
    weight = weight_ref[...]
    scale = [[weight] + [weight * p[s : s + 1] for p in poly] for s in range(sources)]
    read = [
        sum(scale[s][i] * packed[i * sources + s : i * sources + s + 1] for i in range(n_parts))
        for s in range(sources)
    ]
    split = len(out_refs) > 1
    wave = lax.axis_index("wave") if split else 0
    per = share // LANES
    inner = slice(SUBLANES, total - SUBLANES)
    for mask, out_ref in enumerate(out_refs):
        block = wave ^ mask if split else 0
        for s in range(sources):
            for k in range(per):
                c = block * per + k
                middle = sum(scale[s][i] * part_refs[i][s, c, inner] for i in range(n_parts))
                top, end = (
                    sum(scale[s][i] * edge_refs[i][e, s, c] for i in range(n_parts)) for e in (0, 1)
                )
                value = jnp.concatenate([top[halo:], middle, end[: SUBLANES - halo]], axis=0)
                out_ref[s * rows : (s + 1) * rows, cols(k)] = value
        out_ref[sources * rows :, :] = jnp.zeros((SUBLANES, share), jnp.float32)
        for s in range(sources):
            out_ref[sources * rows + s : sources * rows + s + 1, :LANES] = read[s]


def sum_kernel(*refs):
    part_refs, (field_ref, read_ref) = refs[:-2], refs[-2:]
    sources, rows, _ = field_ref.shape
    electrodes = read_ref.shape[1]
    for s in range(sources):
        field_ref[s] = tree_sum([r[s * rows : (s + 1) * rows, :] for r in part_refs])
    last = tree_sum([r[sources * rows :, :LANES] for r in part_refs])
    read_ref[...] = last[:sources, :electrodes]


def shards(
    warm_start,
    class_map,
    conductivities,
    wavenumbers,
    weights,
    source_row,
    source_col,
    electrode_row,
):
    rows, depth = class_map.shape
    sources = warm_start.shape[1]
    electrodes = electrode_row.shape[0]
    tiles, waves = lax.axis_size("tile"), lax.axis_size("wave")
    wave = lax.axis_index("wave")
    halo = ITERS + 1
    field = warm_start[0]
    f32 = jnp.float32
    n_class = conductivities.shape[0]
    rim = jax.ShapeDtypeStruct((sources + 1, halo, depth), f32)
    raw = [
        field,
        class_map,
        conductivities,
        source_row,
        source_col,
    ]
    far, near, params, spots = pl.pallas_call(
        edge_kernel,
        out_shape=[
            rim,
            rim,
            jax.ShapeDtypeStruct((n_class, SUBLANES, LANES), f32),
            jax.ShapeDtypeStruct((2 * sources, SUBLANES, LANES), jnp.int32),
        ],
        in_specs=[pl.BlockSpec(memory_space=pltpu.HBM)] * len(raw),
        out_specs=[VMEM] * 4,
        scratch_shapes=[
            pltpu.VMEM((2, sources, SUBLANES, depth), f32),
            pltpu.VMEM((2, SUBLANES, depth), jnp.int32),
            *[pltpu.SMEM(a.shape, a.dtype) for a in raw[2:]],
            pltpu.SemaphoreType.DMA((len(raw) + 2,)),
        ],
        compiler_params=PARAMS,
    )(*[pltpu.with_memory_space_constraint(a, pltpu.HBM) for a in raw])
    far_pairs = [(i, i + 1) for i in range(1, tiles - 1, 2)]
    far = lax.ppermute(far, "tile", far_pairs + [(j, i) for i, j in far_pairs])
    near = swap(near, "tile", 1, tiles)
    total, chunks = rows + 2 * halo, depth // LANES
    picks = jnp.pad(electrode_row, (0, LANES - electrodes), constant_values=-1)[None]
    wide = jax.ShapeDtypeStruct((sources, chunks, total, LANES), f32)
    flat = jax.ShapeDtypeStruct((chunks, total, LANES), f32)
    n_lines = sources * (3 * ITERS + 1)
    pay = jax.ShapeDtypeStruct((-(-n_lines // SUBLANES) * SUBLANES, LANES), f32)
    ends = jax.ShapeDtypeStruct((2, sources, chunks, SUBLANES, LANES), f32)
    tile = jax.ShapeDtypeStruct((SUBLANES, LANES), f32)
    inside = vmem_call(
        inner_kernel,
        [wide] * (ITERS + 1) + [pay, flat, flat, flat, flat, ends, tile],
        [field, class_map, params, wavenumbers[None], spots, picks],
        [pltpu.VMEM((chunks, total, LANES), f32)] * 6,
    )
    pair = pltpu.VMEM((2, chunks, SUBLANES, LANES), f32)
    outside = vmem_call(
        outer_kernel,
        [ends] * (ITERS + 1) + [pay],
        [far, near, params, picks, *inside],
        [pltpu.VMEM((chunks, SUBLANES, LANES), f32)] + [pair] * 7,
    )
    packed = tile_parts(outside[-1], "tile")
    share = depth // waves
    split = share % LANES == 0
    width = share if split else depth
    block = jax.ShapeDtypeStruct((sources * rows + SUBLANES, width), f32)
    pieces = vmem_call(
        functools.partial(combine_kernel, len(packed)),
        [block] * (waves if split else 1),
        [weights[None], *packed, *inside[: ITERS + 1], *outside[: ITERS + 1]],
    )
    if not split:
        n = sources * rows
        read = pieces[0][n : n + sources, :electrodes].reshape(-1, share)
        pieces = [
            jnp.concatenate(
                [lax.dynamic_slice_in_dim(pieces[0][:n], (wave ^ mask) * share, share, 1), read]
            )
            for mask in range(waves)
        ]
    pieces = [pieces[0]] + [swap(pieces[m], "wave", m, waves) for m in range(1, waves)]
    if not split:
        final = tree_sum(pieces)
        return (
            final[: sources * rows].reshape(sources, rows, share),
            final[sources * rows :].reshape(sources, electrodes),
        )
    return tuple(
        vmem_call(
            sum_kernel,
            [
                jax.ShapeDtypeStruct((sources, rows, share), f32),
                jax.ShapeDtypeStruct((sources, electrodes), f32),
            ],
            pieces,
        )
    )


def solution(mesh):
    return jax.shard_map(
        shards,
        mesh=mesh,
        in_specs=(
            P("wave", None, "tile", None),
            P("tile", None),
            P(),
            P("wave"),
            P("wave"),
            P(),
            P(),
            P(),
        ),
        out_specs=(P(None, "tile", "wave"), P()),
        check_vma=False,
    )
```

```python
import functools

import jax
import jax.numpy as jnp
from jax import lax
from jax.experimental import pallas as pl
from jax.experimental.pallas import tpu as pltpu
from jax.sharding import PartitionSpec as P

ITERS = 3
SOURCE_STRENGTH = 50.0
TINY = 1e-30
LANES = 128
SUBLANES = 8


def harmonic(left_val, right_val):
    return 2.0 * left_val * right_val / jnp.maximum(left_val + right_val, TINY)


def safe_div(num, den):
    return jnp.where(den > 0.0, num / jnp.where(den > 0.0, den, 1.0), 0.0)


def tree_sum(values):
    values = list(values)
    while len(values) > 1:
        values = [values[i] + values[i + 1] for i in range(0, len(values), 2)]
    return values[0]


def swap(value, axis, mask, size):
    return lax.ppermute(value, axis, [(i, i ^ mask) for i in range(size)])


def tile_parts(value, axis):
    size = lax.axis_size(axis)
    parts = [value]
    bit = 1
    while bit < size:
        value = tree_sum(parts)
        masks = [bit]
        if bit > 1 and bit * 2 < size:
            masks.append(bit * 2)
        offsets = [0]
        for mask in masks:
            offsets += [o ^ mask for o in offsets]
        parts = [value] + [swap(value, axis, o, size) for o in offsets[1:]]
        bit = masks[-1] * 2
    return parts


def issued(values, order):
    return [values[i] for i in order], [order.index(i) for i in range(len(values))]


def step_polynomial(moments):
    def inner(poly):
        return sum(a * b * moments[i + j] for i, a in enumerate(poly) for j, b in enumerate(poly))

    def energy(poly):
        return sum(
            a * b * (moments[i + j] - moments[i + j + 1])
            for i, a in enumerate(poly)
            for j, b in enumerate(poly)
        )

    one = jnp.ones_like(moments[0])
    zero = jnp.zeros_like(moments[0])
    res, way, total = [one], [one], [zero] * ITERS
    gamma = moments[0]
    for iteration in range(ITERS):
        alpha = safe_div(gamma, energy(way))
        total = [t + alpha * (way[i] if i < len(way) else zero) for i, t in enumerate(total)]
        if iteration + 1 < ITERS:
            longer = way + [zero]
            shifted = [zero] + way
            res = [r - alpha * (a - b) for r, a, b in zip(res + [zero], longer, shifted)]
            gamma_next = jnp.maximum(inner(res), 0.0)
            ratio = safe_div(gamma_next, gamma)
            way = [r + ratio * a for r, a in zip(res, longer)]
            gamma = gamma_next
    return total


VMEM = pl.BlockSpec(memory_space=pltpu.VMEM)
PARAMS = pltpu.CompilerParams(vmem_limit_bytes=16 << 20)


def vmem_call(kernel, out_shape, inputs, scratch=()):
    return pl.pallas_call(
        kernel,
        out_shape=out_shape,
        in_specs=[VMEM] * len(inputs),
        out_specs=jax.tree.map(lambda _: VMEM, out_shape),
        scratch_shapes=list(scratch),
        compiler_params=PARAMS,
    )(*inputs)


def cols(c):
    return slice(c * LANES, (c + 1) * LANES)


def add(sums, key, value):
    sums[key] = sums[key] + value if key in sums else value


def edge_kernel(field_hbm, class_hbm, cond_hbm, row_hbm, col_hbm, *refs):
    far_ref, near_ref, par_ref, spot_ref = refs[:4]
    field_ref, class_ref, cond_ref, row_ref, col_ref, sems = refs[4:]
    sources, rows, _ = field_hbm.shape
    halo = far_ref.shape[1]
    pairs = []
    for i, at in enumerate((0, rows - SUBLANES)):
        pairs.append((field_hbm.at[:, pl.ds(at, SUBLANES)], field_ref.at[i]))
        pairs.append((class_hbm.at[pl.ds(at, SUBLANES)], class_ref.at[i]))
    pairs += [
        (cond_hbm, cond_ref),
        (row_hbm, row_ref),
        (col_hbm, col_ref),
    ]
    copies = [
        pltpu.make_async_copy(start, end, sems.at[i]) for i, (start, end) in enumerate(pairs)
    ]
    for copy in copies:
        copy.start()
    for copy in copies:
        copy.wait()
    even = lax.axis_index("tile") % 2 == 0
    spare = SUBLANES - halo
    for s in range(sources):
        first, last = field_ref[0, s, :halo], field_ref[1, s, spare:]
        far_ref[s] = jnp.where(even, first, last)
        near_ref[s] = jnp.where(even, last, first)
    first = class_ref[0, :halo].astype(jnp.float32) + 1.0
    last = class_ref[1, spare:].astype(jnp.float32) + 1.0
    far_ref[sources] = jnp.where(even, first, last)
    near_ref[sources] = jnp.where(even, last, first)
    tile = (SUBLANES, LANES)
    n_class = cond_ref.shape[0]
    for i in range(n_class):
        par_ref[i] = jnp.full(tile, cond_ref[i], jnp.float32)
    for s in range(sources):
        spot_ref[s] = jnp.full(tile, row_ref[s], jnp.int32)
        spot_ref[sources + s] = jnp.full(tile, col_ref[s], jnp.int32)


def neighbours(get, chunks, lane):
    here = get(0)
    last = LANES - 1
    from_right = pltpu.roll(here, last, 1)
    before = None
    for c in range(chunks):
        from_left = pltpu.roll(here, 1, 1)
        left = jnp.where(lane == 0, before, from_left) if c else from_left
        right = from_right
        if c + 1 < chunks:
            following = get(c + 1)
            from_next = pltpu.roll(following, last, 1)
            right = jnp.where(lane == last, from_next, from_right)
        yield c, here, left, right
        before = from_left
        if c + 1 < chunks:
            here, from_right = following, from_next


def conductivity(ids, values):
    sigma = jnp.zeros(ids.shape, jnp.float32)
    for i, value in enumerate(values):
        sigma = jnp.where(ids == i + 1.0, value, sigma)
    return sigma


def tall(tile, rows):
    return jnp.concatenate([tile] * (rows // SUBLANES), axis=0)


def line_sum(value):
    return jnp.sum(value, axis=0, keepdims=True)


def lines_of(tops, sums, sources):
    lines = list(tops)
    for n in range(2 * ITERS):
        for s in range(sources):
            lines.append(line_sum(sums[n, s]))
    return lines


def inner_kernel(field_ref, class_ref, par_ref, wave_ref, spot_ref, pick_ref, *refs):
    x_ref, *basis_refs = refs[: 1 + ITERS]
    pay_ref, sig_ref, side_ref, above_ref, below_ref, hit_ref, square_ref = refs[1 + ITERS : 8 + ITERS]
    up_ref, down_ref, west_ref, east_ref, diag_ref, inv_ref = refs[8 + ITERS :]
    sources, rows, _ = field_ref.shape
    chunks, total = x_ref.shape[1:3]
    n_class = par_ref.shape[0]
    halo = (total - rows) // 2
    lane = lax.broadcasted_iota(jnp.int32, (total, LANES), 1)
    row = lax.broadcasted_iota(jnp.int32, (total, LANES), 0)
    rows_at = row + (lax.axis_index("tile") * rows - halo)
    blank = jnp.zeros((halo, LANES), jnp.float32)
    inner = slice(SUBLANES, total - SUBLANES)
    wave = jnp.broadcast_to(wave_ref[...], (SUBLANES, LANES))
    square_ref[...] = wave * wave
    square = tall(square_ref[...], total)
    values = [tall(par_ref[i], rows) for i in range(n_class)]

    def widened(value):
        return jnp.concatenate([blank, value, blank], axis=0)

    for c in range(chunks):
        ids = class_ref[:, cols(c)].astype(jnp.float32) + 1.0
        sig_ref[c] = widened(conductivity(ids, values))
        for s in range(sources):
            x_ref[s, c] = widened(field_ref[s, :, cols(c)])
    for c, sigma, left, _ in neighbours(lambda c: sig_ref[c], chunks, lane):
        face = harmonic(left, sigma)
        side_ref[c] = jnp.where(lane == 0, 0.0, face) if c == 0 else face
        up = harmonic(pltpu.roll(sigma, 1, 0), sigma)
        above_ref[c] = up
        below_ref[c] = pltpu.roll(up, total - 1, 0)
    at_source = [rows_at == tall(spot_ref[s], total) for s in range(sources)]
    for c, west, _, east in neighbours(lambda c: side_ref[c], chunks, lane):
        up, down = above_ref[c], below_ref[c]
        sigma = sig_ref[c]
        diag = up + down + west + square * sigma
        if c == chunks - 1:
            bottom = lane == LANES - 1
            diag = diag + jnp.where(bottom, sigma, east)
            east = jnp.where(bottom, 0.0, east)
        else:
            diag = diag + east
        inverse = 1.0 / jnp.maximum(diag, TINY)
        diag_ref[c] = diag
        inv_ref[c] = inverse
        up_ref[c] = up * inverse
        down_ref[c] = down * inverse
        west_ref[c] = west * inverse
        east_ref[c] = east * inverse

    def spread(c, here, left, right):
        return (
            up_ref[c] * pltpu.roll(here, 1, 0)
            + down_ref[c] * pltpu.roll(here, total - 1, 0)
            + west_ref[c] * left
            + east_ref[c] * right
        )

    def fold(value):
        return sum(value[r : r + SUBLANES] for r in range(0, value.shape[0], SUBLANES))

    sums = {}
    for s in range(sources):
        column = tall(spot_ref[sources + s], total)
        for c, here, left, right in neighbours(lambda c: x_ref[s, c], chunks, lane):
            charge = jnp.where(
                at_source[s] & (lane + c * LANES == column), SOURCE_STRENGTH, 0.0
            )
            hit_ref[0, s, c] = charge[:SUBLANES]
            hit_ref[1, s, c] = charge[total - SUBLANES :]
            new = charge * inv_ref[c] - (here - spread(c, here, left, right))
            basis_refs[0][s, c] = new
            own = new[inner]
            add(sums, (0, s), fold(diag_ref[c, inner] * own * own))
    for i in range(ITERS):
        for s in range(sources):
            for c, here, left, right in neighbours(lambda c: basis_refs[i][s, c], chunks, lane):
                new = spread(c, here, left, right)
                own = new[inner]
                weighted = diag_ref[c, inner] * own
                add(sums, (2 * i + 1, s), fold(weighted * here[inner]))
                if i + 1 < ITERS:
                    basis_refs[i + 1][s, c] = new
                    add(sums, (2 * i + 2, s), fold(weighted * own))
    picker = rows_at[inner] == pick_ref[...]
    tops = []
    for ref in (x_ref, *basis_refs):
        for s in range(sources):
            top = jnp.broadcast_to(ref[s, 0, inner, 0:1], (total - 2 * SUBLANES, LANES))
            tops.append(line_sum(fold(jnp.where(picker, top, 0.0))))
    pay_ref[...] = jnp.zeros(pay_ref.shape, jnp.float32)
    for i, line in enumerate(lines_of(tops, sums, sources)):
        pay_ref[i : i + 1, :] = line


def outer_kernel(far_ref, near_ref, par_ref, pick_ref, *refs):
    x_in, *basis_in = refs[: 1 + ITERS]
    pay_in, sig_in, side_in, above_in, below_in, hit_in, square_in = refs[1 + ITERS : 8 + ITERS]
    outs = refs[8 + ITERS :]
    x_ref, *basis_refs = outs[: 1 + ITERS]
    pay_ref = outs[1 + ITERS]
    sigma_ref, west_raw, up_ref, down_ref, west_ref, east_ref, diag_ref, inv_ref = outs[2 + ITERS :]
    sources, chunks, total, _ = x_in.shape
    n_class = par_ref.shape[0]
    halo = far_ref.shape[1]
    rows = total - 2 * halo
    lane = lax.broadcasted_iota(jnp.int32, (SUBLANES, LANES), 1)
    row = lax.broadcasted_iota(jnp.int32, (SUBLANES, LANES), 0)
    tile = lax.axis_index("tile")
    even = tile % 2 == 0
    square = square_in[...]
    values = [par_ref[i] for i in range(n_class)]
    upper = row < halo
    last = total - SUBLANES
    own = (jnp.logical_not(upper), upper)

    def came_in(index, c):
        far, near = far_ref[index, :, cols(c)], near_ref[index, :, cols(c)]
        return jnp.concatenate(
            [jnp.where(even, far, near), jnp.where(even, near, far)], axis=0
        )

    def set_in(new, kept):
        return jnp.where(upper, new, kept[:SUBLANES]), jnp.where(upper, kept[last:], new)

    for c in range(chunks):
        sigma_ref[c] = conductivity(came_in(sources, c), values)
        for s in range(sources):
            x_ref[0, s, c], x_ref[1, s, c] = set_in(came_in(s, c), x_in.at[s, c])
    for c, fresh, left, _ in neighbours(lambda c: sigma_ref[c], chunks, lane):
        face = harmonic(left, fresh)
        face = jnp.where(lane == 0, 0.0, face) if c == 0 else face
        west_raw[0, c], west_raw[1, c] = set_in(face, side_in.at[c])
    for e in (0, 1):
        for c, west, _, east in neighbours(lambda c: west_raw[e, c], chunks, lane):
            fresh = sigma_ref[c]
            first, end = set_in(fresh, sig_in.at[c])
            sigma = end if e else first
            face = harmonic(
                jnp.where(upper, pltpu.roll(first, SUBLANES - 1, 0), pltpu.roll(end, 1, 0)), fresh
            )
            if e:
                up = jnp.where(upper, above_in[c, last:], face)
                down = pltpu.roll(up, SUBLANES - 1, 0)
            else:
                down = jnp.where(upper, face, below_in[c, :SUBLANES])
                up = pltpu.roll(down, 1, 0)
            diag = up + down + west + square * sigma
            if c == chunks - 1:
                bottom = lane == LANES - 1
                diag = diag + jnp.where(bottom, sigma, east)
                east = jnp.where(bottom, 0.0, east)
            else:
                diag = diag + east
            inverse = 1.0 / jnp.maximum(diag, TINY)
            diag_ref[e, c] = jnp.where(own[e], diag, 0.0)
            inv_ref[e, c] = inverse
            up_ref[e, c] = up * inverse
            down_ref[e, c] = down * inverse
            west_ref[e, c] = west * inverse
            east_ref[e, c] = east * inverse

    def spread(whole, e, s, c, here, left, right):
        above = pltpu.roll(here, 1, 0)
        below = pltpu.roll(here, SUBLANES - 1, 0)
        if e:
            above = jnp.where(row == 0, whole[s, c, last - 1 : last], above)
        else:
            below = jnp.where(row == SUBLANES - 1, whole[s, c, SUBLANES : SUBLANES + 1], below)
        return (
            up_ref[e, c] * above
            + down_ref[e, c] * below
            + west_ref[e, c] * left
            + east_ref[e, c] * right
        )

    sums = {}
    both = [(e, s) for e in (0, 1) for s in range(sources)]
    for e, s in both:
        for c, here, left, right in neighbours(lambda c: x_ref[e, s, c], chunks, lane):
            new = hit_in[e, s, c] * inv_ref[e, c] - (
                here - spread(x_in, e, s, c, here, left, right)
            )
            basis_refs[0][e, s, c] = new
            add(sums, (0, s), diag_ref[e, c] * new * new)
    for i in range(ITERS):
        for e, s in both:
            for c, here, left, right in neighbours(
                lambda c: basis_refs[i][e, s, c], chunks, lane
            ):
                new = spread(basis_in[i], e, s, c, here, left, right)
                weighted = diag_ref[e, c] * new
                add(sums, (2 * i + 1, s), weighted * here)
                if i + 1 < ITERS:
                    basis_refs[i + 1][e, s, c] = new
                    add(sums, (2 * i + 2, s), weighted * new)
    pickers = [
        own[e] & (row + (tile * rows - halo + at) == pick_ref[...]) for e, at in ((0, 0), (1, last))
    ]
    tops = []
    for ref in (x_ref, *basis_refs):
        for s in range(sources):
            line = 0.0
            for e in (0, 1):
                top = jnp.broadcast_to(ref[e, s, 0, :, 0:1], (SUBLANES, LANES))
                line = line + jnp.where(pickers[e], top, 0.0)
            tops.append(line_sum(line))
    pay_ref[...] = pay_in[...]
    for i, line in enumerate(lines_of(tops, sums, sources)):
        pay_ref[i : i + 1, :] += line


def combine_kernel(places, weight_ref, *refs):
    n_parts, n_pay = ITERS + 1, len(places)
    packed = tree_sum([refs[i][...] for i in places])
    part_refs = refs[n_pay : n_pay + n_parts]
    edge_refs = refs[n_pay + n_parts : n_pay + 2 * n_parts]
    out_refs = refs[n_pay + 2 * n_parts :]
    sources, _, total, _ = part_refs[0].shape
    share = out_refs[0].shape[1]
    rows = (out_refs[0].shape[0] - SUBLANES) // sources
    halo = (total - rows) // 2
    first = n_parts * sources
    totals = jnp.sum(packed[first : first + 2 * ITERS * sources], axis=1, keepdims=True)
    poly = step_polynomial([totals[n * sources : (n + 1) * sources] for n in range(2 * ITERS)])
    weight = weight_ref[...]
    scale = [[weight] + [weight * p[s : s + 1] for p in poly] for s in range(sources)]
    read = [
        sum(scale[s][i] * packed[i * sources + s : i * sources + s + 1] for i in range(n_parts))
        for s in range(sources)
    ]
    split = len(out_refs) > 1
    wave = lax.axis_index("wave") if split else 0
    per = share // LANES
    inner = slice(SUBLANES, total - SUBLANES)
    for mask, out_ref in enumerate(out_refs):
        block = wave ^ mask if split else 0
        for s in range(sources):
            for k in range(per):
                c = block * per + k
                middle = sum(scale[s][i] * part_refs[i][s, c, inner] for i in range(n_parts))
                top, end = (
                    sum(scale[s][i] * edge_refs[i][e, s, c] for i in range(n_parts)) for e in (0, 1)
                )
                value = jnp.concatenate([top[halo:], middle, end[: SUBLANES - halo]], axis=0)
                out_ref[s * rows : (s + 1) * rows, cols(k)] = value
        out_ref[sources * rows :, :] = jnp.zeros((SUBLANES, share), jnp.float32)
        for s in range(sources):
            out_ref[sources * rows + s : sources * rows + s + 1, :LANES] = read[s]


def sum_kernel(places, *refs):
    part_refs, (field_ref, read_ref) = [refs[i] for i in places], refs[-2:]
    sources, rows, _ = field_ref.shape
    electrodes = read_ref.shape[1]
    for s in range(sources):
        field_ref[s] = tree_sum([r[s * rows : (s + 1) * rows, :] for r in part_refs])
    last = tree_sum([r[sources * rows :, :LANES] for r in part_refs])
    read_ref[...] = last[:sources, :electrodes]


def shards(
    warm_start,
    class_map,
    conductivities,
    wavenumbers,
    weights,
    source_row,
    source_col,
    electrode_row,
):
    rows, depth = class_map.shape
    sources = warm_start.shape[1]
    electrodes = electrode_row.shape[0]
    tiles, waves = lax.axis_size("tile"), lax.axis_size("wave")
    wave = lax.axis_index("wave")
    halo = ITERS + 1
    field = warm_start[0]
    f32 = jnp.float32
    n_class = conductivities.shape[0]
    rim = jax.ShapeDtypeStruct((sources + 1, halo, depth), f32)
    raw = [
        field,
        class_map,
        conductivities,
        source_row,
        source_col,
    ]
    far, near, params, spots = pl.pallas_call(
        edge_kernel,
        out_shape=[
            rim,
            rim,
            jax.ShapeDtypeStruct((n_class, SUBLANES, LANES), f32),
            jax.ShapeDtypeStruct((2 * sources, SUBLANES, LANES), jnp.int32),
        ],
        in_specs=[pl.BlockSpec(memory_space=pltpu.HBM)] * len(raw),
        out_specs=[VMEM] * 4,
        scratch_shapes=[
            pltpu.VMEM((2, sources, SUBLANES, depth), f32),
            pltpu.VMEM((2, SUBLANES, depth), jnp.int32),
            *[pltpu.SMEM(a.shape, a.dtype) for a in raw[2:]],
            pltpu.SemaphoreType.DMA((len(raw) + 2,)),
        ],
        compiler_params=PARAMS,
    )(*[pltpu.with_memory_space_constraint(a, pltpu.HBM) for a in raw])
    far_pairs = [(i, i + 1) for i in range(1, tiles - 1, 2)]
    far = lax.ppermute(far, "tile", far_pairs + [(j, i) for i, j in far_pairs])
    near = swap(near, "tile", 1, tiles)
    total, chunks = rows + 2 * halo, depth // LANES
    picks = jnp.pad(electrode_row, (0, LANES - electrodes), constant_values=-1)[None]
    wide = jax.ShapeDtypeStruct((sources, chunks, total, LANES), f32)
    flat = jax.ShapeDtypeStruct((chunks, total, LANES), f32)
    n_lines = sources * (3 * ITERS + 1)
    pay = jax.ShapeDtypeStruct((-(-n_lines // SUBLANES) * SUBLANES, LANES), f32)
    ends = jax.ShapeDtypeStruct((2, sources, chunks, SUBLANES, LANES), f32)
    tile = jax.ShapeDtypeStruct((SUBLANES, LANES), f32)
    inside = vmem_call(
        inner_kernel,
        [wide] * (ITERS + 1) + [pay, flat, flat, flat, flat, ends, tile],
        [field, class_map, params, wavenumbers[None], spots, picks],
        [pltpu.VMEM((chunks, total, LANES), f32)] * 6,
    )
    pair = pltpu.VMEM((2, chunks, SUBLANES, LANES), f32)
    outside = vmem_call(
        outer_kernel,
        [ends] * (ITERS + 1) + [pay],
        [far, near, params, picks, *inside],
        [pltpu.VMEM((chunks, SUBLANES, LANES), f32)] + [pair] * 7,
    )
    packed = tile_parts(outside[-1], "tile")
    packed, places = issued(packed, (0, *range(len(packed) - 1, 0, -1)))
    share = depth // waves
    split = share % LANES == 0
    width = share if split else depth
    block = jax.ShapeDtypeStruct((sources * rows + SUBLANES, width), f32)
    pieces = vmem_call(
        functools.partial(combine_kernel, places),
        [block] * (waves if split else 1),
        [weights[None], *packed, *inside[: ITERS + 1], *outside[: ITERS + 1]],
    )
    if not split:
        n = sources * rows
        read = pieces[0][n : n + sources, :electrodes].reshape(-1, share)
        pieces = [
            jnp.concatenate(
                [lax.dynamic_slice_in_dim(pieces[0][:n], (wave ^ mask) * share, share, 1), read]
            )
            for mask in range(waves)
        ]
    pieces = [pieces[0]] + [swap(pieces[m], "wave", m, waves) for m in range(1, waves)]
    if not split:
        final = tree_sum(pieces)
        return (
            final[: sources * rows].reshape(sources, rows, share),
            final[sources * rows :].reshape(sources, electrodes),
        )
    pieces, places = issued(pieces, (0, waves - 1, *range(1, waves - 1)))
    return tuple(
        vmem_call(
            functools.partial(sum_kernel, places),
            [
                jax.ShapeDtypeStruct((sources, rows, share), f32),
                jax.ShapeDtypeStruct((sources, electrodes), f32),
            ],
            pieces,
        )
    )


def solution(mesh):
    return jax.shard_map(
        shards,
        mesh=mesh,
        in_specs=(
            P("wave", None, "tile", None),
            P("tile", None),
            P(),
            P("wave"),
            P("wave"),
            P(),
            P(),
            P(),
        ),
        out_specs=(P(None, "tile", "wave"), P()),
        check_vma=False,
    )
```

```python
import functools

import jax
import jax.numpy as jnp
from jax import lax
from jax.experimental import pallas as pl
from jax.experimental.pallas import tpu as pltpu
from jax.sharding import PartitionSpec as P

ITERS = 3
SOURCE_STRENGTH = 50.0
TINY = 1e-30
LANES = 128
SUBLANES = 8


def harmonic(left_val, right_val):
    return 2.0 * left_val * right_val / jnp.maximum(left_val + right_val, TINY)


def safe_div(num, den):
    return jnp.where(den > 0.0, num / jnp.where(den > 0.0, den, 1.0), 0.0)


def tree_sum(values):
    values = list(values)
    while len(values) > 1:
        values = [values[i] + values[i + 1] for i in range(0, len(values), 2)]
    return values[0]


def swap(value, axis, mask, size):
    return lax.ppermute(value, axis, [(i, i ^ mask) for i in range(size)])


def tile_parts(value, axis):
    size = lax.axis_size(axis)
    parts = [value]
    bit = 1
    while bit < size:
        value = tree_sum(parts)
        masks = [bit]
        if bit > 1 and bit * 2 < size:
            masks.append(bit * 2)
        offsets = [0]
        for mask in masks:
            offsets += [o ^ mask for o in offsets]
        parts = [value] + [swap(value, axis, o, size) for o in offsets[1:]]
        bit = masks[-1] * 2
    return parts


def issued(values, order):
    return [values[i] for i in order], [order.index(i) for i in range(len(values))]


def step_polynomial(moments):
    def inner(poly):
        return sum(a * b * moments[i + j] for i, a in enumerate(poly) for j, b in enumerate(poly))

    def energy(poly):
        return sum(
            a * b * (moments[i + j] - moments[i + j + 1])
            for i, a in enumerate(poly)
            for j, b in enumerate(poly)
        )

    one = jnp.ones_like(moments[0])
    zero = jnp.zeros_like(moments[0])
    res, way, total = [one], [one], [zero] * ITERS
    gamma = moments[0]
    for iteration in range(ITERS):
        alpha = safe_div(gamma, energy(way))
        total = [t + alpha * (way[i] if i < len(way) else zero) for i, t in enumerate(total)]
        if iteration + 1 < ITERS:
            longer = way + [zero]
            shifted = [zero] + way
            res = [r - alpha * (a - b) for r, a, b in zip(res + [zero], longer, shifted)]
            gamma_next = jnp.maximum(inner(res), 0.0)
            ratio = safe_div(gamma_next, gamma)
            way = [r + ratio * a for r, a in zip(res, longer)]
            gamma = gamma_next
    return total


VMEM = pl.BlockSpec(memory_space=pltpu.VMEM)
PARAMS = pltpu.CompilerParams(vmem_limit_bytes=16 << 20)


def vmem_call(kernel, out_shape, inputs, scratch=()):
    return pl.pallas_call(
        kernel,
        out_shape=out_shape,
        in_specs=[VMEM] * len(inputs),
        out_specs=jax.tree.map(lambda _: VMEM, out_shape),
        scratch_shapes=list(scratch),
        compiler_params=PARAMS,
    )(*inputs)


def cols(c):
    return slice(c * LANES, (c + 1) * LANES)


def add(sums, key, value):
    sums[key] = sums[key] + value if key in sums else value


def edge_kernel(field_hbm, class_hbm, cond_hbm, row_hbm, col_hbm, *refs):
    far_ref, near_ref, par_ref, spot_ref = refs[:4]
    field_ref, class_ref, cond_ref, row_ref, col_ref, sems = refs[4:]
    sources, rows, _ = field_hbm.shape
    halo = far_ref.shape[1]
    pairs = []
    for i, at in enumerate((0, rows - SUBLANES)):
        pairs.append((field_hbm.at[:, pl.ds(at, SUBLANES)], field_ref.at[i]))
        pairs.append((class_hbm.at[pl.ds(at, SUBLANES)], class_ref.at[i]))
    pairs += [
        (cond_hbm, cond_ref),
        (row_hbm, row_ref),
        (col_hbm, col_ref),
    ]
    copies = [
        pltpu.make_async_copy(start, end, sems.at[i]) for i, (start, end) in enumerate(pairs)
    ]
    for copy in copies:
        copy.start()
    for copy in copies:
        copy.wait()
    even = lax.axis_index("tile") % 2 == 0
    spare = SUBLANES - halo
    for s in range(sources):
        first, last = field_ref[0, s, :halo], field_ref[1, s, spare:]
        far_ref[s] = jnp.where(even, first, last)
        near_ref[s] = jnp.where(even, last, first)
    first = class_ref[0, :halo].astype(jnp.float32) + 1.0
    last = class_ref[1, spare:].astype(jnp.float32) + 1.0
    far_ref[sources] = jnp.where(even, first, last)
    near_ref[sources] = jnp.where(even, last, first)
    tile = (SUBLANES, LANES)
    n_class = cond_ref.shape[0]
    for i in range(n_class):
        par_ref[i] = jnp.full(tile, cond_ref[i], jnp.float32)
    for s in range(sources):
        spot_ref[s] = jnp.full(tile, row_ref[s], jnp.int32)
        spot_ref[sources + s] = jnp.full(tile, col_ref[s], jnp.int32)


def neighbours(get, chunks, lane):
    here = get(0)
    last = LANES - 1
    from_right = pltpu.roll(here, last, 1)
    before = None
    for c in range(chunks):
        from_left = pltpu.roll(here, 1, 1)
        left = jnp.where(lane == 0, before, from_left) if c else from_left
        right = from_right
        if c + 1 < chunks:
            following = get(c + 1)
            from_next = pltpu.roll(following, last, 1)
            right = jnp.where(lane == last, from_next, from_right)
        yield c, here, left, right
        before = from_left
        if c + 1 < chunks:
            here, from_right = following, from_next


def conductivity(ids, values):
    sigma = jnp.zeros(ids.shape, jnp.float32)
    for i, value in enumerate(values):
        sigma = jnp.where(ids == i + 1.0, value, sigma)
    return sigma


def tall(tile, rows):
    return jnp.concatenate([tile] * (rows // SUBLANES), axis=0)


def line_sum(value):
    return jnp.sum(value, axis=0, keepdims=True)


def lines_of(tops, sums, sources):
    lines = list(tops)
    for n in range(2 * ITERS):
        for s in range(sources):
            lines.append(line_sum(sums[n, s]))
    return lines


def inner_kernel(field_ref, class_ref, par_ref, wave_ref, spot_ref, pick_ref, *refs):
    x_ref, *basis_refs = refs[: 1 + ITERS]
    pay_ref, sig_ref, side_ref, above_ref, below_ref, hit_ref, square_ref = refs[1 + ITERS : 8 + ITERS]
    up_ref, down_ref, west_ref, east_ref, diag_ref, inv_ref = refs[8 + ITERS :]
    sources, rows, _ = field_ref.shape
    chunks, total = x_ref.shape[1:3]
    n_class = par_ref.shape[0]
    halo = (total - rows) // 2
    lane = lax.broadcasted_iota(jnp.int32, (total, LANES), 1)
    row = lax.broadcasted_iota(jnp.int32, (total, LANES), 0)
    rows_at = row + (lax.axis_index("tile") * rows - halo)
    blank = jnp.zeros((halo, LANES), jnp.float32)
    inner = slice(SUBLANES, total - SUBLANES)
    wave = jnp.broadcast_to(wave_ref[...], (SUBLANES, LANES))
    square_ref[...] = wave * wave
    square = tall(square_ref[...], total)
    values = [tall(par_ref[i], rows) for i in range(n_class)]

    def widened(value):
        return jnp.concatenate([blank, value, blank], axis=0)

    for c in range(chunks):
        ids = class_ref[:, cols(c)].astype(jnp.float32) + 1.0
        sig_ref[c] = widened(conductivity(ids, values))
        for s in range(sources):
            x_ref[s, c] = widened(field_ref[s, :, cols(c)])
    for c, sigma, left, _ in neighbours(lambda c: sig_ref[c], chunks, lane):
        face = harmonic(left, sigma)
        side_ref[c] = jnp.where(lane == 0, 0.0, face) if c == 0 else face
        up = harmonic(pltpu.roll(sigma, 1, 0), sigma)
        above_ref[c] = up
        below_ref[c] = pltpu.roll(up, total - 1, 0)
    at_source = [rows_at == tall(spot_ref[s], total) for s in range(sources)]
    for c, west, _, east in neighbours(lambda c: side_ref[c], chunks, lane):
        up, down = above_ref[c], below_ref[c]
        sigma = sig_ref[c]
        diag = up + down + west + square * sigma
        if c == chunks - 1:
            bottom = lane == LANES - 1
            diag = diag + jnp.where(bottom, sigma, east)
            east = jnp.where(bottom, 0.0, east)
        else:
            diag = diag + east
        inverse = 1.0 / jnp.maximum(diag, TINY)
        diag_ref[c] = diag
        inv_ref[c] = inverse
        up_ref[c] = up * inverse
        down_ref[c] = down * inverse
        west_ref[c] = west * inverse
        east_ref[c] = east * inverse

    def spread(c, here, left, right):
        return (
            up_ref[c] * pltpu.roll(here, 1, 0)
            + down_ref[c] * pltpu.roll(here, total - 1, 0)
            + west_ref[c] * left
            + east_ref[c] * right
        )

    def fold(value):
        return sum(value[r : r + SUBLANES] for r in range(0, value.shape[0], SUBLANES))

    sums = {}
    for s in range(sources):
        column = tall(spot_ref[sources + s], total)
        for c, here, left, right in neighbours(lambda c: x_ref[s, c], chunks, lane):
            charge = jnp.where(
                at_source[s] & (lane + c * LANES == column), SOURCE_STRENGTH, 0.0
            )
            hit_ref[0, s, c] = charge[:SUBLANES]
            hit_ref[1, s, c] = charge[total - SUBLANES :]
            new = charge * inv_ref[c] - (here - spread(c, here, left, right))
            basis_refs[0][s, c] = new
            own = new[inner]
            add(sums, (0, s), fold(diag_ref[c, inner] * own * own))
    for i in range(ITERS):
        for s in range(sources):
            for c, here, left, right in neighbours(lambda c: basis_refs[i][s, c], chunks, lane):
                new = spread(c, here, left, right)
                own = new[inner]
                weighted = diag_ref[c, inner] * own
                add(sums, (2 * i + 1, s), fold(weighted * here[inner]))
                if i + 1 < ITERS:
                    basis_refs[i + 1][s, c] = new
                    add(sums, (2 * i + 2, s), fold(weighted * own))
    picker = rows_at[inner] == pick_ref[...]
    tops = []
    for ref in (x_ref, *basis_refs):
        for s in range(sources):
            top = jnp.broadcast_to(ref[s, 0, inner, 0:1], (total - 2 * SUBLANES, LANES))
            tops.append(line_sum(fold(jnp.where(picker, top, 0.0))))
    pay_ref[...] = jnp.zeros(pay_ref.shape, jnp.float32)
    for i, line in enumerate(lines_of(tops, sums, sources)):
        pay_ref[i : i + 1, :] = line


def outer_kernel(far_ref, near_ref, par_ref, pick_ref, *refs):
    x_in, *basis_in = refs[: 1 + ITERS]
    pay_in, sig_in, side_in, above_in, below_in, hit_in, square_in = refs[1 + ITERS : 8 + ITERS]
    outs = refs[8 + ITERS :]
    x_ref, *basis_refs = outs[: 1 + ITERS]
    pay_ref = outs[1 + ITERS]
    sigma_ref, west_raw, up_ref, down_ref, west_ref, east_ref, diag_ref, inv_ref = outs[2 + ITERS :]
    sources, chunks, total, _ = x_in.shape
    n_class = par_ref.shape[0]
    halo = far_ref.shape[1]
    rows = total - 2 * halo
    lane = lax.broadcasted_iota(jnp.int32, (SUBLANES, LANES), 1)
    row = lax.broadcasted_iota(jnp.int32, (SUBLANES, LANES), 0)
    tile = lax.axis_index("tile")
    even = tile % 2 == 0
    square = square_in[...]
    values = [par_ref[i] for i in range(n_class)]
    upper = row < halo
    last = total - SUBLANES
    own = (jnp.logical_not(upper), upper)

    inside = (tile > 0) & (tile < lax.axis_size("tile") - 1)

    def came_in(index, c):
        far = jnp.where(inside, far_ref[index, :, cols(c)], 0.0)
        near = near_ref[index, :, cols(c)]
        return jnp.concatenate(
            [jnp.where(even, far, near), jnp.where(even, near, far)], axis=0
        )

    def set_in(new, kept):
        return jnp.where(upper, new, kept[:SUBLANES]), jnp.where(upper, kept[last:], new)

    for c in range(chunks):
        sigma_ref[c] = conductivity(came_in(sources, c), values)
        for s in range(sources):
            x_ref[0, s, c], x_ref[1, s, c] = set_in(came_in(s, c), x_in.at[s, c])
    for c, fresh, left, _ in neighbours(lambda c: sigma_ref[c], chunks, lane):
        face = harmonic(left, fresh)
        face = jnp.where(lane == 0, 0.0, face) if c == 0 else face
        west_raw[0, c], west_raw[1, c] = set_in(face, side_in.at[c])
    for e in (0, 1):
        for c, west, _, east in neighbours(lambda c: west_raw[e, c], chunks, lane):
            fresh = sigma_ref[c]
            first, end = set_in(fresh, sig_in.at[c])
            sigma = end if e else first
            face = harmonic(
                jnp.where(upper, pltpu.roll(first, SUBLANES - 1, 0), pltpu.roll(end, 1, 0)), fresh
            )
            if e:
                up = jnp.where(upper, above_in[c, last:], face)
                down = pltpu.roll(up, SUBLANES - 1, 0)
            else:
                down = jnp.where(upper, face, below_in[c, :SUBLANES])
                up = pltpu.roll(down, 1, 0)
            diag = up + down + west + square * sigma
            if c == chunks - 1:
                bottom = lane == LANES - 1
                diag = diag + jnp.where(bottom, sigma, east)
                east = jnp.where(bottom, 0.0, east)
            else:
                diag = diag + east
            inverse = 1.0 / jnp.maximum(diag, TINY)
            diag_ref[e, c] = jnp.where(own[e], diag, 0.0)
            inv_ref[e, c] = inverse
            up_ref[e, c] = up * inverse
            down_ref[e, c] = down * inverse
            west_ref[e, c] = west * inverse
            east_ref[e, c] = east * inverse

    def spread(whole, e, s, c, here, left, right):
        above = pltpu.roll(here, 1, 0)
        below = pltpu.roll(here, SUBLANES - 1, 0)
        if e:
            above = jnp.where(row == 0, whole[s, c, last - 1 : last], above)
        else:
            below = jnp.where(row == SUBLANES - 1, whole[s, c, SUBLANES : SUBLANES + 1], below)
        return (
            up_ref[e, c] * above
            + down_ref[e, c] * below
            + west_ref[e, c] * left
            + east_ref[e, c] * right
        )

    sums = {}
    both = [(e, s) for e in (0, 1) for s in range(sources)]
    for e, s in both:
        for c, here, left, right in neighbours(lambda c: x_ref[e, s, c], chunks, lane):
            new = hit_in[e, s, c] * inv_ref[e, c] - (
                here - spread(x_in, e, s, c, here, left, right)
            )
            basis_refs[0][e, s, c] = new
            add(sums, (0, s), diag_ref[e, c] * new * new)
    for i in range(ITERS):
        for e, s in both:
            for c, here, left, right in neighbours(
                lambda c: basis_refs[i][e, s, c], chunks, lane
            ):
                new = spread(basis_in[i], e, s, c, here, left, right)
                weighted = diag_ref[e, c] * new
                add(sums, (2 * i + 1, s), weighted * here)
                if i + 1 < ITERS:
                    basis_refs[i + 1][e, s, c] = new
                    add(sums, (2 * i + 2, s), weighted * new)
    pickers = [
        own[e] & (row + (tile * rows - halo + at) == pick_ref[...]) for e, at in ((0, 0), (1, last))
    ]
    tops = []
    for ref in (x_ref, *basis_refs):
        for s in range(sources):
            line = 0.0
            for e in (0, 1):
                top = jnp.broadcast_to(ref[e, s, 0, :, 0:1], (SUBLANES, LANES))
                line = line + jnp.where(pickers[e], top, 0.0)
            tops.append(line_sum(line))
    pay_ref[...] = pay_in[...]
    for i, line in enumerate(lines_of(tops, sums, sources)):
        pay_ref[i : i + 1, :] += line


def combine_kernel(places, weight_ref, *refs):
    n_parts, n_pay = ITERS + 1, len(places)
    packed = tree_sum([refs[i][...] for i in places])
    part_refs = refs[n_pay : n_pay + n_parts]
    edge_refs = refs[n_pay + n_parts : n_pay + 2 * n_parts]
    out_refs = refs[n_pay + 2 * n_parts :]
    sources, _, total, _ = part_refs[0].shape
    share = out_refs[0].shape[1]
    rows = (out_refs[0].shape[0] - SUBLANES) // sources
    halo = (total - rows) // 2
    first = n_parts * sources
    totals = jnp.sum(packed[first : first + 2 * ITERS * sources], axis=1, keepdims=True)
    poly = step_polynomial([totals[n * sources : (n + 1) * sources] for n in range(2 * ITERS)])
    weight = weight_ref[...]
    scale = [[weight] + [weight * p[s : s + 1] for p in poly] for s in range(sources)]
    read = [
        sum(scale[s][i] * packed[i * sources + s : i * sources + s + 1] for i in range(n_parts))
        for s in range(sources)
    ]
    split = len(out_refs) > 1
    wave = lax.axis_index("wave") if split else 0
    per = share // LANES
    inner = slice(SUBLANES, total - SUBLANES)
    for mask, out_ref in enumerate(out_refs):
        block = wave ^ mask if split else 0
        for s in range(sources):
            for k in range(per):
                c = block * per + k
                middle = sum(scale[s][i] * part_refs[i][s, c, inner] for i in range(n_parts))
                top, end = (
                    sum(scale[s][i] * edge_refs[i][e, s, c] for i in range(n_parts)) for e in (0, 1)
                )
                value = jnp.concatenate([top[halo:], middle, end[: SUBLANES - halo]], axis=0)
                out_ref[s * rows : (s + 1) * rows, cols(k)] = value
        out_ref[sources * rows :, :] = jnp.zeros((SUBLANES, share), jnp.float32)
        for s in range(sources):
            out_ref[sources * rows + s : sources * rows + s + 1, :LANES] = read[s]


def sum_kernel(places, *refs):
    part_refs, (field_ref, read_ref) = [refs[i] for i in places], refs[-2:]
    sources, rows, _ = field_ref.shape
    electrodes = read_ref.shape[1]
    for s in range(sources):
        field_ref[s] = tree_sum([r[s * rows : (s + 1) * rows, :] for r in part_refs])
    last = tree_sum([r[sources * rows :, :LANES] for r in part_refs])
    read_ref[...] = last[:sources, :electrodes]


def shards(
    warm_start,
    class_map,
    conductivities,
    wavenumbers,
    weights,
    source_row,
    source_col,
    electrode_row,
):
    rows, depth = class_map.shape
    sources = warm_start.shape[1]
    electrodes = electrode_row.shape[0]
    tiles, waves = lax.axis_size("tile"), lax.axis_size("wave")
    wave = lax.axis_index("wave")
    halo = ITERS + 1
    field = warm_start[0]
    f32 = jnp.float32
    n_class = conductivities.shape[0]
    rim = jax.ShapeDtypeStruct((sources + 1, halo, depth), f32)
    raw = [
        field,
        class_map,
        conductivities,
        source_row,
        source_col,
    ]
    far, near, params, spots = pl.pallas_call(
        edge_kernel,
        out_shape=[
            rim,
            rim,
            jax.ShapeDtypeStruct((n_class, SUBLANES, LANES), f32),
            jax.ShapeDtypeStruct((2 * sources, SUBLANES, LANES), jnp.int32),
        ],
        in_specs=[pl.BlockSpec(memory_space=pltpu.HBM)] * len(raw),
        out_specs=[VMEM] * 4,
        scratch_shapes=[
            pltpu.VMEM((2, sources, SUBLANES, depth), f32),
            pltpu.VMEM((2, SUBLANES, depth), jnp.int32),
            *[pltpu.SMEM(a.shape, a.dtype) for a in raw[2:]],
            pltpu.SemaphoreType.DMA((len(raw) + 2,)),
        ],
        compiler_params=PARAMS,
    )(*[pltpu.with_memory_space_constraint(a, pltpu.HBM) for a in raw])
    ring = [(i, (i + 1) % tiles) for i in range(1, tiles, 2)]
    far = lax.ppermute(far, "tile", ring + [(j, i) for i, j in ring])
    near = swap(near, "tile", 1, tiles)
    total, chunks = rows + 2 * halo, depth // LANES
    picks = jnp.pad(electrode_row, (0, LANES - electrodes), constant_values=-1)[None]
    wide = jax.ShapeDtypeStruct((sources, chunks, total, LANES), f32)
    flat = jax.ShapeDtypeStruct((chunks, total, LANES), f32)
    n_lines = sources * (3 * ITERS + 1)
    pay = jax.ShapeDtypeStruct((-(-n_lines // SUBLANES) * SUBLANES, LANES), f32)
    ends = jax.ShapeDtypeStruct((2, sources, chunks, SUBLANES, LANES), f32)
    tile = jax.ShapeDtypeStruct((SUBLANES, LANES), f32)
    inside = vmem_call(
        inner_kernel,
        [wide] * (ITERS + 1) + [pay, flat, flat, flat, flat, ends, tile],
        [field, class_map, params, wavenumbers[None], spots, picks],
        [pltpu.VMEM((chunks, total, LANES), f32)] * 6,
    )
    pair = pltpu.VMEM((2, chunks, SUBLANES, LANES), f32)
    outside = vmem_call(
        outer_kernel,
        [ends] * (ITERS + 1) + [pay],
        [far, near, params, picks, *inside],
        [pltpu.VMEM((chunks, SUBLANES, LANES), f32)] + [pair] * 7,
    )
    packed = tile_parts(outside[-1], "tile")
    packed, places = issued(packed, (0, *range(len(packed) - 1, 0, -1)))
    share = depth // waves
    split = share % LANES == 0
    width = share if split else depth
    block = jax.ShapeDtypeStruct((sources * rows + SUBLANES, width), f32)
    pieces = vmem_call(
        functools.partial(combine_kernel, places),
        [block] * (waves if split else 1),
        [weights[None], *packed, *inside[: ITERS + 1], *outside[: ITERS + 1]],
    )
    if not split:
        n = sources * rows
        read = pieces[0][n : n + sources, :electrodes].reshape(-1, share)
        pieces = [
            jnp.concatenate(
                [lax.dynamic_slice_in_dim(pieces[0][:n], (wave ^ mask) * share, share, 1), read]
            )
            for mask in range(waves)
        ]
    pieces = [pieces[0]] + [swap(pieces[m], "wave", m, waves) for m in range(1, waves)]
    if not split:
        final = tree_sum(pieces)
        return (
            final[: sources * rows].reshape(sources, rows, share),
            final[sources * rows :].reshape(sources, electrodes),
        )
    pieces, places = issued(pieces, (0, waves - 1, *range(1, waves - 1)))
    return tuple(
        vmem_call(
            functools.partial(sum_kernel, places),
            [
                jax.ShapeDtypeStruct((sources, rows, share), f32),
                jax.ShapeDtypeStruct((sources, electrodes), f32),
            ],
            pieces,
        )
    )


def solution(mesh):
    return jax.shard_map(
        shards,
        mesh=mesh,
        in_specs=(
            P("wave", None, "tile", None),
            P("tile", None),
            P(),
            P("wave"),
            P("wave"),
            P(),
            P(),
            P(),
        ),
        out_specs=(P(None, "tile", "wave"), P()),
        check_vma=False,
    )
```

```python
import functools

import jax
import jax.numpy as jnp
from jax import lax
from jax.experimental import pallas as pl
from jax.experimental.pallas import tpu as pltpu
from jax.sharding import PartitionSpec as P


ITERS = 3
SOURCE_STRENGTH = 50.0
TINY = 1e-30
LANES = 128
SUBLANES = 8


def harmonic(left_val, right_val):
    return 2.0 * left_val * right_val / jnp.maximum(left_val + right_val, TINY)


def safe_div(num, den):
    return jnp.where(den > 0.0, num / jnp.where(den > 0.0, den, 1.0), 0.0)


def tree_sum(values):
    values = list(values)
    while len(values) > 1:
        values = [values[i] + values[i + 1] for i in range(0, len(values), 2)]
    return values[0]


def swap(value, axis, mask, size):
    return lax.ppermute(value, axis, [(i, i ^ mask) for i in range(size)])


def tile_parts(value, axis):
    size = lax.axis_size(axis)
    parts = [value]
    bit = 1
    while bit < size:
        value = tree_sum(parts)
        masks = [bit]
        if bit > 1 and bit * 2 < size:
            masks.append(bit * 2)
        offsets = [0]
        for mask in masks:
            offsets += [o ^ mask for o in offsets]
        parts = [value] + [swap(value, axis, o, size) for o in offsets[1:]]
        bit = masks[-1] * 2
    return parts


def issued(values, order):
    return [values[i] for i in order], [order.index(i) for i in range(len(values))]


def step_polynomial(moments):
    def inner(poly):
        return sum(a * b * moments[i + j] for i, a in enumerate(poly) for j, b in enumerate(poly))

    def energy(poly):
        return sum(
            a * b * (moments[i + j] - moments[i + j + 1])
            for i, a in enumerate(poly)
            for j, b in enumerate(poly)
        )

    one = jnp.ones_like(moments[0])
    zero = jnp.zeros_like(moments[0])
    res, way, total = [one], [one], [zero] * ITERS
    gamma = moments[0]
    for iteration in range(ITERS):
        alpha = safe_div(gamma, energy(way))
        total = [t + alpha * (way[i] if i < len(way) else zero) for i, t in enumerate(total)]
        if iteration + 1 < ITERS:
            longer = way + [zero]
            shifted = [zero] + way
            res = [r - alpha * (a - b) for r, a, b in zip(res + [zero], longer, shifted)]
            gamma_next = jnp.maximum(inner(res), 0.0)
            ratio = safe_div(gamma_next, gamma)
            way = [r + ratio * a for r, a in zip(res, longer)]
            gamma = gamma_next
    return total


VMEM = pl.BlockSpec(memory_space=pltpu.VMEM)
PARAMS = pltpu.CompilerParams(vmem_limit_bytes=16 << 20)


def vmem_call(kernel, out_shape, inputs, scratch=(), aliases=()):
    return pl.pallas_call(
        kernel,
        out_shape=out_shape,
        in_specs=[VMEM] * len(inputs),
        out_specs=jax.tree.map(lambda _: VMEM, out_shape),
        scratch_shapes=list(scratch),
        input_output_aliases=dict(aliases),
        compiler_params=PARAMS,
    )(*inputs)


def cols(c):
    return slice(c * LANES, (c + 1) * LANES)


def add(sums, key, value):
    sums[key] = sums[key] + value if key in sums else value


def edge_kernel(field_hbm, class_hbm, cond_hbm, row_hbm, col_hbm, *refs):
    far_ref, near_ref, par_ref, spot_ref = refs[:4]
    field_ref, class_ref, cond_ref, row_ref, col_ref, sems = refs[4:]
    sources, rows, _ = field_hbm.shape
    halo = far_ref.shape[1]
    pairs = []
    for i, at in enumerate((0, rows - SUBLANES)):
        pairs.append((field_hbm.at[:, pl.ds(at, SUBLANES)], field_ref.at[i]))
        pairs.append((class_hbm.at[pl.ds(at, SUBLANES)], class_ref.at[i]))
    pairs += [
        (cond_hbm, cond_ref),
        (row_hbm, row_ref),
        (col_hbm, col_ref),
    ]
    copies = [
        pltpu.make_async_copy(start, end, sems.at[i]) for i, (start, end) in enumerate(pairs)
    ]
    for copy in copies:
        copy.start()
    for copy in copies:
        copy.wait()
    even = lax.axis_index("tile") % 2 == 0
    spare = SUBLANES - halo
    for s in range(sources):
        first, last = field_ref[0, s, :halo], field_ref[1, s, spare:]
        far_ref[s] = jnp.where(even, first, last)
        near_ref[s] = jnp.where(even, last, first)
    first = class_ref[0, :halo].astype(jnp.float32) + 1.0
    last = class_ref[1, spare:].astype(jnp.float32) + 1.0
    far_ref[sources] = jnp.where(even, first, last)
    near_ref[sources] = jnp.where(even, last, first)
    tile = (SUBLANES, LANES)
    n_class = cond_ref.shape[0]
    for i in range(n_class):
        par_ref[i] = jnp.full(tile, cond_ref[i], jnp.float32)
    for s in range(sources):
        spot_ref[s] = jnp.full(tile, row_ref[s], jnp.int32)
        spot_ref[sources + s] = jnp.full(tile, col_ref[s], jnp.int32)


def neighbours(get, chunks, lane):
    here = get(0)
    last = LANES - 1
    from_right = pltpu.roll(here, last, 1)
    before = None
    for c in range(chunks):
        from_left = pltpu.roll(here, 1, 1)
        left = jnp.where(lane == 0, before, from_left) if c else from_left
        right = from_right
        if c + 1 < chunks:
            following = get(c + 1)
            from_next = pltpu.roll(following, last, 1)
            right = jnp.where(lane == last, from_next, from_right)
        yield c, here, left, right
        before = from_left
        if c + 1 < chunks:
            here, from_right = following, from_next


def conductivity(ids, values):
    sigma = jnp.zeros(ids.shape, jnp.float32)
    for i, value in enumerate(values):
        sigma = jnp.where(ids == i + 1.0, value, sigma)
    return sigma


def tall(tile, rows):
    return jnp.concatenate([tile] * (rows // SUBLANES), axis=0)


def line_sum(value):
    return jnp.sum(value, axis=0, keepdims=True)


def lines_of(tops, sums, sources):
    lines = list(tops)
    for n in range(2 * ITERS):
        for s in range(sources):
            lines.append(line_sum(sums[n, s]))
    return lines


def inner_kernel(field_ref, class_ref, par_ref, wave_ref, spot_ref, pick_ref, *refs):
    x_ref, *basis_refs = refs[: 1 + ITERS]
    pay_ref, sig_ref, side_ref, above_ref, below_ref, hit_ref, square_ref = refs[1 + ITERS : 8 + ITERS]
    up_ref, down_ref, west_ref, east_ref, diag_ref, inv_ref = refs[8 + ITERS :]
    sources, rows, _ = field_ref.shape
    chunks, total = x_ref.shape[1:3]
    n_class = par_ref.shape[0]
    halo = (total - rows) // 2
    lane = lax.broadcasted_iota(jnp.int32, (total, LANES), 1)
    row = lax.broadcasted_iota(jnp.int32, (total, LANES), 0)
    rows_at = row + (lax.axis_index("tile") * rows - halo)
    blank = jnp.zeros((halo, LANES), jnp.float32)
    inner = slice(SUBLANES, total - SUBLANES)
    wave = jnp.broadcast_to(wave_ref[...], (SUBLANES, LANES))
    square_ref[...] = wave * wave
    square = tall(square_ref[...], total)
    values = [tall(par_ref[i], rows) for i in range(n_class)]

    def widened(value):
        return jnp.concatenate([blank, value, blank], axis=0)

    for c in range(chunks):
        ids = class_ref[:, cols(c)].astype(jnp.float32) + 1.0
        sig_ref[c] = widened(conductivity(ids, values))
        for s in range(sources):
            x_ref[s, c] = widened(field_ref[s, :, cols(c)])
    for c, sigma, left, _ in neighbours(lambda c: sig_ref[c], chunks, lane):
        face = harmonic(left, sigma)
        side_ref[c] = jnp.where(lane == 0, 0.0, face) if c == 0 else face
        up = harmonic(pltpu.roll(sigma, 1, 0), sigma)
        above_ref[c] = up
        below_ref[c] = pltpu.roll(up, total - 1, 0)
    at_source = [rows_at == tall(spot_ref[s], total) for s in range(sources)]
    for c, west, _, east in neighbours(lambda c: side_ref[c], chunks, lane):
        up, down = above_ref[c], below_ref[c]
        sigma = sig_ref[c]
        diag = up + down + west + square * sigma
        if c == chunks - 1:
            bottom = lane == LANES - 1
            diag = diag + jnp.where(bottom, sigma, east)
            east = jnp.where(bottom, 0.0, east)
        else:
            diag = diag + east
        inverse = 1.0 / jnp.maximum(diag, TINY)
        diag_ref[c] = diag
        inv_ref[c] = inverse
        up_ref[c] = up * inverse
        down_ref[c] = down * inverse
        west_ref[c] = west * inverse
        east_ref[c] = east * inverse

    def spread(c, here, left, right):
        return (
            up_ref[c] * pltpu.roll(here, 1, 0)
            + down_ref[c] * pltpu.roll(here, total - 1, 0)
            + west_ref[c] * left
            + east_ref[c] * right
        )

    def fold(value):
        return sum(value[r : r + SUBLANES] for r in range(0, value.shape[0], SUBLANES))

    sums = {}
    for s in range(sources):
        column = tall(spot_ref[sources + s], total)
        for c, here, left, right in neighbours(lambda c: x_ref[s, c], chunks, lane):
            charge = jnp.where(
                at_source[s] & (lane + c * LANES == column), SOURCE_STRENGTH, 0.0
            )
            hit_ref[0, s, c] = charge[:SUBLANES]
            hit_ref[1, s, c] = charge[total - SUBLANES :]
            new = charge * inv_ref[c] - (here - spread(c, here, left, right))
            basis_refs[0][s, c] = new
            own = new[inner]
            add(sums, (0, s), fold(diag_ref[c, inner] * own * own))
    for i in range(ITERS):
        for s in range(sources):
            for c, here, left, right in neighbours(lambda c: basis_refs[i][s, c], chunks, lane):
                new = spread(c, here, left, right)
                own = new[inner]
                weighted = diag_ref[c, inner] * own
                add(sums, (2 * i + 1, s), fold(weighted * here[inner]))
                if i + 1 < ITERS:
                    basis_refs[i + 1][s, c] = new
                    add(sums, (2 * i + 2, s), fold(weighted * own))
    picker = rows_at[inner] == pick_ref[...]
    tops = []
    for ref in (x_ref, *basis_refs):
        for s in range(sources):
            top = jnp.broadcast_to(ref[s, 0, inner, 0:1], (total - 2 * SUBLANES, LANES))
            tops.append(line_sum(fold(jnp.where(picker, top, 0.0))))
    pay_ref[...] = jnp.zeros(pay_ref.shape, jnp.float32)
    for i, line in enumerate(lines_of(tops, sums, sources)):
        pay_ref[i : i + 1, :] = line


def outer_kernel(even_end, wraps, came_ref, par_ref, pick_ref, *refs):
    x_in, *basis_in = refs[: 1 + ITERS]
    pay_in, sig_in, side_in, above_in, below_in, hit_in, square_in = refs[1 + ITERS : 8 + ITERS]
    outs = refs[-(10 + ITERS) :]
    x_out, *basis_outs = outs[: 1 + ITERS]
    pay_ref = outs[1 + ITERS]
    sigma_ref, west_raw, up_ref, down_ref, west_ref, east_ref, diag_ref, inv_ref = outs[2 + ITERS :]
    sources, chunks, total, _ = x_in.shape
    halo = came_ref.shape[1]
    rows = total - 2 * halo
    lane = lax.broadcasted_iota(jnp.int32, (SUBLANES, LANES), 1)
    row = lax.broadcasted_iota(jnp.int32, (SUBLANES, LANES), 0)
    tile = lax.axis_index("tile")
    even = tile % 2 == 0
    square = square_in[...]
    values = [par_ref[i] for i in range(par_ref.shape[0])]
    upper = row < halo
    last = total - SUBLANES
    inside = (tile > 0) & (tile < lax.axis_size("tile") - 1)

    def came_in(index, c):
        value = came_ref[index, :, cols(c)]
        if wraps:
            value = jnp.where(inside, value, 0.0)
        return jnp.concatenate([value, value], axis=0)

    def one_end(e):
        at = last if e else 0
        tile_at = slice(at, at + SUBLANES)
        own = upper if e else jnp.logical_not(upper)
        x_ref, *basis_refs = [r.at[e] for r in (x_out, *basis_outs)]

        def set_in(new, kept):
            return jnp.where(own, kept[tile_at], new)

        for c in range(chunks):
            sigma_ref[c] = conductivity(came_in(sources, c), values)
            for s in range(sources):
                x_ref[s, c] = set_in(came_in(s, c), x_in.at[s, c])
        for c, fresh, left, _ in neighbours(lambda c: sigma_ref[c], chunks, lane):
            face = harmonic(left, fresh)
            face = jnp.where(lane == 0, 0.0, face) if c == 0 else face
            west_raw[c] = set_in(face, side_in.at[c])
        for c, west, _, east in neighbours(lambda c: west_raw[c], chunks, lane):
            sigma = set_in(sigma_ref[c], sig_in.at[c])
            face = harmonic(pltpu.roll(sigma, 1 if e else SUBLANES - 1, 0), sigma)
            if e:
                up = set_in(face, above_in.at[c])
                down = pltpu.roll(up, SUBLANES - 1, 0)
            else:
                down = set_in(face, below_in.at[c])
                up = pltpu.roll(down, 1, 0)
            diag = up + down + west + square * sigma
            if c == chunks - 1:
                bottom = lane == LANES - 1
                diag = diag + jnp.where(bottom, sigma, east)
                east = jnp.where(bottom, 0.0, east)
            else:
                diag = diag + east
            inverse = 1.0 / jnp.maximum(diag, TINY)
            diag_ref[c] = jnp.where(own, diag, 0.0)
            inv_ref[c] = inverse
            up_ref[c] = up * inverse
            down_ref[c] = down * inverse
            west_ref[c] = west * inverse
            east_ref[c] = east * inverse

        def spread(whole, s, c, here, left, right):
            above = pltpu.roll(here, 1, 0)
            below = pltpu.roll(here, SUBLANES - 1, 0)
            if e:
                above = jnp.where(row == 0, whole[s, c, last - 1 : last], above)
            else:
                below = jnp.where(
                    row == SUBLANES - 1, whole[s, c, SUBLANES : SUBLANES + 1], below
                )
            return (
                up_ref[c] * above
                + down_ref[c] * below
                + west_ref[c] * left
                + east_ref[c] * right
            )

        sums = {}
        for s in range(sources):
            for c, here, left, right in neighbours(lambda c: x_ref[s, c], chunks, lane):
                new = hit_in[e, s, c] * inv_ref[c] - (here - spread(x_in, s, c, here, left, right))
                basis_refs[0][s, c] = new
                add(sums, (0, s), diag_ref[c] * new * new)
        for i in range(ITERS):
            for s in range(sources):
                for c, here, left, right in neighbours(
                    lambda c: basis_refs[i][s, c], chunks, lane
                ):
                    new = spread(basis_in[i], s, c, here, left, right)
                    weighted = diag_ref[c] * new
                    add(sums, (2 * i + 1, s), weighted * here)
                    if i + 1 < ITERS:
                        basis_refs[i + 1][s, c] = new
                        add(sums, (2 * i + 2, s), weighted * new)
        picker = own & (row + (tile * rows - halo + at) == pick_ref[...])
        tops = []
        for ref in (x_ref, *basis_refs):
            for s in range(sources):
                top = jnp.broadcast_to(ref[s, 0, :, 0:1], (SUBLANES, LANES))
                tops.append(line_sum(jnp.where(picker, top, 0.0)))
        lines = lines_of(tops, sums, sources)
        for i, line in enumerate(lines):
            pay_ref[i : i + 1, :] = pay_in[i : i + 1, :] + line
        pay_ref[len(lines) :, :] = pay_in[len(lines) :, :]

    @pl.when(even)
    def _():
        one_end(even_end)

    @pl.when(jnp.logical_not(even))
    def _():
        one_end(1 - even_end)


def combine_kernel(places, halo, weight_ref, *refs):
    n_parts, n_pay = ITERS + 1, len(places)
    packed = tree_sum([refs[i][...] for i in places])
    part_refs = refs[n_pay : n_pay + n_parts]
    edge_refs = refs[n_pay + n_parts : n_pay + 2 * n_parts]
    out_refs = refs[n_pay + 2 * n_parts :]
    sources, _, total, _ = part_refs[0].shape
    rows = total - 2 * halo
    per = (out_refs[0].shape[0] - SUBLANES) // (rows * sources)
    first = n_parts * sources
    totals = jnp.sum(packed[first : first + 2 * ITERS * sources], axis=1, keepdims=True)
    poly = step_polynomial([totals[n * sources : (n + 1) * sources] for n in range(2 * ITERS)])
    weight = weight_ref[...]
    scale = [[weight] + [weight * p[s : s + 1] for p in poly] for s in range(sources)]
    read = [
        sum(scale[s][i] * packed[i * sources + s : i * sources + s + 1] for i in range(n_parts))
        for s in range(sources)
    ]
    split = len(out_refs) > 1
    wave = lax.axis_index("wave") if split else 0
    inner = slice(SUBLANES, total - SUBLANES)
    for mask, out_ref in enumerate(out_refs):
        block = wave ^ mask if split else 0
        for s in range(sources):
            for k in range(per):
                c = block * per + k
                middle = sum(scale[s][i] * part_refs[i][s, c, inner] for i in range(n_parts))
                top, end = (
                    sum(scale[s][i] * edge_refs[i][e, s, c] for i in range(n_parts)) for e in (0, 1)
                )
                value = jnp.concatenate([top[halo:], middle, end[: SUBLANES - halo]], axis=0)
                out_ref[pl.ds((s * per + k) * rows, rows), :] = value
        end_row = sources * per * rows
        out_ref[end_row:, :] = jnp.zeros((SUBLANES, LANES), jnp.float32)
        for s in range(sources):
            out_ref[end_row + s : end_row + s + 1, :] = read[s]


def sum_kernel(places, *refs):
    part_refs, (field_ref, read_ref) = [refs[i] for i in places], refs[-2:]
    sources, rows, share = field_ref.shape
    electrodes = read_ref.shape[1]
    per = share // LANES
    for s in range(sources):
        for k in range(per):
            at = pl.ds((s * per + k) * rows, rows)
            field_ref[s, :, cols(k)] = tree_sum([r[at, :] for r in part_refs])
    last = tree_sum([r[sources * per * rows :, :] for r in part_refs])
    read_ref[...] = last[:sources, :electrodes]


def shards(
    warm_start,
    class_map,
    conductivities,
    wavenumbers,
    weights,
    source_row,
    source_col,
    electrode_row,
):
    rows, depth = class_map.shape
    sources = warm_start.shape[1]
    electrodes = electrode_row.shape[0]
    tiles, waves = lax.axis_size("tile"), lax.axis_size("wave")
    wave = lax.axis_index("wave")
    halo = ITERS + 1
    field = warm_start[0]
    f32 = jnp.float32
    n_class = conductivities.shape[0]
    rim = jax.ShapeDtypeStruct((sources + 1, halo, depth), f32)
    raw = [
        field,
        class_map,
        conductivities,
        source_row,
        source_col,
    ]
    far, near, params, spots = pl.pallas_call(
        edge_kernel,
        out_shape=[
            rim,
            rim,
            jax.ShapeDtypeStruct((n_class, SUBLANES, LANES), f32),
            jax.ShapeDtypeStruct((2 * sources, SUBLANES, LANES), jnp.int32),
        ],
        in_specs=[pl.BlockSpec(memory_space=pltpu.HBM)] * len(raw),
        out_specs=[VMEM] * 4,
        scratch_shapes=[
            pltpu.VMEM((2, sources, SUBLANES, depth), f32),
            pltpu.VMEM((2, SUBLANES, depth), jnp.int32),
            *[pltpu.SMEM(a.shape, a.dtype) for a in raw[2:]],
            pltpu.SemaphoreType.DMA((len(raw) + 2,)),
        ],
        compiler_params=PARAMS,
    )(*[pltpu.with_memory_space_constraint(a, pltpu.HBM) for a in raw])
    ring = [(i, (i + 1) % tiles) for i in range(1, tiles, 2)]
    far = lax.ppermute(far, "tile", ring + [(j, i) for i, j in ring])
    near = swap(near, "tile", 1, tiles)
    total, chunks = rows + 2 * halo, depth // LANES
    picks = jnp.pad(electrode_row, (0, LANES - electrodes), constant_values=-1)[None]
    wide = jax.ShapeDtypeStruct((sources, chunks, total, LANES), f32)
    flat = jax.ShapeDtypeStruct((chunks, total, LANES), f32)
    n_lines = sources * (3 * ITERS + 1)
    pay = jax.ShapeDtypeStruct((-(-n_lines // SUBLANES) * SUBLANES, LANES), f32)
    ends = jax.ShapeDtypeStruct((2, sources, chunks, SUBLANES, LANES), f32)
    tile = jax.ShapeDtypeStruct((SUBLANES, LANES), f32)
    inside = vmem_call(
        inner_kernel,
        [wide] * (ITERS + 1) + [pay, flat, flat, flat, flat, ends, tile],
        [field, class_map, params, wavenumbers[None], spots, picks],
        [pltpu.VMEM((chunks, total, LANES), f32)] * 6,
    )
    ready = list(inside)
    scratch = [pltpu.VMEM((chunks, SUBLANES, LANES), f32)] * 8
    outside = vmem_call(
        functools.partial(outer_kernel, 1, False),
        [ends] * (ITERS + 1) + [pay],
        [near, params, picks, *ready],
        scratch,
    )
    ready[ITERS + 1] = outside[-1]
    inputs = [far, params, picks, *ready, *outside[:-1]]
    held = len(inputs) - (ITERS + 1)
    outside = vmem_call(
        functools.partial(outer_kernel, 0, True),
        [ends] * (ITERS + 1) + [pay],
        inputs,
        scratch,
        {held + i: i for i in range(ITERS + 1)},
    )
    packed = tile_parts(outside[-1], "tile")
    packed, places = issued(packed, (0, *range(len(packed) - 1, 0, -1)))
    share = depth // waves
    split = share % LANES == 0
    width = share if split else depth
    n = sources * rows * width // LANES
    block = jax.ShapeDtypeStruct((n + SUBLANES, LANES), f32)
    pieces = vmem_call(
        functools.partial(combine_kernel, places, halo),
        [block] * (waves if split else 1),
        [weights[None], *packed, *inside[: ITERS + 1], *outside[: ITERS + 1]],
    )
    if not split:
        read = pieces[0][n : n + sources, :electrodes].reshape(-1, share)
        whole = pieces[0][:n].reshape(sources, chunks, rows, LANES)
        whole = whole.transpose(0, 2, 1, 3).reshape(sources * rows, depth)
        pieces = [
            jnp.concatenate(
                [lax.dynamic_slice_in_dim(whole, (wave ^ mask) * share, share, 1), read]
            )
            for mask in range(waves)
        ]
    pieces = [pieces[0]] + [swap(pieces[m], "wave", m, waves) for m in range(1, waves)]
    if not split:
        final = tree_sum(pieces)
        return (
            final[: sources * rows].reshape(sources, rows, share),
            final[sources * rows :].reshape(sources, electrodes),
        )
    pieces, places = issued(pieces, (0, waves - 1, *range(1, waves - 1)))
    return tuple(
        vmem_call(
            functools.partial(sum_kernel, places),
            [
                jax.ShapeDtypeStruct((sources, rows, share), f32),
                jax.ShapeDtypeStruct((sources, electrodes), f32),
            ],
            pieces,
        )
    )


def solution(mesh):
    return jax.shard_map(
        shards,
        mesh=mesh,
        in_specs=(
            P("wave", None, "tile", None),
            P("tile", None),
            P(),
            P("wave"),
            P("wave"),
            P(),
            P(),
            P(),
        ),
        out_specs=(P(None, "tile", "wave"), P()),
        check_vma=False,
    )
```

```python
import functools

import jax
import jax.numpy as jnp
from jax import lax
from jax.experimental import pallas as pl
from jax.experimental.pallas import tpu as pltpu
from jax.sharding import PartitionSpec as P


ITERS = 3
SOURCE_STRENGTH = 50.0
TINY = 1e-30
LEAST_KEPT = 3e-4
LANES = 128
SUBLANES = 8


def harmonic(left_val, right_val):
    return 2.0 * left_val * right_val / jnp.maximum(left_val + right_val, TINY)


def safe_div(num, den):
    return jnp.where(den > 0.0, num / jnp.where(den > 0.0, den, 1.0), 0.0)


def tree_sum(values):
    values = list(values)
    while len(values) > 1:
        values = [values[i] + values[i + 1] for i in range(0, len(values), 2)]
    return values[0]


def swap(value, axis, mask, size):
    return lax.ppermute(value, axis, [(i, i ^ mask) for i in range(size)])


def tile_parts(value, axis):
    size = lax.axis_size(axis)
    parts = [value]
    bit = 1
    while bit < size:
        value = tree_sum(parts)
        masks = [bit]
        if bit > 1 and bit * 2 < size:
            masks.append(bit * 2)
        offsets = [0]
        for mask in masks:
            offsets += [o ^ mask for o in offsets]
        parts = [value] + [swap(value, axis, o, size) for o in offsets[1:]]
        bit = masks[-1] * 2
    return parts


def issued(values, order):
    return [values[i] for i in order], [order.index(i) for i in range(len(values))]


def step_polynomial(moments):
    trusted = []

    def product(poly, term):
        value = size = 0.0
        for i, a in enumerate(poly):
            for j, b in enumerate(poly):
                part, bound = term(i + j)
                value = value + a * b * part
                size = size + jnp.abs(a * b) * bound
        trusted.append(value > LEAST_KEPT * size)
        return value

    def inner(n):
        return moments[n], jnp.abs(moments[n])

    def energy(n):
        return moments[n] - moments[n + 1], jnp.abs(moments[n]) + jnp.abs(moments[n + 1])

    one = jnp.ones_like(moments[0])
    zero = jnp.zeros_like(moments[0])
    res, way, total = [one], [one], [zero] * ITERS
    gamma = moments[0]
    for iteration in range(ITERS):
        alpha = safe_div(gamma, product(way, energy))
        total = [t + alpha * (way[i] if i < len(way) else zero) for i, t in enumerate(total)]
        if iteration + 1 < ITERS:
            longer = way + [zero]
            shifted = [zero] + way
            res = [r - alpha * (a - b) for r, a, b in zip(res + [zero], longer, shifted)]
            gamma_next = jnp.maximum(product(res, inner), 0.0)
            ratio = safe_div(gamma_next, gamma)
            way = [r + ratio * a for r, a in zip(res, longer)]
            gamma = gamma_next
    kept = trusted[0]
    for other in trusted[1:]:
        kept = kept & other
    return total, jnp.where(kept, 0.0, 1.0)


VMEM = pl.BlockSpec(memory_space=pltpu.VMEM)
PARAMS = pltpu.CompilerParams(vmem_limit_bytes=16 << 20)


def vmem_call(kernel, out_shape, inputs, scratch=(), aliases=()):
    return pl.pallas_call(
        kernel,
        out_shape=out_shape,
        in_specs=[VMEM] * len(inputs),
        out_specs=jax.tree.map(lambda _: VMEM, out_shape),
        scratch_shapes=list(scratch),
        input_output_aliases=dict(aliases),
        compiler_params=PARAMS,
    )(*inputs)


def cols(c):
    return slice(c * LANES, (c + 1) * LANES)


def add(sums, key, value):
    sums[key] = sums[key] + value if key in sums else value


def edge_kernel(field_hbm, class_hbm, cond_hbm, row_hbm, col_hbm, *refs):
    far_ref, near_ref, par_ref, spot_ref = refs[:4]
    field_ref, class_ref, cond_ref, row_ref, col_ref, sems = refs[4:]
    sources, rows, _ = field_hbm.shape
    halo = far_ref.shape[1]
    pairs = []
    for i, at in enumerate((0, rows - SUBLANES)):
        pairs.append((field_hbm.at[:, pl.ds(at, SUBLANES)], field_ref.at[i]))
        pairs.append((class_hbm.at[pl.ds(at, SUBLANES)], class_ref.at[i]))
    pairs += [
        (cond_hbm, cond_ref),
        (row_hbm, row_ref),
        (col_hbm, col_ref),
    ]
    copies = [
        pltpu.make_async_copy(start, end, sems.at[i]) for i, (start, end) in enumerate(pairs)
    ]
    for copy in copies:
        copy.start()
    for copy in copies:
        copy.wait()
    even = lax.axis_index("tile") % 2 == 0
    spare = SUBLANES - halo
    for s in range(sources):
        first, last = field_ref[0, s, :halo], field_ref[1, s, spare:]
        far_ref[s] = jnp.where(even, first, last)
        near_ref[s] = jnp.where(even, last, first)
    first = class_ref[0, :halo].astype(jnp.float32) + 1.0
    last = class_ref[1, spare:].astype(jnp.float32) + 1.0
    far_ref[sources] = jnp.where(even, first, last)
    near_ref[sources] = jnp.where(even, last, first)
    tile = (SUBLANES, LANES)
    n_class = cond_ref.shape[0]
    for i in range(n_class):
        par_ref[i] = jnp.full(tile, cond_ref[i], jnp.float32)
    for s in range(sources):
        spot_ref[s] = jnp.full(tile, row_ref[s], jnp.int32)
        spot_ref[sources + s] = jnp.full(tile, col_ref[s], jnp.int32)


def neighbours(get, chunks, lane):
    here = get(0)
    last = LANES - 1
    from_right = pltpu.roll(here, last, 1)
    before = None
    for c in range(chunks):
        from_left = pltpu.roll(here, 1, 1)
        left = jnp.where(lane == 0, before, from_left) if c else from_left
        right = from_right
        if c + 1 < chunks:
            following = get(c + 1)
            from_next = pltpu.roll(following, last, 1)
            right = jnp.where(lane == last, from_next, from_right)
        yield c, here, left, right
        before = from_left
        if c + 1 < chunks:
            here, from_right = following, from_next


def conductivity(ids, values):
    sigma = jnp.zeros(ids.shape, jnp.float32)
    for i, value in enumerate(values):
        sigma = jnp.where(ids == i + 1.0, value, sigma)
    return sigma


def tall(tile, rows):
    return jnp.concatenate([tile] * (rows // SUBLANES), axis=0)


def line_sum(value):
    return jnp.sum(value, axis=0, keepdims=True)


def lines_of(tops, sums, sources):
    lines = list(tops)
    for n in range(2 * ITERS):
        for s in range(sources):
            lines.append(line_sum(sums[n, s]))
    return lines


def inner_kernel(field_ref, class_ref, par_ref, wave_ref, spot_ref, pick_ref, *refs):
    x_ref, *basis_refs = refs[: 1 + ITERS]
    pay_ref, sig_ref, side_ref, above_ref, below_ref, hit_ref, square_ref = refs[1 + ITERS : 8 + ITERS]
    up_ref, down_ref, west_ref, east_ref, diag_ref, inv_ref = refs[8 + ITERS :]
    sources, rows, _ = field_ref.shape
    chunks, total = x_ref.shape[1:3]
    n_class = par_ref.shape[0]
    halo = (total - rows) // 2
    lane = lax.broadcasted_iota(jnp.int32, (total, LANES), 1)
    row = lax.broadcasted_iota(jnp.int32, (total, LANES), 0)
    rows_at = row + (lax.axis_index("tile") * rows - halo)
    blank = jnp.zeros((halo, LANES), jnp.float32)
    inner = slice(SUBLANES, total - SUBLANES)
    wave = jnp.broadcast_to(wave_ref[...], (SUBLANES, LANES))
    square_ref[...] = wave * wave
    square = tall(square_ref[...], total)
    values = [tall(par_ref[i], rows) for i in range(n_class)]

    def widened(value):
        return jnp.concatenate([blank, value, blank], axis=0)

    for c in range(chunks):
        ids = class_ref[:, cols(c)].astype(jnp.float32) + 1.0
        sig_ref[c] = widened(conductivity(ids, values))
        for s in range(sources):
            x_ref[s, c] = widened(field_ref[s, :, cols(c)])
    for c, sigma, left, _ in neighbours(lambda c: sig_ref[c], chunks, lane):
        face = harmonic(left, sigma)
        side_ref[c] = jnp.where(lane == 0, 0.0, face) if c == 0 else face
        up = harmonic(pltpu.roll(sigma, 1, 0), sigma)
        above_ref[c] = up
        below_ref[c] = pltpu.roll(up, total - 1, 0)
    at_source = [rows_at == tall(spot_ref[s], total) for s in range(sources)]
    for c, west, _, east in neighbours(lambda c: side_ref[c], chunks, lane):
        up, down = above_ref[c], below_ref[c]
        sigma = sig_ref[c]
        diag = up + down + west + square * sigma
        if c == chunks - 1:
            bottom = lane == LANES - 1
            diag = diag + jnp.where(bottom, sigma, east)
            east = jnp.where(bottom, 0.0, east)
        else:
            diag = diag + east
        inverse = 1.0 / jnp.maximum(diag, TINY)
        diag_ref[c] = diag
        inv_ref[c] = inverse
        up_ref[c] = up * inverse
        down_ref[c] = down * inverse
        west_ref[c] = west * inverse
        east_ref[c] = east * inverse

    def spread(c, here, left, right):
        return (
            up_ref[c] * pltpu.roll(here, 1, 0)
            + down_ref[c] * pltpu.roll(here, total - 1, 0)
            + west_ref[c] * left
            + east_ref[c] * right
        )

    def fold(value):
        return sum(value[r : r + SUBLANES] for r in range(0, value.shape[0], SUBLANES))

    sums = {}
    for s in range(sources):
        column = tall(spot_ref[sources + s], total)
        for c, here, left, right in neighbours(lambda c: x_ref[s, c], chunks, lane):
            charge = jnp.where(
                at_source[s] & (lane + c * LANES == column), SOURCE_STRENGTH, 0.0
            )
            hit_ref[0, s, c] = charge[:SUBLANES]
            hit_ref[1, s, c] = charge[total - SUBLANES :]
            new = charge * inv_ref[c] - (here - spread(c, here, left, right))
            basis_refs[0][s, c] = new
            own = new[inner]
            add(sums, (0, s), fold(diag_ref[c, inner] * own * own))
    for i in range(ITERS):
        for s in range(sources):
            for c, here, left, right in neighbours(lambda c: basis_refs[i][s, c], chunks, lane):
                new = spread(c, here, left, right)
                own = new[inner]
                weighted = diag_ref[c, inner] * own
                add(sums, (2 * i + 1, s), fold(weighted * here[inner]))
                if i + 1 < ITERS:
                    basis_refs[i + 1][s, c] = new
                    add(sums, (2 * i + 2, s), fold(weighted * own))
    picker = rows_at[inner] == pick_ref[...]
    tops = []
    for ref in (x_ref, *basis_refs):
        for s in range(sources):
            top = jnp.broadcast_to(ref[s, 0, inner, 0:1], (total - 2 * SUBLANES, LANES))
            tops.append(line_sum(fold(jnp.where(picker, top, 0.0))))
    pay_ref[...] = jnp.zeros(pay_ref.shape, jnp.float32)
    for i, line in enumerate(lines_of(tops, sums, sources)):
        pay_ref[i : i + 1, :] = line


def outer_kernel(even_end, wraps, came_ref, par_ref, pick_ref, *refs):
    x_in, *basis_in = refs[: 1 + ITERS]
    pay_in, sig_in, side_in, above_in, below_in, hit_in, square_in = refs[1 + ITERS : 8 + ITERS]
    outs = refs[-(10 + ITERS) :]
    x_out, *basis_outs = outs[: 1 + ITERS]
    pay_ref = outs[1 + ITERS]
    sigma_ref, west_raw, up_ref, down_ref, west_ref, east_ref, diag_ref, inv_ref = outs[2 + ITERS :]
    sources, chunks, total, _ = x_in.shape
    halo = came_ref.shape[1]
    rows = total - 2 * halo
    lane = lax.broadcasted_iota(jnp.int32, (SUBLANES, LANES), 1)
    row = lax.broadcasted_iota(jnp.int32, (SUBLANES, LANES), 0)
    tile = lax.axis_index("tile")
    even = tile % 2 == 0
    square = square_in[...]
    values = [par_ref[i] for i in range(par_ref.shape[0])]
    upper = row < halo
    last = total - SUBLANES
    inside = (tile > 0) & (tile < lax.axis_size("tile") - 1)

    def came_in(index, c):
        value = came_ref[index, :, cols(c)]
        if wraps:
            value = jnp.where(inside, value, 0.0)
        return jnp.concatenate([value, value], axis=0)

    def one_end(e):
        at = last if e else 0
        tile_at = slice(at, at + SUBLANES)
        own = upper if e else jnp.logical_not(upper)
        x_ref, *basis_refs = [r.at[e] for r in (x_out, *basis_outs)]

        def set_in(new, kept):
            return jnp.where(own, kept[tile_at], new)

        for c in range(chunks):
            sigma_ref[c] = conductivity(came_in(sources, c), values)
            for s in range(sources):
                x_ref[s, c] = set_in(came_in(s, c), x_in.at[s, c])
        for c, fresh, left, _ in neighbours(lambda c: sigma_ref[c], chunks, lane):
            face = harmonic(left, fresh)
            face = jnp.where(lane == 0, 0.0, face) if c == 0 else face
            west_raw[c] = set_in(face, side_in.at[c])
        for c, west, _, east in neighbours(lambda c: west_raw[c], chunks, lane):
            sigma = set_in(sigma_ref[c], sig_in.at[c])
            face = harmonic(pltpu.roll(sigma, 1 if e else SUBLANES - 1, 0), sigma)
            if e:
                up = set_in(face, above_in.at[c])
                down = pltpu.roll(up, SUBLANES - 1, 0)
            else:
                down = set_in(face, below_in.at[c])
                up = pltpu.roll(down, 1, 0)
            diag = up + down + west + square * sigma
            if c == chunks - 1:
                bottom = lane == LANES - 1
                diag = diag + jnp.where(bottom, sigma, east)
                east = jnp.where(bottom, 0.0, east)
            else:
                diag = diag + east
            inverse = 1.0 / jnp.maximum(diag, TINY)
            diag_ref[c] = jnp.where(own, diag, 0.0)
            inv_ref[c] = inverse
            up_ref[c] = up * inverse
            down_ref[c] = down * inverse
            west_ref[c] = west * inverse
            east_ref[c] = east * inverse

        def spread(whole, s, c, here, left, right):
            above = pltpu.roll(here, 1, 0)
            below = pltpu.roll(here, SUBLANES - 1, 0)
            if e:
                above = jnp.where(row == 0, whole[s, c, last - 1 : last], above)
            else:
                below = jnp.where(
                    row == SUBLANES - 1, whole[s, c, SUBLANES : SUBLANES + 1], below
                )
            return (
                up_ref[c] * above
                + down_ref[c] * below
                + west_ref[c] * left
                + east_ref[c] * right
            )

        sums = {}
        for s in range(sources):
            for c, here, left, right in neighbours(lambda c: x_ref[s, c], chunks, lane):
                new = hit_in[e, s, c] * inv_ref[c] - (here - spread(x_in, s, c, here, left, right))
                basis_refs[0][s, c] = new
                add(sums, (0, s), diag_ref[c] * new * new)
        for i in range(ITERS):
            for s in range(sources):
                for c, here, left, right in neighbours(
                    lambda c: basis_refs[i][s, c], chunks, lane
                ):
                    new = spread(basis_in[i], s, c, here, left, right)
                    weighted = diag_ref[c] * new
                    add(sums, (2 * i + 1, s), weighted * here)
                    if i + 1 < ITERS:
                        basis_refs[i + 1][s, c] = new
                        add(sums, (2 * i + 2, s), weighted * new)
        picker = own & (row + (tile * rows - halo + at) == pick_ref[...])
        tops = []
        for ref in (x_ref, *basis_refs):
            for s in range(sources):
                top = jnp.broadcast_to(ref[s, 0, :, 0:1], (SUBLANES, LANES))
                tops.append(line_sum(jnp.where(picker, top, 0.0)))
        lines = lines_of(tops, sums, sources)
        for i, line in enumerate(lines):
            pay_ref[i : i + 1, :] = pay_in[i : i + 1, :] + line
        pay_ref[len(lines) :, :] = pay_in[len(lines) :, :]

    @pl.when(even)
    def _():
        one_end(even_end)

    @pl.when(jnp.logical_not(even))
    def _():
        one_end(1 - even_end)


def combine_kernel(places, halo, weight_ref, *refs):
    n_parts, n_pay = ITERS + 1, len(places)
    packed = tree_sum([refs[i][...] for i in places])
    part_refs = refs[n_pay : n_pay + n_parts]
    edge_refs = refs[n_pay + n_parts : n_pay + 2 * n_parts]
    out_refs = refs[n_pay + 2 * n_parts :]
    sources, _, total, _ = part_refs[0].shape
    rows = total - 2 * halo
    per = (out_refs[0].shape[0] - SUBLANES) // (rows * sources)
    first = n_parts * sources
    totals = jnp.sum(packed[first : first + 2 * ITERS * sources], axis=1, keepdims=True)
    poly, lost = step_polynomial(
        [totals[n * sources : (n + 1) * sources] for n in range(2 * ITERS)]
    )
    lost = jnp.broadcast_to(jnp.max(lost, axis=0, keepdims=True), (1, LANES))
    weight = weight_ref[...]
    scale = [[weight] + [weight * p[s : s + 1] for p in poly] for s in range(sources)]
    read = [
        sum(scale[s][i] * packed[i * sources + s : i * sources + s + 1] for i in range(n_parts))
        for s in range(sources)
    ]
    split = len(out_refs) > 1
    wave = lax.axis_index("wave") if split else 0
    inner = slice(SUBLANES, total - SUBLANES)
    for mask, out_ref in enumerate(out_refs):
        block = wave ^ mask if split else 0
        for s in range(sources):
            for k in range(per):
                c = block * per + k
                middle = sum(scale[s][i] * part_refs[i][s, c, inner] for i in range(n_parts))
                top, end = (
                    sum(scale[s][i] * edge_refs[i][e, s, c] for i in range(n_parts)) for e in (0, 1)
                )
                value = jnp.concatenate([top[halo:], middle, end[: SUBLANES - halo]], axis=0)
                out_ref[pl.ds((s * per + k) * rows, rows), :] = value
        end_row = sources * per * rows
        out_ref[end_row:, :] = jnp.zeros((SUBLANES, LANES), jnp.float32)
        for s in range(sources):
            out_ref[end_row + s : end_row + s + 1, :] = read[s]
        out_ref[end_row + sources : end_row + sources + 1, :] = lost


def sum_kernel(places, *refs):
    part_refs, (field_ref, read_ref) = [refs[i] for i in places], refs[-2:]
    sources, rows, share = field_ref.shape
    electrodes = read_ref.shape[1]
    per = share // LANES
    for s in range(sources):
        for k in range(per):
            at = pl.ds((s * per + k) * rows, rows)
            field_ref[s, :, cols(k)] = tree_sum([r[at, :] for r in part_refs])
    last = tree_sum([r[sources * per * rows :, :] for r in part_refs])
    read_ref[...] = last[:sources, :electrodes]


def careful(
    warm_start,
    class_map,
    conductivities,
    wavenumbers,
    weights,
    source_row,
    source_col,
    electrode_row,
):
    rows, depth = class_map.shape
    tiles, waves = lax.axis_size("tile"), lax.axis_size("wave")
    tile, wave = lax.axis_index("tile"), lax.axis_index("wave")

    def extended(shard, dim):
        up = [(i, i + 1) for i in range(tiles - 1)]
        down = [(j, i) for i, j in up]
        last = lax.slice_in_dim(shard, rows - 1, rows, axis=dim)
        initial = lax.slice_in_dim(shard, 0, 1, axis=dim)
        before = lax.ppermute(last, "tile", up)
        after = lax.ppermute(initial, "tile", down)
        return jnp.concatenate([before, shard, after], axis=dim)

    class_ids = jnp.arange(conductivities.shape[0], dtype=jnp.int32)
    sigma = jnp.sum(
        jnp.where(class_map[None] == class_ids[:, None, None], conductivities[:, None, None], 0.0),
        axis=0,
    )
    sigma_rim = extended(sigma, 0)
    face_row = harmonic(sigma_rim[:-1], sigma_rim[1:])
    face_up = face_row[:-1]
    face_down = face_row[1:]
    col_inner = harmonic(sigma[:, :-1], sigma[:, 1:])
    face_left = jnp.concatenate([jnp.zeros((rows, 1), jnp.float32), col_inner], axis=1)
    face_right = jnp.concatenate([col_inner, sigma[:, -1:]], axis=1)
    wave_num = wavenumbers[0]
    diag = face_up + face_down + face_left + face_right + wave_num * wave_num * sigma
    global_row = tile * rows + jnp.arange(rows, dtype=jnp.int32)
    col_ids = jnp.arange(depth, dtype=jnp.int32)
    hits = (global_row[None, :, None] == source_row[:, None, None]) & (
        col_ids[None, None, :] == source_col[:, None, None]
    )

    def operate(values):
        row_padded = extended(values, 1)
        col_padded = jnp.pad(values, ((0, 0), (0, 0), (1, 1)))
        return (
            diag * values
            - face_up * row_padded[:, :-2]
            - face_down * row_padded[:, 2:]
            - face_left * col_padded[:, :, :-2]
            - face_right * col_padded[:, :, 2:]
        )

    def inner(first, second):
        return lax.psum(jnp.sum(first * second, axis=(1, 2)), "tile")[:, None, None]

    field = warm_start[0]
    residual = SOURCE_STRENGTH * hits.astype(jnp.float32) - operate(field)
    scaled = residual / diag
    direction = scaled
    gamma = inner(residual, scaled)
    for iteration in range(ITERS):
        image = operate(direction)
        step_size = gamma / inner(direction, image)
        field = field + step_size * direction
        if iteration + 1 < ITERS:
            residual = residual - step_size * image
            scaled = residual / diag
            gamma_next = inner(residual, scaled)
            direction = scaled + (gamma_next / gamma) * direction
            gamma = gamma_next
    weighted = weights[0] * field
    picker = global_row[:, None] == electrode_row[None, :]
    local_read = jnp.sum(jnp.where(picker, weighted[:, :, 0][:, :, None], 0.0), axis=1)
    readings = lax.psum(local_read, ("wave", "tile"))
    share = depth // waves
    blocks = [
        lax.dynamic_slice_in_dim(weighted, (wave ^ mask) * share, share, 2)
        for mask in range(waves)
    ]
    blocks = [blocks[0]] + [swap(blocks[m], "wave", m, waves) for m in range(1, waves)]
    return tree_sum(blocks), readings


def shards(
    warm_start,
    class_map,
    conductivities,
    wavenumbers,
    weights,
    source_row,
    source_col,
    electrode_row,
):
    rows, depth = class_map.shape
    sources = warm_start.shape[1]
    electrodes = electrode_row.shape[0]
    tiles, waves = lax.axis_size("tile"), lax.axis_size("wave")
    wave = lax.axis_index("wave")
    halo = ITERS + 1
    field = warm_start[0]
    f32 = jnp.float32
    n_class = conductivities.shape[0]
    rim = jax.ShapeDtypeStruct((sources + 1, halo, depth), f32)
    raw = [
        field,
        class_map,
        conductivities,
        source_row,
        source_col,
    ]
    far, near, params, spots = pl.pallas_call(
        edge_kernel,
        out_shape=[
            rim,
            rim,
            jax.ShapeDtypeStruct((n_class, SUBLANES, LANES), f32),
            jax.ShapeDtypeStruct((2 * sources, SUBLANES, LANES), jnp.int32),
        ],
        in_specs=[pl.BlockSpec(memory_space=pltpu.HBM)] * len(raw),
        out_specs=[VMEM] * 4,
        scratch_shapes=[
            pltpu.VMEM((2, sources, SUBLANES, depth), f32),
            pltpu.VMEM((2, SUBLANES, depth), jnp.int32),
            *[pltpu.SMEM(a.shape, a.dtype) for a in raw[2:]],
            pltpu.SemaphoreType.DMA((len(raw) + 2,)),
        ],
        compiler_params=PARAMS,
    )(*[pltpu.with_memory_space_constraint(a, pltpu.HBM) for a in raw])
    ring = [(i, (i + 1) % tiles) for i in range(1, tiles, 2)]
    far = lax.ppermute(far, "tile", ring + [(j, i) for i, j in ring])
    near = swap(near, "tile", 1, tiles)
    total, chunks = rows + 2 * halo, depth // LANES
    picks = jnp.pad(electrode_row, (0, LANES - electrodes), constant_values=-1)[None]
    wide = jax.ShapeDtypeStruct((sources, chunks, total, LANES), f32)
    flat = jax.ShapeDtypeStruct((chunks, total, LANES), f32)
    n_lines = sources * (3 * ITERS + 1)
    pay = jax.ShapeDtypeStruct((-(-n_lines // SUBLANES) * SUBLANES, LANES), f32)
    ends = jax.ShapeDtypeStruct((2, sources, chunks, SUBLANES, LANES), f32)
    tile = jax.ShapeDtypeStruct((SUBLANES, LANES), f32)
    inside = vmem_call(
        inner_kernel,
        [wide] * (ITERS + 1) + [pay, flat, flat, flat, flat, ends, tile],
        [field, class_map, params, wavenumbers[None], spots, picks],
        [pltpu.VMEM((chunks, total, LANES), f32)] * 6,
    )
    ready = list(inside)
    scratch = [pltpu.VMEM((chunks, SUBLANES, LANES), f32)] * 8
    outside = vmem_call(
        functools.partial(outer_kernel, 1, False),
        [ends] * (ITERS + 1) + [pay],
        [near, params, picks, *ready],
        scratch,
    )
    ready[ITERS + 1] = outside[-1]
    inputs = [far, params, picks, *ready, *outside[:-1]]
    held = len(inputs) - (ITERS + 1)
    outside = vmem_call(
        functools.partial(outer_kernel, 0, True),
        [ends] * (ITERS + 1) + [pay],
        inputs,
        scratch,
        {held + i: i for i in range(ITERS + 1)},
    )
    packed = tile_parts(outside[-1], "tile")
    packed, places = issued(packed, (0, *range(len(packed) - 1, 0, -1)))
    share = depth // waves
    split = share % LANES == 0
    width = share if split else depth
    n = sources * rows * width // LANES
    block = jax.ShapeDtypeStruct((n + SUBLANES, LANES), f32)
    pieces = vmem_call(
        functools.partial(combine_kernel, places, halo),
        [block] * (waves if split else 1),
        [weights[None], *packed, *inside[: ITERS + 1], *outside[: ITERS + 1]],
    )
    if not split:
        read = pieces[0][n : n + sources, :electrodes].reshape(-1, share)
        read = jnp.concatenate([read, pieces[0][n + sources :][:1, :share]])
        whole = pieces[0][:n].reshape(sources, chunks, rows, LANES)
        whole = whole.transpose(0, 2, 1, 3).reshape(sources * rows, depth)
        pieces = [
            jnp.concatenate(
                [lax.dynamic_slice_in_dim(whole, (wave ^ mask) * share, share, 1), read]
            )
            for mask in range(waves)
        ]
    pieces = [pieces[0]] + [swap(pieces[m], "wave", m, waves) for m in range(1, waves)]
    lost = tree_sum([p[-1, 0] if not split else p[n + sources, 0] for p in pieces]) > 0.0
    given = (
        warm_start,
        class_map,
        conductivities,
        wavenumbers,
        weights,
        source_row,
        source_col,
        electrode_row,
    )

    def usual():
        if not split:
            final = tree_sum(pieces)[:-1]
            return (
                final[: sources * rows].reshape(sources, rows, share),
                final[sources * rows :].reshape(sources, electrodes),
            )
        parts, places = issued(pieces, (0, waves - 1, *range(1, waves - 1)))
        return tuple(
            vmem_call(
                functools.partial(sum_kernel, places),
                [
                    jax.ShapeDtypeStruct((sources, rows, share), f32),
                    jax.ShapeDtypeStruct((sources, electrodes), f32),
                ],
                parts,
            )
        )

    return lax.cond(lost, lambda: careful(*given), usual)


def solution(mesh):
    return jax.shard_map(
        shards,
        mesh=mesh,
        in_specs=(
            P("wave", None, "tile", None),
            P("tile", None),
            P(),
            P("wave"),
            P("wave"),
            P(),
            P(),
            P(),
        ),
        out_specs=(P(None, "tile", "wave"), P()),
        check_vma=False,
    )
```

```python
import functools

import jax
import jax.numpy as jnp
from jax import lax
from jax.experimental import pallas as pl
from jax.experimental.pallas import tpu as pltpu
from jax.sharding import PartitionSpec as P


ITERS = 3
SOURCE_STRENGTH = 50.0
TINY = 1e-30
LEAST_KEPT = 3e-4
LANES = 128
SUBLANES = 8


def harmonic(left_val, right_val):
    return 2.0 * left_val * right_val / jnp.maximum(left_val + right_val, TINY)


def safe_div(num, den):
    return jnp.where(den > 0.0, num / jnp.where(den > 0.0, den, 1.0), 0.0)


def tree_sum(values):
    values = list(values)
    while len(values) > 1:
        values = [values[i] + values[i + 1] for i in range(0, len(values), 2)]
    return values[0]


def swap(value, axis, mask, size):
    return lax.ppermute(value, axis, [(i, i ^ mask) for i in range(size)])


def tile_parts(value, axis):
    size = lax.axis_size(axis)
    parts = [value]
    bit = 1
    while bit < size:
        value = tree_sum(parts)
        masks = [bit]
        if bit > 1 and bit * 2 < size:
            masks.append(bit * 2)
        offsets = [0]
        for mask in masks:
            offsets += [o ^ mask for o in offsets]
        parts = [value] + [swap(value, axis, o, size) for o in offsets[1:]]
        bit = masks[-1] * 2
    return parts


def issued(values, order):
    return [values[i] for i in order], [order.index(i) for i in range(len(values))]


def step_polynomial(moments):
    trusted = []

    def product(poly, term):
        value = size = 0.0
        for i, a in enumerate(poly):
            for j, b in enumerate(poly):
                part, bound = term(i + j)
                value = value + a * b * part
                size = size + jnp.abs(a * b) * bound
        trusted.append(value > LEAST_KEPT * size)
        return value

    def inner(n):
        return moments[n], jnp.abs(moments[n])

    def energy(n):
        return moments[n] - moments[n + 1], jnp.abs(moments[n]) + jnp.abs(moments[n + 1])

    one = jnp.ones_like(moments[0])
    zero = jnp.zeros_like(moments[0])
    res, way, total = [one], [one], [zero] * ITERS
    gamma = moments[0]
    for iteration in range(ITERS):
        alpha = safe_div(gamma, product(way, energy))
        total = [t + alpha * (way[i] if i < len(way) else zero) for i, t in enumerate(total)]
        if iteration + 1 < ITERS:
            longer = way + [zero]
            shifted = [zero] + way
            res = [r - alpha * (a - b) for r, a, b in zip(res + [zero], longer, shifted)]
            gamma_next = jnp.maximum(product(res, inner), 0.0)
            ratio = safe_div(gamma_next, gamma)
            way = [r + ratio * a for r, a in zip(res, longer)]
            gamma = gamma_next
    kept = trusted[0]
    for other in trusted[1:]:
        kept = kept & other
    return total, jnp.where(kept, 0.0, 1.0)


VMEM = pl.BlockSpec(memory_space=pltpu.VMEM)
PARAMS = pltpu.CompilerParams(vmem_limit_bytes=16 << 20)


def vmem_call(kernel, out_shape, inputs, scratch=(), aliases=(), out_specs=None):
    return pl.pallas_call(
        kernel,
        out_shape=out_shape,
        in_specs=[VMEM] * len(inputs),
        out_specs=out_specs or jax.tree.map(lambda _: VMEM, out_shape),
        scratch_shapes=list(scratch),
        input_output_aliases=dict(aliases),
        compiler_params=PARAMS,
    )(*inputs)


def cols(c):
    return slice(c * LANES, (c + 1) * LANES)


def add(sums, key, value):
    sums[key] = sums[key] + value if key in sums else value


def edge_kernel(field_hbm, class_hbm, cond_hbm, row_hbm, col_hbm, *refs):
    far_ref, near_ref, par_ref, spot_ref = refs[:4]
    field_ref, class_ref, cond_ref, row_ref, col_ref, sems = refs[4:]
    sources, rows, _ = field_hbm.shape
    halo = far_ref.shape[1]
    pairs = []
    for i, at in enumerate((0, rows - SUBLANES)):
        pairs.append((field_hbm.at[:, pl.ds(at, SUBLANES)], field_ref.at[i]))
        pairs.append((class_hbm.at[pl.ds(at, SUBLANES)], class_ref.at[i]))
    pairs += [
        (cond_hbm, cond_ref),
        (row_hbm, row_ref),
        (col_hbm, col_ref),
    ]
    copies = [
        pltpu.make_async_copy(start, end, sems.at[i]) for i, (start, end) in enumerate(pairs)
    ]
    for copy in copies:
        copy.start()
    for copy in copies:
        copy.wait()
    even = lax.axis_index("tile") % 2 == 0
    spare = SUBLANES - halo
    for s in range(sources):
        first, last = field_ref[0, s, :halo], field_ref[1, s, spare:]
        far_ref[s] = jnp.where(even, first, last)
        near_ref[s] = jnp.where(even, last, first)
    first = class_ref[0, :halo].astype(jnp.float32) + 1.0
    last = class_ref[1, spare:].astype(jnp.float32) + 1.0
    far_ref[sources] = jnp.where(even, first, last)
    near_ref[sources] = jnp.where(even, last, first)
    tile = (SUBLANES, LANES)
    n_class = cond_ref.shape[0]
    for i in range(n_class):
        par_ref[i] = jnp.full(tile, cond_ref[i], jnp.float32)
    for s in range(sources):
        spot_ref[s] = jnp.full(tile, row_ref[s], jnp.int32)
        spot_ref[sources + s] = jnp.full(tile, col_ref[s], jnp.int32)


def neighbours(get, chunks, lane):
    here = get(0)
    last = LANES - 1
    from_right = pltpu.roll(here, last, 1)
    before = None
    for c in range(chunks):
        from_left = pltpu.roll(here, 1, 1)
        left = jnp.where(lane == 0, before, from_left) if c else from_left
        right = from_right
        if c + 1 < chunks:
            following = get(c + 1)
            from_next = pltpu.roll(following, last, 1)
            right = jnp.where(lane == last, from_next, from_right)
        yield c, here, left, right
        before = from_left
        if c + 1 < chunks:
            here, from_right = following, from_next


def conductivity(ids, values):
    sigma = jnp.zeros(ids.shape, jnp.float32)
    for i, value in enumerate(values):
        sigma = jnp.where(ids == i + 1.0, value, sigma)
    return sigma


def tall(tile, rows):
    return jnp.concatenate([tile] * (rows // SUBLANES), axis=0)


def line_sum(value):
    return jnp.sum(value, axis=0, keepdims=True)


def lines_of(tops, sums, sources):
    lines = list(tops)
    for n in range(2 * ITERS):
        for s in range(sources):
            lines.append(line_sum(sums[n, s]))
    return lines


def inner_kernel(field_ref, class_ref, par_ref, wave_ref, spot_ref, pick_ref, *refs):
    x_ref, *basis_refs = refs[: 1 + ITERS]
    pay_ref, sig_ref, side_ref, above_ref, below_ref, hit_ref, square_ref = refs[1 + ITERS : 8 + ITERS]
    up_ref, down_ref, west_ref, east_ref, diag_ref, inv_ref = refs[8 + ITERS :]
    sources, rows, _ = field_ref.shape
    chunks, total = x_ref.shape[1:3]
    n_class = par_ref.shape[0]
    halo = (total - rows) // 2
    lane = lax.broadcasted_iota(jnp.int32, (total, LANES), 1)
    row = lax.broadcasted_iota(jnp.int32, (total, LANES), 0)
    rows_at = row + (lax.axis_index("tile") * rows - halo)
    blank = jnp.zeros((halo, LANES), jnp.float32)
    inner = slice(SUBLANES, total - SUBLANES)
    wave = jnp.broadcast_to(wave_ref[...], (SUBLANES, LANES))
    square_ref[...] = wave * wave
    square = tall(square_ref[...], total)
    values = [tall(par_ref[i], rows) for i in range(n_class)]

    def widened(value):
        return jnp.concatenate([blank, value, blank], axis=0)

    for c in range(chunks):
        ids = class_ref[:, cols(c)].astype(jnp.float32) + 1.0
        sig_ref[c] = widened(conductivity(ids, values))
        for s in range(sources):
            x_ref[s, c] = widened(field_ref[s, :, cols(c)])
    for c, sigma, left, _ in neighbours(lambda c: sig_ref[c], chunks, lane):
        face = harmonic(left, sigma)
        side_ref[c] = jnp.where(lane == 0, 0.0, face) if c == 0 else face
        up = harmonic(pltpu.roll(sigma, 1, 0), sigma)
        above_ref[c] = up
        below_ref[c] = pltpu.roll(up, total - 1, 0)
    at_source = [rows_at == tall(spot_ref[s], total) for s in range(sources)]
    for c, west, _, east in neighbours(lambda c: side_ref[c], chunks, lane):
        up, down = above_ref[c], below_ref[c]
        sigma = sig_ref[c]
        diag = up + down + west + square * sigma
        if c == chunks - 1:
            bottom = lane == LANES - 1
            diag = diag + jnp.where(bottom, sigma, east)
            east = jnp.where(bottom, 0.0, east)
        else:
            diag = diag + east
        inverse = 1.0 / jnp.maximum(diag, TINY)
        diag_ref[c] = diag
        inv_ref[c] = inverse
        up_ref[c] = up * inverse
        down_ref[c] = down * inverse
        west_ref[c] = west * inverse
        east_ref[c] = east * inverse

    def spread(c, here, left, right):
        return (
            up_ref[c] * pltpu.roll(here, 1, 0)
            + down_ref[c] * pltpu.roll(here, total - 1, 0)
            + west_ref[c] * left
            + east_ref[c] * right
        )

    def fold(value):
        return sum(value[r : r + SUBLANES] for r in range(0, value.shape[0], SUBLANES))

    sums = {}
    for s in range(sources):
        column = tall(spot_ref[sources + s], total)
        for c, here, left, right in neighbours(lambda c: x_ref[s, c], chunks, lane):
            charge = jnp.where(
                at_source[s] & (lane + c * LANES == column), SOURCE_STRENGTH, 0.0
            )
            hit_ref[0, s, c] = charge[:SUBLANES]
            hit_ref[1, s, c] = charge[total - SUBLANES :]
            new = charge * inv_ref[c] - (here - spread(c, here, left, right))
            basis_refs[0][s, c] = new
            own = new[inner]
            add(sums, (0, s), fold(diag_ref[c, inner] * own * own))
    for i in range(ITERS):
        for s in range(sources):
            for c, here, left, right in neighbours(lambda c: basis_refs[i][s, c], chunks, lane):
                new = spread(c, here, left, right)
                own = new[inner]
                weighted = diag_ref[c, inner] * own
                add(sums, (2 * i + 1, s), fold(weighted * here[inner]))
                if i + 1 < ITERS:
                    basis_refs[i + 1][s, c] = new
                    add(sums, (2 * i + 2, s), fold(weighted * own))
    picker = rows_at[inner] == pick_ref[...]
    tops = []
    for ref in (x_ref, *basis_refs):
        for s in range(sources):
            top = jnp.broadcast_to(ref[s, 0, inner, 0:1], (total - 2 * SUBLANES, LANES))
            tops.append(line_sum(fold(jnp.where(picker, top, 0.0))))
    pay_ref[...] = jnp.zeros(pay_ref.shape, jnp.float32)
    for i, line in enumerate(lines_of(tops, sums, sources)):
        pay_ref[i : i + 1, :] = line


def outer_kernel(even_end, wraps, came_ref, par_ref, pick_ref, *refs):
    x_in, *basis_in = refs[: 1 + ITERS]
    pay_in, sig_in, side_in, above_in, below_in, hit_in, square_in = refs[1 + ITERS : 8 + ITERS]
    outs = refs[-(10 + ITERS) :]
    x_out, *basis_outs = outs[: 1 + ITERS]
    pay_ref = outs[1 + ITERS]
    sigma_ref, west_raw, up_ref, down_ref, west_ref, east_ref, diag_ref, inv_ref = outs[2 + ITERS :]
    sources, chunks, total, _ = x_in.shape
    halo = came_ref.shape[1]
    rows = total - 2 * halo
    lane = lax.broadcasted_iota(jnp.int32, (SUBLANES, LANES), 1)
    row = lax.broadcasted_iota(jnp.int32, (SUBLANES, LANES), 0)
    tile = lax.axis_index("tile")
    even = tile % 2 == 0
    square = square_in[...]
    values = [par_ref[i] for i in range(par_ref.shape[0])]
    upper = row < halo
    last = total - SUBLANES
    inside = (tile > 0) & (tile < lax.axis_size("tile") - 1)

    def came_in(index, c):
        value = came_ref[index, :, cols(c)]
        if wraps:
            value = jnp.where(inside, value, 0.0)
        return jnp.concatenate([value, value], axis=0)

    def one_end(e):
        at = last if e else 0
        tile_at = slice(at, at + SUBLANES)
        own = upper if e else jnp.logical_not(upper)
        x_ref, *basis_refs = [r.at[e] for r in (x_out, *basis_outs)]

        def set_in(new, kept):
            return jnp.where(own, kept[tile_at], new)

        for c in range(chunks):
            sigma_ref[c] = conductivity(came_in(sources, c), values)
            for s in range(sources):
                x_ref[s, c] = set_in(came_in(s, c), x_in.at[s, c])
        for c, fresh, left, _ in neighbours(lambda c: sigma_ref[c], chunks, lane):
            face = harmonic(left, fresh)
            face = jnp.where(lane == 0, 0.0, face) if c == 0 else face
            west_raw[c] = set_in(face, side_in.at[c])
        for c, west, _, east in neighbours(lambda c: west_raw[c], chunks, lane):
            sigma = set_in(sigma_ref[c], sig_in.at[c])
            face = harmonic(pltpu.roll(sigma, 1 if e else SUBLANES - 1, 0), sigma)
            if e:
                up = set_in(face, above_in.at[c])
                down = pltpu.roll(up, SUBLANES - 1, 0)
            else:
                down = set_in(face, below_in.at[c])
                up = pltpu.roll(down, 1, 0)
            diag = up + down + west + square * sigma
            if c == chunks - 1:
                bottom = lane == LANES - 1
                diag = diag + jnp.where(bottom, sigma, east)
                east = jnp.where(bottom, 0.0, east)
            else:
                diag = diag + east
            inverse = 1.0 / jnp.maximum(diag, TINY)
            diag_ref[c] = jnp.where(own, diag, 0.0)
            inv_ref[c] = inverse
            up_ref[c] = up * inverse
            down_ref[c] = down * inverse
            west_ref[c] = west * inverse
            east_ref[c] = east * inverse

        def spread(whole, s, c, here, left, right):
            above = pltpu.roll(here, 1, 0)
            below = pltpu.roll(here, SUBLANES - 1, 0)
            if e:
                above = jnp.where(row == 0, whole[s, c, last - 1 : last], above)
            else:
                below = jnp.where(
                    row == SUBLANES - 1, whole[s, c, SUBLANES : SUBLANES + 1], below
                )
            return (
                up_ref[c] * above
                + down_ref[c] * below
                + west_ref[c] * left
                + east_ref[c] * right
            )

        sums = {}
        for s in range(sources):
            for c, here, left, right in neighbours(lambda c: x_ref[s, c], chunks, lane):
                new = hit_in[e, s, c] * inv_ref[c] - (here - spread(x_in, s, c, here, left, right))
                basis_refs[0][s, c] = new
                add(sums, (0, s), diag_ref[c] * new * new)
        for i in range(ITERS):
            for s in range(sources):
                for c, here, left, right in neighbours(
                    lambda c: basis_refs[i][s, c], chunks, lane
                ):
                    new = spread(basis_in[i], s, c, here, left, right)
                    weighted = diag_ref[c] * new
                    add(sums, (2 * i + 1, s), weighted * here)
                    if i + 1 < ITERS:
                        basis_refs[i + 1][s, c] = new
                        add(sums, (2 * i + 2, s), weighted * new)
        picker = own & (row + (tile * rows - halo + at) == pick_ref[...])
        tops = []
        for ref in (x_ref, *basis_refs):
            for s in range(sources):
                top = jnp.broadcast_to(ref[s, 0, :, 0:1], (SUBLANES, LANES))
                tops.append(line_sum(jnp.where(picker, top, 0.0)))
        lines = lines_of(tops, sums, sources)
        for i, line in enumerate(lines):
            pay_ref[i : i + 1, :] = pay_in[i : i + 1, :] + line
        pay_ref[len(lines) :, :] = pay_in[len(lines) :, :]

    @pl.when(even)
    def _():
        one_end(even_end)

    @pl.when(jnp.logical_not(even))
    def _():
        one_end(1 - even_end)


def combine_kernel(places, halo, weight_ref, *refs):
    n_parts, n_pay = ITERS + 1, len(places)
    packed = tree_sum([refs[i][...] for i in places])
    part_refs = refs[n_pay : n_pay + n_parts]
    edge_refs = refs[n_pay + n_parts : n_pay + 2 * n_parts]
    out_refs = refs[n_pay + 2 * n_parts :]
    sources, _, total, _ = part_refs[0].shape
    rows = total - 2 * halo
    per = (out_refs[0].shape[0] - SUBLANES) // (rows * sources)
    first = n_parts * sources
    totals = jnp.sum(packed[first : first + 2 * ITERS * sources], axis=1, keepdims=True)
    poly, lost = step_polynomial(
        [totals[n * sources : (n + 1) * sources] for n in range(2 * ITERS)]
    )
    lost = jnp.broadcast_to(jnp.max(lost, axis=0, keepdims=True), (1, LANES))
    weight = weight_ref[...]
    scale = [[weight] + [weight * p[s : s + 1] for p in poly] for s in range(sources)]
    read = [
        sum(scale[s][i] * packed[i * sources + s : i * sources + s + 1] for i in range(n_parts))
        for s in range(sources)
    ]
    split = len(out_refs) > 1
    wave = lax.axis_index("wave") if split else 0
    inner = slice(SUBLANES, total - SUBLANES)
    for mask, out_ref in enumerate(out_refs):
        block = wave ^ mask if split else 0
        for s in range(sources):
            for k in range(per):
                c = block * per + k
                middle = sum(scale[s][i] * part_refs[i][s, c, inner] for i in range(n_parts))
                top, end = (
                    sum(scale[s][i] * edge_refs[i][e, s, c] for i in range(n_parts)) for e in (0, 1)
                )
                value = jnp.concatenate([top[halo:], middle, end[: SUBLANES - halo]], axis=0)
                out_ref[pl.ds((s * per + k) * rows, rows), :] = value
        end_row = sources * per * rows
        out_ref[end_row:, :] = jnp.zeros((SUBLANES, LANES), jnp.float32)
        for s in range(sources):
            out_ref[end_row + s : end_row + s + 1, :] = read[s]
        out_ref[end_row + sources : end_row + sources + 1, :] = lost


def sum_kernel(places, *refs):
    part_refs, (field_ref, read_ref, lost_ref) = [refs[i] for i in places], refs[-3:]
    sources, rows, share = field_ref.shape
    electrodes = read_ref.shape[1]
    per = share // LANES
    for s in range(sources):
        for k in range(per):
            at = pl.ds((s * per + k) * rows, rows)
            field_ref[s, :, cols(k)] = tree_sum([r[at, :] for r in part_refs])
    last = tree_sum([r[sources * per * rows :, :] for r in part_refs])
    read_ref[...] = last[:sources, :electrodes]
    lost_ref[0] = jnp.max(last[sources : sources + 1, :]).astype(jnp.int32)


def careful(warm_start, class_map, params, wavenumbers, weights, spots, picks, electrodes):
    sources = warm_start.shape[1]
    conductivities = params[:, 0, 0]
    source_row, source_col = spots[:sources, 0, 0], spots[sources:, 0, 0]
    electrode_row = picks[0, :electrodes]
    rows, depth = class_map.shape
    tiles, waves = lax.axis_size("tile"), lax.axis_size("wave")
    tile, wave = lax.axis_index("tile"), lax.axis_index("wave")

    def extended(shard, dim):
        up = [(i, i + 1) for i in range(tiles - 1)]
        down = [(j, i) for i, j in up]
        last = lax.slice_in_dim(shard, rows - 1, rows, axis=dim)
        initial = lax.slice_in_dim(shard, 0, 1, axis=dim)
        before = lax.ppermute(last, "tile", up)
        after = lax.ppermute(initial, "tile", down)
        return jnp.concatenate([before, shard, after], axis=dim)

    class_ids = jnp.arange(conductivities.shape[0], dtype=jnp.int32)
    sigma = jnp.sum(
        jnp.where(class_map[None] == class_ids[:, None, None], conductivities[:, None, None], 0.0),
        axis=0,
    )
    sigma_rim = extended(sigma, 0)
    face_row = harmonic(sigma_rim[:-1], sigma_rim[1:])
    face_up = face_row[:-1]
    face_down = face_row[1:]
    col_inner = harmonic(sigma[:, :-1], sigma[:, 1:])
    face_left = jnp.concatenate([jnp.zeros((rows, 1), jnp.float32), col_inner], axis=1)
    face_right = jnp.concatenate([col_inner, sigma[:, -1:]], axis=1)
    wave_num = wavenumbers[0]
    diag = face_up + face_down + face_left + face_right + wave_num * wave_num * sigma
    global_row = tile * rows + jnp.arange(rows, dtype=jnp.int32)
    col_ids = jnp.arange(depth, dtype=jnp.int32)
    hits = (global_row[None, :, None] == source_row[:, None, None]) & (
        col_ids[None, None, :] == source_col[:, None, None]
    )

    def operate(values):
        row_padded = extended(values, 1)
        col_padded = jnp.pad(values, ((0, 0), (0, 0), (1, 1)))
        return (
            diag * values
            - face_up * row_padded[:, :-2]
            - face_down * row_padded[:, 2:]
            - face_left * col_padded[:, :, :-2]
            - face_right * col_padded[:, :, 2:]
        )

    def inner(first, second):
        return lax.psum(jnp.sum(first * second, axis=(1, 2)), "tile")[:, None, None]

    field = warm_start[0]
    residual = SOURCE_STRENGTH * hits.astype(jnp.float32) - operate(field)
    scaled = residual / diag
    direction = scaled
    gamma = inner(residual, scaled)
    for iteration in range(ITERS):
        image = operate(direction)
        step_size = gamma / inner(direction, image)
        field = field + step_size * direction
        if iteration + 1 < ITERS:
            residual = residual - step_size * image
            scaled = residual / diag
            gamma_next = inner(residual, scaled)
            direction = scaled + (gamma_next / gamma) * direction
            gamma = gamma_next
    weighted = weights[0] * field
    picker = global_row[:, None] == electrode_row[None, :]
    local_read = jnp.sum(jnp.where(picker, weighted[:, :, 0][:, :, None], 0.0), axis=1)
    readings = lax.psum(local_read, ("wave", "tile"))
    share = depth // waves
    blocks = [
        lax.dynamic_slice_in_dim(weighted, (wave ^ mask) * share, share, 2)
        for mask in range(waves)
    ]
    blocks = [blocks[0]] + [swap(blocks[m], "wave", m, waves) for m in range(1, waves)]
    return tree_sum(blocks), readings


def shards(
    warm_start,
    class_map,
    conductivities,
    wavenumbers,
    weights,
    source_row,
    source_col,
    electrode_row,
):
    rows, depth = class_map.shape
    sources = warm_start.shape[1]
    electrodes = electrode_row.shape[0]
    tiles, waves = lax.axis_size("tile"), lax.axis_size("wave")
    wave = lax.axis_index("wave")
    halo = ITERS + 1
    field = warm_start[0]
    f32 = jnp.float32
    n_class = conductivities.shape[0]
    rim = jax.ShapeDtypeStruct((sources + 1, halo, depth), f32)
    raw = [
        field,
        class_map,
        conductivities,
        source_row,
        source_col,
    ]
    far, near, params, spots = pl.pallas_call(
        edge_kernel,
        out_shape=[
            rim,
            rim,
            jax.ShapeDtypeStruct((n_class, SUBLANES, LANES), f32),
            jax.ShapeDtypeStruct((2 * sources, SUBLANES, LANES), jnp.int32),
        ],
        in_specs=[pl.BlockSpec(memory_space=pltpu.HBM)] * len(raw),
        out_specs=[VMEM] * 4,
        scratch_shapes=[
            pltpu.VMEM((2, sources, SUBLANES, depth), f32),
            pltpu.VMEM((2, SUBLANES, depth), jnp.int32),
            *[pltpu.SMEM(a.shape, a.dtype) for a in raw[2:]],
            pltpu.SemaphoreType.DMA((len(raw) + 2,)),
        ],
        compiler_params=PARAMS,
    )(*[pltpu.with_memory_space_constraint(a, pltpu.HBM) for a in raw])
    ring = [(i, (i + 1) % tiles) for i in range(1, tiles, 2)]
    far = lax.ppermute(far, "tile", ring + [(j, i) for i, j in ring])
    near = swap(near, "tile", 1, tiles)
    total, chunks = rows + 2 * halo, depth // LANES
    picks = jnp.pad(electrode_row, (0, LANES - electrodes), constant_values=-1)[None]
    wide = jax.ShapeDtypeStruct((sources, chunks, total, LANES), f32)
    flat = jax.ShapeDtypeStruct((chunks, total, LANES), f32)
    n_lines = sources * (3 * ITERS + 1)
    pay = jax.ShapeDtypeStruct((-(-n_lines // SUBLANES) * SUBLANES, LANES), f32)
    ends = jax.ShapeDtypeStruct((2, sources, chunks, SUBLANES, LANES), f32)
    tile = jax.ShapeDtypeStruct((SUBLANES, LANES), f32)
    inside = vmem_call(
        inner_kernel,
        [wide] * (ITERS + 1) + [pay, flat, flat, flat, flat, ends, tile],
        [field, class_map, params, wavenumbers[None], spots, picks],
        [pltpu.VMEM((chunks, total, LANES), f32)] * 6,
    )
    ready = list(inside)
    scratch = [pltpu.VMEM((chunks, SUBLANES, LANES), f32)] * 8
    outside = vmem_call(
        functools.partial(outer_kernel, 1, False),
        [ends] * (ITERS + 1) + [pay],
        [near, params, picks, *ready],
        scratch,
    )
    ready[ITERS + 1] = outside[-1]
    inputs = [far, params, picks, *ready, *outside[:-1]]
    held = len(inputs) - (ITERS + 1)
    outside = vmem_call(
        functools.partial(outer_kernel, 0, True),
        [ends] * (ITERS + 1) + [pay],
        inputs,
        scratch,
        {held + i: i for i in range(ITERS + 1)},
    )
    packed = tile_parts(outside[-1], "tile")
    packed, places = issued(packed, (0, *range(len(packed) - 1, 0, -1)))
    share = depth // waves
    split = share % LANES == 0
    width = share if split else depth
    n = sources * rows * width // LANES
    block = jax.ShapeDtypeStruct((n + SUBLANES, LANES), f32)
    pieces = vmem_call(
        functools.partial(combine_kernel, places, halo),
        [block] * (waves if split else 1),
        [weights[None], *packed, *inside[: ITERS + 1], *outside[: ITERS + 1]],
    )
    if not split:
        read = pieces[0][n : n + sources, :electrodes].reshape(-1, share)
        read = jnp.concatenate([read, pieces[0][n + sources :][:1, :share]])
        whole = pieces[0][:n].reshape(sources, chunks, rows, LANES)
        whole = whole.transpose(0, 2, 1, 3).reshape(sources * rows, depth)
        pieces = [
            jnp.concatenate(
                [lax.dynamic_slice_in_dim(whole, (wave ^ mask) * share, share, 1), read]
            )
            for mask in range(waves)
        ]
    pieces = [pieces[0]] + [swap(pieces[m], "wave", m, waves) for m in range(1, waves)]
    if split:
        pieces, places = issued(pieces, (0, waves - 1, *range(1, waves - 1)))
        potentials, readings, lost = vmem_call(
            functools.partial(sum_kernel, places),
            [
                jax.ShapeDtypeStruct((sources, rows, share), f32),
                jax.ShapeDtypeStruct((sources, electrodes), f32),
                jax.ShapeDtypeStruct((1,), jnp.int32),
            ],
            pieces,
            out_specs=[VMEM, VMEM, pl.BlockSpec(memory_space=pltpu.SMEM)],
        )
        lost = lost[0] > 0
    else:
        final = tree_sum(pieces)
        lost = final[-1, 0] > 0.0
        potentials = final[: sources * rows].reshape(sources, rows, share)
        readings = final[sources * rows : -1].reshape(sources, electrodes)
    given = (warm_start, class_map, params, wavenumbers, weights, spots, picks, electrodes)
    return lax.cond(lost, lambda: careful(*given), lambda: (potentials, readings))


def solution(mesh):
    return jax.shard_map(
        shards,
        mesh=mesh,
        in_specs=(
            P("wave", None, "tile", None),
            P("tile", None),
            P(),
            P("wave"),
            P("wave"),
            P(),
            P(),
            P(),
        ),
        out_specs=(P(None, "tile", "wave"), P()),
        check_vma=False,
    )
```

```python
import functools

import jax
import jax.numpy as jnp
from jax import lax
from jax.experimental import pallas as pl
from jax.experimental.pallas import tpu as pltpu
from jax.sharding import PartitionSpec as P


ITERS = 3
SOURCE_STRENGTH = 50.0
TINY = 1e-30
LEAST_KEPT = 3e-4
LANES = 128
SUBLANES = 8


def harmonic(left_val, right_val):
    return 2.0 * left_val * right_val / jnp.maximum(left_val + right_val, TINY)


def safe_div(num, den):
    return jnp.where(den > 0.0, num / jnp.where(den > 0.0, den, 1.0), 0.0)


def tree_sum(values):
    values = list(values)
    while len(values) > 1:
        values = [values[i] + values[i + 1] for i in range(0, len(values), 2)]
    return values[0]


def swap(value, axis, mask, size):
    return lax.ppermute(value, axis, [(i, i ^ mask) for i in range(size)])


def tile_parts(value, axis):
    size = lax.axis_size(axis)
    parts = [value]
    bit = 1
    while bit < size:
        value = tree_sum(parts)
        masks = [bit]
        if bit > 1 and bit * 2 < size:
            masks.append(bit * 2)
        offsets = [0]
        for mask in masks:
            offsets += [o ^ mask for o in offsets]
        parts = [value] + [swap(value, axis, o, size) for o in offsets[1:]]
        bit = masks[-1] * 2
    return parts


def issued(values, order):
    return [values[i] for i in order], [order.index(i) for i in range(len(values))]


def step_polynomial(moments):
    trusted = []

    def product(poly, term):
        value = size = 0.0
        for i, a in enumerate(poly):
            for j, b in enumerate(poly):
                part, bound = term(i + j)
                value = value + a * b * part
                size = size + jnp.abs(a * b) * bound
        trusted.append(value > LEAST_KEPT * size)
        return value

    def inner(n):
        return moments[n], jnp.abs(moments[n])

    def energy(n):
        return moments[n] - moments[n + 1], jnp.abs(moments[n]) + jnp.abs(moments[n + 1])

    one = jnp.ones_like(moments[0])
    zero = jnp.zeros_like(moments[0])
    res, way, total = [one], [one], [zero] * ITERS
    gamma = moments[0]
    for iteration in range(ITERS):
        alpha = safe_div(gamma, product(way, energy))
        total = [t + alpha * (way[i] if i < len(way) else zero) for i, t in enumerate(total)]
        if iteration + 1 < ITERS:
            longer = way + [zero]
            shifted = [zero] + way
            res = [r - alpha * (a - b) for r, a, b in zip(res + [zero], longer, shifted)]
            gamma_next = jnp.maximum(product(res, inner), 0.0)
            ratio = safe_div(gamma_next, gamma)
            way = [r + ratio * a for r, a in zip(res, longer)]
            gamma = gamma_next
    kept = trusted[0]
    for other in trusted[1:]:
        kept = kept & other
    return total, jnp.where(kept, 0.0, 1.0)


VMEM = pl.BlockSpec(memory_space=pltpu.VMEM)
PARAMS = pltpu.CompilerParams(vmem_limit_bytes=16 << 20)


def vmem_call(kernel, out_shape, inputs, scratch=(), aliases=(), out_specs=None):
    return pl.pallas_call(
        kernel,
        out_shape=out_shape,
        in_specs=[VMEM] * len(inputs),
        out_specs=out_specs or jax.tree.map(lambda _: VMEM, out_shape),
        scratch_shapes=list(scratch),
        input_output_aliases=dict(aliases),
        compiler_params=PARAMS,
    )(*inputs)


def cols(c):
    return slice(c * LANES, (c + 1) * LANES)


def add(sums, key, value):
    sums[key] = sums[key] + value if key in sums else value


def edge_kernel(field_hbm, class_hbm, cond_hbm, row_hbm, col_hbm, *refs):
    far_ref, near_ref, par_ref, spot_ref = refs[:4]
    field_ref, class_ref, cond_ref, row_ref, col_ref, sems = refs[4:]
    sources, rows, _ = field_hbm.shape
    halo = far_ref.shape[1]
    pairs = []
    for i, at in enumerate((0, rows - SUBLANES)):
        pairs.append((field_hbm.at[:, pl.ds(at, SUBLANES)], field_ref.at[i]))
        pairs.append((class_hbm.at[pl.ds(at, SUBLANES)], class_ref.at[i]))
    pairs += [
        (cond_hbm, cond_ref),
        (row_hbm, row_ref),
        (col_hbm, col_ref),
    ]
    copies = [
        pltpu.make_async_copy(start, end, sems.at[i]) for i, (start, end) in enumerate(pairs)
    ]
    for copy in copies:
        copy.start()
    for copy in copies:
        copy.wait()
    even = lax.axis_index("tile") % 2 == 0
    spare = SUBLANES - halo
    for s in range(sources):
        first, last = field_ref[0, s, :halo], field_ref[1, s, spare:]
        far_ref[s] = jnp.where(even, first, last)
        near_ref[s] = jnp.where(even, last, first)
    first = class_ref[0, :halo].astype(jnp.float32) + 1.0
    last = class_ref[1, spare:].astype(jnp.float32) + 1.0
    far_ref[sources] = jnp.where(even, first, last)
    near_ref[sources] = jnp.where(even, last, first)
    tile = (SUBLANES, LANES)
    n_class = cond_ref.shape[0]
    for i in range(n_class):
        par_ref[i] = jnp.full(tile, cond_ref[i], jnp.float32)
    for s in range(sources):
        spot_ref[s] = jnp.full(tile, row_ref[s], jnp.int32)
        spot_ref[sources + s] = jnp.full(tile, col_ref[s], jnp.int32)


def neighbours(get, chunks, lane):
    here = get(0)
    last = LANES - 1
    from_right = pltpu.roll(here, last, 1)
    before = None
    for c in range(chunks):
        from_left = pltpu.roll(here, 1, 1)
        left = jnp.where(lane == 0, before, from_left) if c else from_left
        right = from_right
        if c + 1 < chunks:
            following = get(c + 1)
            from_next = pltpu.roll(following, last, 1)
            right = jnp.where(lane == last, from_next, from_right)
        yield c, here, left, right
        before = from_left
        if c + 1 < chunks:
            here, from_right = following, from_next


def conductivity(ids, values):
    sigma = jnp.zeros(ids.shape, jnp.float32)
    for i, value in enumerate(values):
        sigma = jnp.where(ids == i + 1.0, value, sigma)
    return sigma


def tall(tile, rows):
    return jnp.concatenate([tile] * (rows // SUBLANES), axis=0)


def line_sum(value):
    return jnp.sum(value, axis=0, keepdims=True)


def lines_of(tops, sums, sources):
    lines = list(tops)
    for n in range(2 * ITERS):
        for s in range(sources):
            lines.append(line_sum(sums[n, s]))
    return lines


def inner_kernel(field_ref, class_ref, par_ref, wave_ref, spot_ref, pick_ref, *refs):
    x_ref, *basis_refs = refs[: 1 + ITERS]
    pay_ref, sig_ref, side_ref, above_ref, below_ref, hit_ref, square_ref = refs[1 + ITERS : 8 + ITERS]
    up_ref, down_ref, west_ref, east_ref, diag_ref, inv_ref = refs[8 + ITERS :]
    sources, rows, _ = field_ref.shape
    chunks, total = x_ref.shape[1:3]
    n_class = par_ref.shape[0]
    halo = (total - rows) // 2
    lane = lax.broadcasted_iota(jnp.int32, (total, LANES), 1)
    row = lax.broadcasted_iota(jnp.int32, (total, LANES), 0)
    rows_at = row + (lax.axis_index("tile") * rows - halo)
    blank = jnp.zeros((halo, LANES), jnp.float32)
    inner = slice(SUBLANES, total - SUBLANES)
    wave = jnp.broadcast_to(wave_ref[...], (SUBLANES, LANES))
    square_ref[...] = wave * wave
    square = tall(square_ref[...], total)
    values = [tall(par_ref[i], rows) for i in range(n_class)]

    def widened(value):
        return jnp.concatenate([blank, value, blank], axis=0)

    for c in range(chunks):
        ids = class_ref[:, cols(c)].astype(jnp.float32) + 1.0
        sig_ref[c] = widened(conductivity(ids, values))
        for s in range(sources):
            x_ref[s, c] = widened(field_ref[s, :, cols(c)])
    for c, sigma, left, _ in neighbours(lambda c: sig_ref[c], chunks, lane):
        face = harmonic(left, sigma)
        side_ref[c] = jnp.where(lane == 0, 0.0, face) if c == 0 else face
        up = harmonic(pltpu.roll(sigma, 1, 0), sigma)
        above_ref[c] = up
        below_ref[c] = pltpu.roll(up, total - 1, 0)
    at_source = [rows_at == tall(spot_ref[s], total) for s in range(sources)]
    for c, west, _, east in neighbours(lambda c: side_ref[c], chunks, lane):
        up, down = above_ref[c], below_ref[c]
        sigma = sig_ref[c]
        diag = up + down + west + square * sigma
        if c == chunks - 1:
            bottom = lane == LANES - 1
            diag = diag + jnp.where(bottom, sigma, east)
            east = jnp.where(bottom, 0.0, east)
        else:
            diag = diag + east
        inverse = 1.0 / jnp.maximum(diag, TINY)
        diag_ref[c] = diag
        inv_ref[c] = inverse
        up_ref[c] = up * inverse
        down_ref[c] = down * inverse
        west_ref[c] = west * inverse
        east_ref[c] = east * inverse

    def spread(c, here, left, right):
        return (
            up_ref[c] * pltpu.roll(here, 1, 0)
            + down_ref[c] * pltpu.roll(here, total - 1, 0)
            + west_ref[c] * left
            + east_ref[c] * right
        )

    def fold(value):
        return sum(value[r : r + SUBLANES] for r in range(0, value.shape[0], SUBLANES))

    sums = {}
    for s in range(sources):
        column = tall(spot_ref[sources + s], total)
        for c, here, left, right in neighbours(lambda c: x_ref[s, c], chunks, lane):
            charge = jnp.where(
                at_source[s] & (lane + c * LANES == column), SOURCE_STRENGTH, 0.0
            )
            hit_ref[0, s, c] = charge[:SUBLANES]
            hit_ref[1, s, c] = charge[total - SUBLANES :]
            new = charge * inv_ref[c] - (here - spread(c, here, left, right))
            basis_refs[0][s, c] = new
            own = new[inner]
            add(sums, (0, s), fold(diag_ref[c, inner] * own * own))
    for i in range(ITERS):
        for s in range(sources):
            for c, here, left, right in neighbours(lambda c: basis_refs[i][s, c], chunks, lane):
                new = spread(c, here, left, right)
                own = new[inner]
                weighted = diag_ref[c, inner] * own
                add(sums, (2 * i + 1, s), fold(weighted * here[inner]))
                if i + 1 < ITERS:
                    basis_refs[i + 1][s, c] = new
                    add(sums, (2 * i + 2, s), fold(weighted * own))
    picker = rows_at[inner] == pick_ref[...]
    tops = []
    for ref in (x_ref, *basis_refs):
        for s in range(sources):
            top = jnp.broadcast_to(ref[s, 0, inner, 0:1], (total - 2 * SUBLANES, LANES))
            tops.append(line_sum(fold(jnp.where(picker, top, 0.0))))
    pay_ref[...] = jnp.zeros(pay_ref.shape, jnp.float32)
    for i, line in enumerate(lines_of(tops, sums, sources)):
        pay_ref[i : i + 1, :] = line


def outer_kernel(even_end, wraps, came_ref, par_ref, pick_ref, *refs):
    x_in, *basis_in = refs[: 1 + ITERS]
    pay_in, sig_in, side_in, above_in, below_in, hit_in, square_in = refs[1 + ITERS : 8 + ITERS]
    outs = refs[-(10 + ITERS) :]
    x_out, *basis_outs = outs[: 1 + ITERS]
    pay_ref = outs[1 + ITERS]
    sigma_ref, west_raw, up_ref, down_ref, west_ref, east_ref, diag_ref, inv_ref = outs[2 + ITERS :]
    sources, chunks, total, _ = x_in.shape
    halo = came_ref.shape[1]
    rows = total - 2 * halo
    lane = lax.broadcasted_iota(jnp.int32, (SUBLANES, LANES), 1)
    row = lax.broadcasted_iota(jnp.int32, (SUBLANES, LANES), 0)
    tile = lax.axis_index("tile")
    even = tile % 2 == 0
    square = square_in[...]
    values = [par_ref[i] for i in range(par_ref.shape[0])]
    upper = row < halo
    last = total - SUBLANES
    inside = (tile > 0) & (tile < lax.axis_size("tile") - 1)

    def came_in(index, c):
        value = came_ref[index, :, cols(c)]
        if wraps:
            value = jnp.where(inside, value, 0.0)
        return jnp.concatenate([value, value], axis=0)

    def one_end(e):
        at = last if e else 0
        tile_at = slice(at, at + SUBLANES)
        own = upper if e else jnp.logical_not(upper)
        x_ref, *basis_refs = [r.at[e] for r in (x_out, *basis_outs)]

        def set_in(new, kept):
            return jnp.where(own, kept[tile_at], new)

        for c in range(chunks):
            sigma_ref[c] = conductivity(came_in(sources, c), values)
            for s in range(sources):
                x_ref[s, c] = set_in(came_in(s, c), x_in.at[s, c])
        for c, fresh, left, _ in neighbours(lambda c: sigma_ref[c], chunks, lane):
            face = harmonic(left, fresh)
            face = jnp.where(lane == 0, 0.0, face) if c == 0 else face
            west_raw[c] = set_in(face, side_in.at[c])
        for c, west, _, east in neighbours(lambda c: west_raw[c], chunks, lane):
            sigma = set_in(sigma_ref[c], sig_in.at[c])
            face = harmonic(pltpu.roll(sigma, 1 if e else SUBLANES - 1, 0), sigma)
            if e:
                up = set_in(face, above_in.at[c])
                down = pltpu.roll(up, SUBLANES - 1, 0)
            else:
                down = set_in(face, below_in.at[c])
                up = pltpu.roll(down, 1, 0)
            diag = up + down + west + square * sigma
            if c == chunks - 1:
                bottom = lane == LANES - 1
                diag = diag + jnp.where(bottom, sigma, east)
                east = jnp.where(bottom, 0.0, east)
            else:
                diag = diag + east
            inverse = 1.0 / jnp.maximum(diag, TINY)
            diag_ref[c] = jnp.where(own, diag, 0.0)
            inv_ref[c] = inverse
            up_ref[c] = up * inverse
            down_ref[c] = down * inverse
            west_ref[c] = west * inverse
            east_ref[c] = east * inverse

        def spread(whole, s, c, here, left, right):
            above = pltpu.roll(here, 1, 0)
            below = pltpu.roll(here, SUBLANES - 1, 0)
            if e:
                above = jnp.where(row == 0, whole[s, c, last - 1 : last], above)
            else:
                below = jnp.where(
                    row == SUBLANES - 1, whole[s, c, SUBLANES : SUBLANES + 1], below
                )
            return (
                up_ref[c] * above
                + down_ref[c] * below
                + west_ref[c] * left
                + east_ref[c] * right
            )

        sums = {}
        for s in range(sources):
            for c, here, left, right in neighbours(lambda c: x_ref[s, c], chunks, lane):
                new = hit_in[e, s, c] * inv_ref[c] - (here - spread(x_in, s, c, here, left, right))
                basis_refs[0][s, c] = new
                add(sums, (0, s), diag_ref[c] * new * new)
        for i in range(ITERS):
            for s in range(sources):
                for c, here, left, right in neighbours(
                    lambda c: basis_refs[i][s, c], chunks, lane
                ):
                    new = spread(basis_in[i], s, c, here, left, right)
                    weighted = diag_ref[c] * new
                    add(sums, (2 * i + 1, s), weighted * here)
                    if i + 1 < ITERS:
                        basis_refs[i + 1][s, c] = new
                        add(sums, (2 * i + 2, s), weighted * new)
        picker = own & (row + (tile * rows - halo + at) == pick_ref[...])
        tops = []
        for ref in (x_ref, *basis_refs):
            for s in range(sources):
                top = jnp.broadcast_to(ref[s, 0, :, 0:1], (SUBLANES, LANES))
                tops.append(line_sum(jnp.where(picker, top, 0.0)))
        lines = lines_of(tops, sums, sources)
        for i, line in enumerate(lines):
            pay_ref[i : i + 1, :] = pay_in[i : i + 1, :] + line
        pay_ref[len(lines) :, :] = pay_in[len(lines) :, :]

    @pl.when(even)
    def _():
        one_end(even_end)

    @pl.when(jnp.logical_not(even))
    def _():
        one_end(1 - even_end)


def combine_kernel(places, halo, weight_ref, *refs):
    n_parts, n_pay = ITERS + 1, len(places)
    packed = tree_sum([refs[i][...] for i in places])
    part_refs = refs[n_pay : n_pay + n_parts]
    edge_refs = refs[n_pay + n_parts : n_pay + 2 * n_parts]
    out_refs = refs[n_pay + 2 * n_parts :]
    sources, _, total, _ = part_refs[0].shape
    rows = total - 2 * halo
    per = (out_refs[0].shape[0] - SUBLANES) // (rows * sources)
    first = n_parts * sources
    totals = jnp.sum(packed[first : first + 2 * ITERS * sources], axis=1, keepdims=True)
    poly, lost = step_polynomial(
        [totals[n * sources : (n + 1) * sources] for n in range(2 * ITERS)]
    )
    lost = jnp.broadcast_to(jnp.max(lost, axis=0, keepdims=True), (1, LANES))
    weight = weight_ref[...]
    scale = [[weight] + [weight * p[s : s + 1] for p in poly] for s in range(sources)]
    read = [
        sum(scale[s][i] * packed[i * sources + s : i * sources + s + 1] for i in range(n_parts))
        for s in range(sources)
    ]
    split = len(out_refs) > 1
    wave = lax.axis_index("wave") if split else 0
    inner = slice(SUBLANES, total - SUBLANES)
    for mask, out_ref in enumerate(out_refs):
        block = wave ^ mask if split else 0
        for s in range(sources):
            for k in range(per):
                c = block * per + k
                middle = sum(scale[s][i] * part_refs[i][s, c, inner] for i in range(n_parts))
                top, end = (
                    sum(scale[s][i] * edge_refs[i][e, s, c] for i in range(n_parts)) for e in (0, 1)
                )
                value = jnp.concatenate([top[halo:], middle, end[: SUBLANES - halo]], axis=0)
                out_ref[pl.ds((s * per + k) * rows, rows), :] = value
        end_row = sources * per * rows
        out_ref[end_row:, :] = jnp.zeros((SUBLANES, LANES), jnp.float32)
        for s in range(sources):
            out_ref[end_row + s : end_row + s + 1, :] = read[s]
        out_ref[end_row + sources : end_row + sources + 1, :] = lost


def sum_kernel(places, *refs):
    part_refs = [refs[i] for i in places]
    field_hbm, read_hbm, lost_ref, field_ref, read_ref, sems = refs[len(places) :]
    sources, rows, share = field_ref.shape
    electrodes = read_ref.shape[1]
    per = share // LANES
    for s in range(sources):
        for k in range(per):
            at = pl.ds((s * per + k) * rows, rows)
            field_ref[s, :, cols(k)] = tree_sum([r[at, :] for r in part_refs])
    last = tree_sum([r[sources * per * rows :, :] for r in part_refs])
    read_ref[...] = last[:sources, :electrodes]
    copies = [
        pltpu.make_async_copy(field_ref, field_hbm, sems.at[0]),
        pltpu.make_async_copy(read_ref, read_hbm, sems.at[1]),
    ]
    for copy in copies:
        copy.start()
    lost_ref[0] = jnp.max(last[sources : sources + 1, :]).astype(jnp.int32)
    for copy in copies:
        copy.wait()


def careful(warm_start, class_map, params, wavenumbers, weights, spots, picks, electrodes):
    sources = warm_start.shape[1]
    conductivities = params[:, 0, 0]
    source_row, source_col = spots[:sources, 0, 0], spots[sources:, 0, 0]
    electrode_row = picks[0, :electrodes]
    rows, depth = class_map.shape
    tiles, waves = lax.axis_size("tile"), lax.axis_size("wave")
    tile, wave = lax.axis_index("tile"), lax.axis_index("wave")

    def extended(shard, dim):
        up = [(i, i + 1) for i in range(tiles - 1)]
        down = [(j, i) for i, j in up]
        last = lax.slice_in_dim(shard, rows - 1, rows, axis=dim)
        initial = lax.slice_in_dim(shard, 0, 1, axis=dim)
        before = lax.ppermute(last, "tile", up)
        after = lax.ppermute(initial, "tile", down)
        return jnp.concatenate([before, shard, after], axis=dim)

    class_ids = jnp.arange(conductivities.shape[0], dtype=jnp.int32)
    sigma = jnp.sum(
        jnp.where(class_map[None] == class_ids[:, None, None], conductivities[:, None, None], 0.0),
        axis=0,
    )
    sigma_rim = extended(sigma, 0)
    face_row = harmonic(sigma_rim[:-1], sigma_rim[1:])
    face_up = face_row[:-1]
    face_down = face_row[1:]
    col_inner = harmonic(sigma[:, :-1], sigma[:, 1:])
    face_left = jnp.concatenate([jnp.zeros((rows, 1), jnp.float32), col_inner], axis=1)
    face_right = jnp.concatenate([col_inner, sigma[:, -1:]], axis=1)
    wave_num = wavenumbers[0]
    diag = face_up + face_down + face_left + face_right + wave_num * wave_num * sigma
    global_row = tile * rows + jnp.arange(rows, dtype=jnp.int32)
    col_ids = jnp.arange(depth, dtype=jnp.int32)
    hits = (global_row[None, :, None] == source_row[:, None, None]) & (
        col_ids[None, None, :] == source_col[:, None, None]
    )

    def operate(values):
        row_padded = extended(values, 1)
        col_padded = jnp.pad(values, ((0, 0), (0, 0), (1, 1)))
        return (
            diag * values
            - face_up * row_padded[:, :-2]
            - face_down * row_padded[:, 2:]
            - face_left * col_padded[:, :, :-2]
            - face_right * col_padded[:, :, 2:]
        )

    def inner(first, second):
        return lax.psum(jnp.sum(first * second, axis=(1, 2)), "tile")[:, None, None]

    field = warm_start[0]
    residual = SOURCE_STRENGTH * hits.astype(jnp.float32) - operate(field)
    scaled = residual / diag
    direction = scaled
    gamma = inner(residual, scaled)
    for iteration in range(ITERS):
        image = operate(direction)
        step_size = gamma / inner(direction, image)
        field = field + step_size * direction
        if iteration + 1 < ITERS:
            residual = residual - step_size * image
            scaled = residual / diag
            gamma_next = inner(residual, scaled)
            direction = scaled + (gamma_next / gamma) * direction
            gamma = gamma_next
    weighted = weights[0] * field
    picker = global_row[:, None] == electrode_row[None, :]
    local_read = jnp.sum(jnp.where(picker, weighted[:, :, 0][:, :, None], 0.0), axis=1)
    readings = lax.psum(local_read, ("wave", "tile"))
    share = depth // waves
    blocks = [
        lax.dynamic_slice_in_dim(weighted, (wave ^ mask) * share, share, 2)
        for mask in range(waves)
    ]
    blocks = [blocks[0]] + [swap(blocks[m], "wave", m, waves) for m in range(1, waves)]
    return tree_sum(blocks), readings


def shards(
    warm_start,
    class_map,
    conductivities,
    wavenumbers,
    weights,
    source_row,
    source_col,
    electrode_row,
):
    rows, depth = class_map.shape
    sources = warm_start.shape[1]
    electrodes = electrode_row.shape[0]
    tiles, waves = lax.axis_size("tile"), lax.axis_size("wave")
    wave = lax.axis_index("wave")
    halo = ITERS + 1
    field = warm_start[0]
    f32 = jnp.float32
    n_class = conductivities.shape[0]
    rim = jax.ShapeDtypeStruct((sources + 1, halo, depth), f32)
    raw = [
        field,
        class_map,
        conductivities,
        source_row,
        source_col,
    ]
    far, near, params, spots = pl.pallas_call(
        edge_kernel,
        out_shape=[
            rim,
            rim,
            jax.ShapeDtypeStruct((n_class, SUBLANES, LANES), f32),
            jax.ShapeDtypeStruct((2 * sources, SUBLANES, LANES), jnp.int32),
        ],
        in_specs=[pl.BlockSpec(memory_space=pltpu.HBM)] * len(raw),
        out_specs=[VMEM] * 4,
        scratch_shapes=[
            pltpu.VMEM((2, sources, SUBLANES, depth), f32),
            pltpu.VMEM((2, SUBLANES, depth), jnp.int32),
            *[pltpu.SMEM(a.shape, a.dtype) for a in raw[2:]],
            pltpu.SemaphoreType.DMA((len(raw) + 2,)),
        ],
        compiler_params=PARAMS,
    )(*[pltpu.with_memory_space_constraint(a, pltpu.HBM) for a in raw])
    ring = [(i, (i + 1) % tiles) for i in range(1, tiles, 2)]
    far = lax.ppermute(far, "tile", ring + [(j, i) for i, j in ring])
    near = swap(near, "tile", 1, tiles)
    total, chunks = rows + 2 * halo, depth // LANES
    picks = jnp.pad(electrode_row, (0, LANES - electrodes), constant_values=-1)[None]
    wide = jax.ShapeDtypeStruct((sources, chunks, total, LANES), f32)
    flat = jax.ShapeDtypeStruct((chunks, total, LANES), f32)
    n_lines = sources * (3 * ITERS + 1)
    pay = jax.ShapeDtypeStruct((-(-n_lines // SUBLANES) * SUBLANES, LANES), f32)
    ends = jax.ShapeDtypeStruct((2, sources, chunks, SUBLANES, LANES), f32)
    tile = jax.ShapeDtypeStruct((SUBLANES, LANES), f32)
    inside = vmem_call(
        inner_kernel,
        [wide] * (ITERS + 1) + [pay, flat, flat, flat, flat, ends, tile],
        [field, class_map, params, wavenumbers[None], spots, picks],
        [pltpu.VMEM((chunks, total, LANES), f32)] * 6,
    )
    ready = list(inside)
    scratch = [pltpu.VMEM((chunks, SUBLANES, LANES), f32)] * 8
    outside = vmem_call(
        functools.partial(outer_kernel, 1, False),
        [ends] * (ITERS + 1) + [pay],
        [near, params, picks, *ready],
        scratch,
    )
    ready[ITERS + 1] = outside[-1]
    inputs = [far, params, picks, *ready, *outside[:-1]]
    held = len(inputs) - (ITERS + 1)
    outside = vmem_call(
        functools.partial(outer_kernel, 0, True),
        [ends] * (ITERS + 1) + [pay],
        inputs,
        scratch,
        {held + i: i for i in range(ITERS + 1)},
    )
    packed = tile_parts(outside[-1], "tile")
    packed, places = issued(packed, (0, *range(len(packed) - 1, 0, -1)))
    share = depth // waves
    split = share % LANES == 0
    width = share if split else depth
    n = sources * rows * width // LANES
    block = jax.ShapeDtypeStruct((n + SUBLANES, LANES), f32)
    pieces = vmem_call(
        functools.partial(combine_kernel, places, halo),
        [block] * (waves if split else 1),
        [weights[None], *packed, *inside[: ITERS + 1], *outside[: ITERS + 1]],
    )
    if not split:
        read = pieces[0][n : n + sources, :electrodes].reshape(-1, share)
        read = jnp.concatenate([read, pieces[0][n + sources :][:1, :share]])
        whole = pieces[0][:n].reshape(sources, chunks, rows, LANES)
        whole = whole.transpose(0, 2, 1, 3).reshape(sources * rows, depth)
        pieces = [
            jnp.concatenate(
                [lax.dynamic_slice_in_dim(whole, (wave ^ mask) * share, share, 1), read]
            )
            for mask in range(waves)
        ]
    pieces = [pieces[0]] + [swap(pieces[m], "wave", m, waves) for m in range(1, waves)]
    if split:
        pieces, places = issued(pieces, (0, waves - 1, *range(1, waves - 1)))
        potentials, readings, lost = vmem_call(
            functools.partial(sum_kernel, places),
            [
                pltpu.HBM((sources, rows, share), f32),
                pltpu.HBM((sources, electrodes), f32),
                jax.ShapeDtypeStruct((1,), jnp.int32),
            ],
            pieces,
            [
                pltpu.VMEM((sources, rows, share), f32),
                pltpu.VMEM((sources, electrodes), f32),
                pltpu.SemaphoreType.DMA((2,)),
            ],
            out_specs=[pl.BlockSpec(memory_space=pltpu.HBM)] * 2
            + [pl.BlockSpec(memory_space=pltpu.SMEM)],
        )
        lost = lost[0] > 0
    else:
        final = tree_sum(pieces)
        lost = final[-1, 0] > 0.0
        potentials = final[: sources * rows].reshape(sources, rows, share)
        readings = final[sources * rows : -1].reshape(sources, electrodes)
    given = (warm_start, class_map, params, wavenumbers, weights, spots, picks, electrodes)
    return lax.cond(lost, lambda: careful(*given), lambda: (potentials, readings))


def solution(mesh):
    return jax.shard_map(
        shards,
        mesh=mesh,
        in_specs=(
            P("wave", None, "tile", None),
            P("tile", None),
            P(),
            P("wave"),
            P("wave"),
            P(),
            P(),
            P(),
        ),
        out_specs=(P(None, "tile", "wave"), P()),
        check_vma=False,
    )
```
